32 devices in a mesh: rows: 4 (over y, x), cols: 8 (over z, core).
Axes of the slice: x: 2, y: 2, z: 4, core: 2. Of those that a mesh axis runs over, the one named last changes fastest.
Arguments:
- images: bfloat16 [2, 64, 256, 1024], P(None, None, 'rows', 'cols'), may hold values from -6 to 6
- first_weight: bfloat16 [9, 64, 64], replicated, may hold values from -0.25 to 0.25
- second_weight: bfloat16 [9, 64, 64], replicated, may hold values from -0.25 to 0.25
- search_ranges: int32 [2, 32, 8], P(None, 'rows', 'cols'), may hold values from 0 to 16, as said below
Outputs:
- matched: bfloat16 [64, 256, 1024], P(None, 'rows', 'cols')
- disparity: float32 [256, 1024], P('rows', 'cols')
The draws below stay inside these ranges and needn't reach their ends.
Inputs may be any that keep to these rules, and one draw needn't show every extreme that they name: search_ranges[0] is 0 to 1 and search_ranges[1] is 1 to 16; some block has search_ranges[0] = 1 together with search_ranges[1] = 16.
All inputs are finite; a program needn't handle non-finite values.
Results may differ from the reference program's by a relative error of at most 0.008.
Values may be sent and summed in bfloat16 or wider, within the bound.
No kernel may reach another device: no remote copies, remote signals or barrier semaphores. Data moves between devices by JAX's collectives and lax.ppermute only.
A program may use at most 128 MiB of HBM per device.

```python
import jax
import jax.numpy as jnp
from jax import lax

C = 64
SEG = 128
RG = 8
MINB = 2
CNTB = 16
FIRST_DILATION = 2
SECOND_DILATION = 4
HOPS = 18
H = 256
W = 1024
GROUPS = 32
BLOCKS = 8


def draw_search_ranges(key, part):
    folded = jax.random.fold_in(key, 7)
    first_key, second_key, third_key = jax.random.split(folded, 3)
    lowest_blocks = jax.random.randint(first_key, (GROUPS * BLOCKS,), 0, MINB)
    powers = jax.random.randint(second_key, (GROUPS * BLOCKS,), 0, 5)
    counts = jnp.minimum(jnp.left_shift(jnp.ones_like(powers), powers), CNTB)
    chosen = jax.random.randint(third_key, (), 0, GROUPS * BLOCKS)
    spot_mask = jnp.arange(GROUPS * BLOCKS) == chosen
    lowest_blocks = jnp.where(spot_mask, MINB - 1, lowest_blocks)
    counts = jnp.where(spot_mask, CNTB, counts)
    return jnp.stack([lowest_blocks, counts]).reshape(2, GROUPS, BLOCKS).astype(jnp.int32)


def block_scale(key, dims, pieces, least, top_value):
    def one(position, blocks):
        heights = jax.random.uniform(jax.random.fold_in(jax.random.fold_in(key, 6), position), (blocks,), jnp.float32, least / len(pieces), top_value / len(pieces))
        return jnp.repeat(jnp.exp(heights), dims[position] // blocks).reshape((-1,) + (1,) * (len(dims) - position - 1))

    gain = one(*pieces[0])
    for cut in pieces[1:]:
        gain = gain * one(*cut)
    return gain


def normal_values(own_key, extent, scale, bound, pieces=(), kind=jnp.bfloat16):
    array = scale * jax.random.normal(own_key, extent, jnp.float32)
    if pieces:
        array = array * block_scale(own_key, extent, pieces, -0.22, 0.18)
    return jnp.clip(array, -bound, bound).astype(kind)


def setup_inputs(seed: int = 0) -> dict:
    keys = jax.random.split(jax.random.key(seed), 5)
    return {
        "images": normal_values(keys[0], (2, C, H, W), 1.0, 6.0, ((2, 4), (3, 8))),
        "first_weight": normal_values(keys[1], (9, C, C), (9 * C) ** -0.5, 0.25),
        "second_weight": normal_values(keys[2], (9, C, C), (9 * C) ** -0.5, 0.25),
        "search_ranges": draw_search_ranges(jax.random.fold_in(keys[4], 71), 0),
    }


sharpness_divisor = 10.0
epsilon = 1e-05

def apply_convolution(images, weights, dilation):
    height = images.shape[2]
    full_width = images.shape[3]
    padded = jnp.pad(images.astype(jnp.float32), ((0, 0), (0, 0), (dilation, dilation), (dilation, dilation)))
    summed = jnp.zeros((images.shape[0], weights.shape[1], height, full_width), jnp.float32)
    for row_tap in range(3):
        for horizontal_offset in range(3):
            window = padded[:, :, row_tap * dilation:row_tap * dilation + height, horizontal_offset * dilation:horizontal_offset * dilation + full_width]
            summed = summed + jnp.einsum('oc,nchw->nohw', weights[3 * row_tap + horizontal_offset].astype(jnp.float32), window)
    return summed

def normalize(feature_maps):
    widened = feature_maps.astype(jnp.float32)
    return (widened * lax.rsqrt(lax.optimization_barrier(jnp.mean(widened * widened, axis=1, keepdims=True)) + epsilon)).astype(jnp.bfloat16)

def reference(images, first_weight, second_weight, search_ranges):
    inner_activations = jax.nn.silu(apply_convolution(images, first_weight, FIRST_DILATION)).astype(jnp.bfloat16)
    feature_maps = (images.astype(jnp.float32) + apply_convolution(inner_activations, second_weight, SECOND_DILATION)).astype(jnp.bfloat16)
    unit_feats = normalize(feature_maps)
    left_unit = unit_feats[0]
    right_unit = unit_feats[1]
    plane_total, height, full_width = left_unit.shape
    padded = jnp.pad(right_unit, ((0, 0), (0, 0), ((HOPS - 1) * SEG, 0)))
    per_row = jnp.repeat(search_ranges, RG, axis=1)
    offsets = (HOPS - 1) * SEG + jnp.arange(SEG, dtype=jnp.int32)[:, None] - jnp.arange(HOPS * SEG, dtype=jnp.int32)[None, :]

    def one_block(block_index):
        start = (block_index * SEG).astype(jnp.int32)
        source_descriptors = lax.dynamic_slice_in_dim(left_unit, start, SEG, 2).astype(jnp.float32)
        target_descriptors = lax.dynamic_slice_in_dim(padded, start, HOPS * SEG, 2).astype(jnp.float32)
        pairing_similarity = jnp.einsum('yrm,yrs->rms', source_descriptors, target_descriptors) * (sharpness_divisor / plane_total)
        interval_bounds = lax.dynamic_slice_in_dim(per_row, block_index.astype(jnp.int32), 1, 2)[:, :, 0]
        low_edge = SEG * interval_bounds[0]
        high_edge = SEG * (interval_bounds[0] + interval_bounds[1])
        inside = (offsets[None] >= low_edge[:, None, None]) & (offsets[None] < high_edge[:, None, None])
        rounded = lax.optimization_barrier(jnp.where(inside, jnp.exp(pairing_similarity), 0.0).astype(jnp.bfloat16))
        weights = rounded.astype(jnp.float32)
        norm_sum = lax.optimization_barrier(jnp.sum(weights, axis=-1))
        shift_sum = lax.optimization_barrier(jnp.sum(weights * offsets.astype(jnp.float32)[None], axis=-1))
        feature_sum = jnp.einsum('him,chm->chi', weights, target_descriptors)
        return ((feature_sum / norm_sum[None]).astype(jnp.bfloat16), shift_sum / norm_sum / SEG)
    matched, disparity = lax.map(one_block, jnp.arange(full_width // SEG, dtype=jnp.int32))
    matched = matched.transpose(1, 2, 0, 3).reshape(plane_total, height, full_width)
    disparity = disparity.transpose(1, 0, 2).reshape(height, full_width)
    return (matched, disparity)
```

```python
import functools

import jax
import jax.numpy as jnp
from jax import lax
from jax.experimental import pallas as pl
from jax.experimental.pallas import tpu as pltpu
from jax.sharding import PartitionSpec as P

RG = 8
FIRST_DILATION = 2
SECOND_DILATION = 4
HOPS = 18
REACH = FIRST_DILATION + SECOND_DILATION
SLOT = 16

sharpness_divisor = 10.0
epsilon = 1e-05
LOG2E = 1.4426950408889634


def lane_iota(shape):
    return lax.broadcasted_iota(jnp.int32, shape, len(shape) - 1)


def pack_kernel(top_ref, mid_ref, bottom_ref, edge_ref, *, groups, spacing):
    channels, segment = mid_ref.shape[1:]
    rows = mid_ref.shape[0]
    slot_of = lane_iota((channels, segment)) // SLOT
    steps = edge_ref.shape[0]
    for q in range(steps):
        packed = jnp.zeros((channels, segment), jnp.float32)
        for g in range(groups):
            row = g * spacing + q
            if row < REACH:
                source = top_ref[row]
            elif row < REACH + rows:
                source = mid_ref[row - REACH]
            else:
                source = bottom_ref[row - REACH - rows]
            shift = (SLOT * g + SLOT // 2) % segment
            packed = jnp.where(slot_of == g, pltpu.roll(source.astype(jnp.float32), shift, 1), packed)
        edge_ref[q] = packed.astype(jnp.bfloat16)


def pack_edges(top, mid, bottom):
    images, rows, channels, segment = mid.shape
    groups = segment // SLOT
    spacing = (rows + 2 * SECOND_DILATION) // groups
    steps = spacing + 2 * FIRST_DILATION
    return pl.pallas_call(
        functools.partial(pack_kernel, groups=groups, spacing=spacing),
        out_shape=jax.ShapeDtypeStruct((images, steps, channels, segment), jnp.bfloat16),
        grid=(images,),
        in_specs=[
            pl.BlockSpec((None, REACH, channels, segment), lambda n: (n, 0, 0, 0)),
            pl.BlockSpec((None, rows, channels, segment), lambda n: (n, 0, 0, 0)),
            pl.BlockSpec((None, REACH, channels, segment), lambda n: (n, 0, 0, 0)),
        ],
        out_specs=pl.BlockSpec((None, steps, channels, segment), lambda n: (n, 0, 0, 0)),
        name="pack_edges",
    )(top, mid, bottom)


def feature_kernel(
    place_ref, top_ref, mid_ref, bottom_ref, own_ref, partner_ref, cross_ref, w1_ref, w2_ref, unit_ref,
    x_ref, edge_ref, p1_ref, p1e_ref, hid_ref, hide_ref, p2_ref, rhs_ref, *, spacing,
):
    rows, channels, segment = mid_ref.shape
    first_row, last_row, first_col, last_col, odd = (place_ref[i] for i in range(5))
    d1, d2 = FIRST_DILATION, SECOND_DILATION
    all_rows = rows + 2 * REACH
    hidden_rows = rows + 2 * d2
    steps = edge_ref.shape[0]
    groups = segment // SLOT
    lanes = lane_iota((channels, segment))
    in_slot = lanes % SLOT
    half = SLOT // 2

    x_ref[0:REACH] = top_ref[...]
    x_ref[REACH : REACH + rows] = mid_ref[...]
    x_ref[REACH + rows :] = bottom_ref[...]

    for q in range(steps):
        own = own_ref[q].astype(jnp.float32)
        partner = partner_ref[q].astype(jnp.float32)
        cross = cross_ref[q].astype(jnp.float32)
        left = jnp.where(odd == 1, partner, cross)
        right = jnp.where(odd == 1, cross, partner)
        shift = half - REACH
        lower = pltpu.roll(jnp.where(in_slot < half, left, own), segment - shift, 1)
        upper = pltpu.roll(jnp.where(in_slot < half, own, right), shift, 1)
        edge_ref[q] = jnp.where(in_slot < half, lower, upper).astype(jnp.bfloat16)

    def shifted(main, edge, slot, amount):
        main = main.astype(jnp.float32)
        edge = edge.astype(jnp.float32)
        low_from = slot * SLOT + REACH - amount
        high_from = slot * SLOT + half + 2
        before = jnp.where(
            lanes < amount,
            pltpu.roll(edge, lax.rem(segment - low_from, segment), 1),
            pltpu.roll(main, amount, 1),
        )
        after = jnp.where(
            lanes >= segment - amount,
            pltpu.roll(edge, lax.rem(2 * segment - amount - high_from, segment), 1),
            pltpu.roll(main, segment - amount, 1),
        )
        return before.astype(jnp.bfloat16), after.astype(jnp.bfloat16)

    def place(slot_index, main, before, after):
        lo = slot_index * segment
        rhs_ref[0:channels, lo : lo + segment] = before
        rhs_ref[channels : 2 * channels, lo : lo + segment] = main
        rhs_ref[2 * channels :, lo : lo + segment] = after

    def slot_and_step(row):
        slot = jnp.minimum(row // spacing, groups - 1)
        return slot, row - slot * spacing

    def conv(source_ref, sides_ref, weight_ref, product_ref, total, amount, width):
        def body(t, _):
            for j in range(width):
                row = t * width + j
                slot, step = slot_and_step(row)
                main = source_ref[row]
                before, after = shifted(main, sides_ref[step], slot, amount)
                place(j, main, before, after)
            product = jnp.dot(
                weight_ref[...], rhs_ref[:, : width * segment], preferred_element_type=jnp.float32
            )
            for j in range(width):
                product_ref[t * width + j] = product[:, j * segment : (j + 1) * segment]
            return 0

        lax.fori_loop(0, total // width, body, 0)

    conv(x_ref, edge_ref, w1_ref, p1_ref, all_rows, d1, 4)

    for q in range(steps):
        main = edge_ref[q]
        wide = main.astype(jnp.float32)
        place(
            0, main, pltpu.roll(wide, d1, 1).astype(jnp.bfloat16),
            pltpu.roll(wide, segment - d1, 1).astype(jnp.bfloat16),
        )
        p1e_ref[q] = jnp.dot(w1_ref[...], rhs_ref[:, :segment], preferred_element_type=jnp.float32)

    def three(product_ref, row, apart):
        return (
            product_ref[row, 0:channels]
            + product_ref[row + apart, channels : 2 * channels]
            + product_ref[row + 2 * apart, 2 * channels :]
        )

    def silu(v):
        return v / (1.0 + jnp.exp(-v))

    def hidden(t, _):
        for j in range(4):
            row = 4 * t + j
            outside = ((row < d2) & (first_row == 1)) | ((row >= d2 + rows) & (last_row == 1))
            value = silu(three(p1_ref, row, d1))
            hid_ref[row] = jnp.where(outside, 0.0, value).astype(jnp.bfloat16)
        return 0

    lax.fori_loop(0, hidden_rows // 4, hidden, 0)

    left_out = (in_slot < REACH) & (first_col == 1)
    right_out = (in_slot >= half + 2) & (last_col == 1)
    for q in range(spacing):
        row = (lanes // SLOT) * spacing + q
        outside = ((row < d2) & (first_row == 1)) | ((row >= d2 + rows) & (last_row == 1)) | left_out | right_out
        value = silu(three(p1e_ref, q, d1))
        hide_ref[q] = jnp.where(outside, 0.0, value).astype(jnp.bfloat16)

    conv(hid_ref, hide_ref, w2_ref, p2_ref, hidden_rows, d2, 4)

    def finish(t, _):
        for j in range(4):
            row = 4 * t + j
            total = x_ref[row + REACH].astype(jnp.float32) + three(p2_ref, row, d2)
            feature = total.astype(jnp.bfloat16).astype(jnp.float32)
            mean = jnp.sum(feature * feature, axis=0, keepdims=True) * (1.0 / channels)
            unit_ref[row] = (feature * lax.rsqrt(mean + epsilon)).astype(jnp.bfloat16)
        return 0

    lax.fori_loop(0, rows // 4, finish, 0)


def unit_features(index, place, top, mid, bottom, own, partner, cross, w1, w2):
    _, rows, channels, segment = mid.shape
    steps = own.shape[1]
    spacing = steps - 2 * FIRST_DILATION
    hidden_rows = rows + 2 * SECOND_DILATION
    all_rows = rows + 2 * REACH

    def image_of(a):
        return pl.BlockSpec((None,) + a.shape[1:], lambda i: (index, 0, 0, 0))

    def whole(a):
        return pl.BlockSpec(a.shape, lambda i: (0,) * a.ndim)

    return pl.pallas_call(
        functools.partial(feature_kernel, spacing=spacing),
        out_shape=jax.ShapeDtypeStruct((rows, channels, segment), jnp.bfloat16),
        grid=(1,),
        in_specs=[pl.BlockSpec(memory_space=pltpu.SMEM)]
        + [image_of(a) for a in (top, mid, bottom, own, partner, cross)]
        + [whole(w1), whole(w2)],
        out_specs=pl.BlockSpec((rows, channels, segment), lambda i: (0, 0, 0)),
        scratch_shapes=[
            pltpu.VMEM((all_rows, channels, segment), jnp.bfloat16),
            pltpu.VMEM((steps, channels, segment), jnp.bfloat16),
            pltpu.VMEM((all_rows, 3 * channels, segment), jnp.float32),
            pltpu.VMEM((steps, 3 * channels, segment), jnp.float32),
            pltpu.VMEM((hidden_rows, channels, segment), jnp.bfloat16),
            pltpu.VMEM((spacing, channels, segment), jnp.bfloat16),
            pltpu.VMEM((hidden_rows, 3 * channels, segment), jnp.float32),
            pltpu.VMEM((3 * channels, 4 * segment), jnp.bfloat16),
        ],
        name=f"unit_features_{index}",
    )(place, top, mid, bottom, own, partner, cross, w1, w2)


def correlate_kernel(
    table_ref, left_ref, even_ref, odd_ref, acc_in_ref, acc_ref, bias_ref, *, step, scale
):
    group = pl.program_id(0)
    rows, channels, segment = left_ref.shape
    block = table_ref[0, 0]
    low = segment * table_ref[1, group]
    high = low + segment * table_ref[2, group]
    base = segment * (block - 2 * (block // 2 - step))
    active = (base + segment - 1 >= low) & (base - 2 * segment + 1 < high) & (block // 2 >= step)
    if step == 0:
        acc_ref[...] = jnp.zeros_like(acc_ref)
    else:
        acc_ref[...] = acc_in_ref[...]

    @pl.when(active)
    def _():
        wide = (segment, 2 * segment)
        offsets = base + lax.broadcasted_iota(jnp.int32, wide, 0) - lax.broadcasted_iota(jnp.int32, wide, 1)
        inside = (offsets >= low) & (offsets < high)
        bias_ref[...] = jnp.where(inside, 0.0, -1e30)
        kind = lax.broadcasted_iota(jnp.int32, (16, 2 * segment), 0)
        column = lax.broadcasted_iota(jnp.int32, (16, 2 * segment), 1)
        extra = jnp.where(kind == 0, 1, jnp.where(kind == 1, column, jnp.where(kind == 2, step, 0)))
        extra = extra.astype(jnp.float32).astype(jnp.bfloat16)
        for r in range(rows):
            keys = jnp.concatenate([even_ref[r], odd_ref[r]], axis=1)
            scores = lax.dot_general(
                left_ref[r], keys, (((0,), (0,)), ((), ())), preferred_element_type=jnp.float32
            )
            weights = jnp.exp2(scores * scale + bias_ref[...]).astype(jnp.bfloat16)
            extended = jnp.concatenate([keys, extra], axis=0)
            acc_ref[r, :, 0 : channels + 16] += lax.dot_general(
                weights, extended, (((1,), (1,)), ((), ())), preferred_element_type=jnp.float32
            )


def correlate(table, left, even, odd, acc, step):
    rows, channels, segment = left.shape
    scale = sharpness_divisor / channels * LOG2E
    acc_spec = pl.BlockSpec((RG, segment, 128), lambda g: (g, 0, 0))
    row_spec = pl.BlockSpec((RG, channels, segment), lambda g: (g, 0, 0))
    first = acc is None
    if first:
        acc = jnp.zeros((8, 128), jnp.float32)
    return pl.pallas_call(
        functools.partial(correlate_kernel, step=step, scale=scale),
        out_shape=jax.ShapeDtypeStruct((rows, segment, 128), jnp.float32),
        grid=(rows // RG,),
        in_specs=[
            pl.BlockSpec(memory_space=pltpu.SMEM),
            row_spec,
            row_spec,
            row_spec,
            pl.BlockSpec((8, 128), lambda g: (0, 0)) if first else acc_spec,
        ],
        out_specs=acc_spec,
        scratch_shapes=[pltpu.VMEM((segment, 2 * segment), jnp.float32)],
        input_output_aliases={} if first else {4: 0},
        name=f"correlate_{step}",
    )(table, left, even, odd, acc)


def finish_kernel(table_ref, acc_ref, matched_ref, disparity_ref, *, channels):
    group = pl.program_id(0)
    rows, segment, _ = acc_ref.shape
    block = table_ref[0, 0]
    low = segment * table_ref[1, group]
    high = low + segment * table_ref[2, group]
    x = block * segment + lax.broadcasted_iota(jnp.int32, (1, segment), 1)
    start = jnp.maximum(low, x + 1)
    beyond = jnp.maximum(high - start, 0)
    beyond_sum = ((start + high - 1) * beyond).astype(jnp.float32) * 0.5
    beyond = beyond.astype(jnp.float32)
    xf = x.astype(jnp.float32)
    chip = (block // 2).astype(jnp.float32)
    for r in range(rows):
        turned = acc_ref[r].T
        near = turned[channels : channels + 1]
        column = turned[channels + 1 : channels + 2]
        steps = turned[channels + 2 : channels + 3]
        norm = near + beyond
        shift = (xf - 2 * segment * chip) * near - column + (2 * segment) * steps + beyond_sum
        matched_ref[r] = (turned[:channels] / norm).astype(jnp.bfloat16)
        disparity_ref[r : r + 1, :] = shift / norm * (1.0 / segment)


def finish(table, acc, channels):
    rows, segment, _ = acc.shape
    return pl.pallas_call(
        functools.partial(finish_kernel, channels=channels),
        out_shape=(
            jax.ShapeDtypeStruct((rows, channels, segment), jnp.bfloat16),
            jax.ShapeDtypeStruct((rows, segment), jnp.float32),
        ),
        grid=(rows // RG,),
        in_specs=[
            pl.BlockSpec(memory_space=pltpu.SMEM),
            pl.BlockSpec((RG, segment, 128), lambda g: (g, 0, 0)),
        ],
        out_specs=(
            pl.BlockSpec((RG, channels, segment), lambda g: (g, 0, 0)),
            pl.BlockSpec((RG, segment), lambda g: (g, 0)),
        ),
        name="finish",
    )(table, acc)


def both_ways(pairs):
    return pairs + [(b, a) for a, b in pairs]


def stacked(weight):
    taps, out_channels, in_channels = weight.shape
    split = weight.reshape(3, 3, out_channels, in_channels).transpose(0, 2, 1, 3)
    return split.reshape(3 * out_channels, 3 * in_channels)


def per_device(images, first_weight, second_weight, search_ranges):
    row_count = lax.axis_size("rows")
    col_count = lax.axis_size("cols")
    row = lax.axis_index("rows")
    col = lax.axis_index("cols")
    rows = images.shape[2]
    segment = images.shape[3]
    channels = images.shape[1]
    odd = col % 2

    mid = images.transpose(0, 2, 1, 3)
    top_rows = mid[:, :REACH]
    bottom_rows = mid[:, rows - REACH :]
    up = [(i, i + 1) for i in range(row_count - 1)]
    top = lax.ppermute(bottom_rows, "rows", up)
    bottom = lax.ppermute(top_rows, "rows", [(b, a) for a, b in up])
    own = pack_edges(top, mid, bottom)
    partner = lax.ppermute(own, "cols", [(i, i ^ 1) for i in range(col_count)])
    cross = lax.ppermute(own, "cols", both_ways([(i, i + 1) for i in range(1, col_count - 1, 2)]))
    place = jnp.stack(
        [row == 0, row == row_count - 1, col == 0, col == col_count - 1, odd == 1]
    ).astype(jnp.int32)
    w1, w2 = stacked(first_weight), stacked(second_weight)
    shared = (place, top, mid, bottom, own, partner, cross, w1, w2)
    right = unit_features(1, *shared)

    groups = rows // RG
    table = jnp.concatenate(
        [jnp.full((1, groups), col, jnp.int32), search_ranges.reshape(2, groups)], axis=0
    )
    chips = col_count // 2
    last = min(chips - 1, (HOPS - 1 + 1) // 2)
    swap = [(i, i ^ 1) for i in range(col_count)]
    hop = [(i, i + 2) for i in range(col_count - 2)]

    def pair(mine):
        theirs = lax.ppermute(mine, "cols", swap)
        return jnp.where(odd == 1, theirs, mine), jnp.where(odd == 1, mine, theirs)

    left = unit_features(0, *shared)
    acc = None
    mine = right
    for step in range(last + 1):
        if step:
            mine = lax.ppermute(mine, "cols", hop)
        even_keys, odd_keys = pair(mine)
        acc = correlate(table, left, even_keys, odd_keys, acc, step)
    matched, disparity = finish(table, acc, channels)
    return matched.transpose(1, 0, 2), disparity


def solution(mesh):
    placed = (P(None, None, "rows", "cols"), P(), P(), P(None, "rows", "cols"))
    return jax.shard_map(
        per_device,
        mesh=mesh,
        in_specs=placed,
        out_specs=(P(None, "rows", "cols"), P("rows", "cols")),
        check_vma=False,
    )
```

```python
import functools

import jax
import jax.numpy as jnp
from jax import lax
from jax.experimental import pallas as pl
from jax.experimental.pallas import tpu as pltpu
from jax.sharding import PartitionSpec as P


RG = 8
FIRST_DILATION = 2
SECOND_DILATION = 4
HOPS = 18
REACH = FIRST_DILATION + SECOND_DILATION
SLOT = 16

sharpness_divisor = 10.0
epsilon = 1e-05
VMEM_LIMIT = 64 << 20
LOG2E = 1.4426950408889634


def lane_iota(shape):
    return lax.broadcasted_iota(jnp.int32, shape, len(shape) - 1)


def cost(microseconds):
    return pl.CostEstimate(
        flops=int(microseconds * 1e9), transcendentals=0, bytes_accessed=int(microseconds * 3e6)
    )


def pack_kernel(x_ref, edge_ref, *, groups, spacing, offset):
    channels, segment = x_ref.shape[1:]
    slot_of = lane_iota((channels, segment)) // SLOT
    for q in range(edge_ref.shape[0]):
        packed = None
        for g in range(groups):
            shift = (SLOT * g + SLOT // 2) % segment
            moved = pltpu.roll(x_ref[offset + g * spacing + q], shift, 1)
            packed = moved if packed is None else jnp.where(slot_of == g, moved, packed)
        edge_ref[q] = packed


def edge_steps(rows, segment):
    spacing = (rows + 2 * SECOND_DILATION) // (segment // SLOT)
    return spacing, spacing + 2 * FIRST_DILATION


def pack_edges(x, rows, offset):
    parts, held, channels, segment = x.shape
    spacing, steps = edge_steps(rows, segment)
    return pl.pallas_call(
        functools.partial(pack_kernel, groups=segment // SLOT, spacing=spacing, offset=offset),
        out_shape=jax.ShapeDtypeStruct((parts, steps, channels, segment), jnp.bfloat16),
        grid=(parts,),
        in_specs=[pl.BlockSpec((None, held, channels, segment), lambda n: (n, 0, 0, 0))],
        out_specs=pl.BlockSpec((None, steps, channels, segment), lambda n: (n, 0, 0, 0)),
        compiler_params=pltpu.CompilerParams(vmem_limit_bytes=VMEM_LIMIT),
        cost_estimate=cost(2),
    )(x)


def feature_kernel(
    place_ref, x_ref, own_ref, partner_ref, cross_ref, w1_ref, w2_ref, unit_ref,
    w_ref, edge_ref, side_ref, p1_ref, p1e_ref, hid_ref, hide_ref, p2_ref, rhs0_ref, rhs1_ref,
    *, spacing, offset, ends, mesh_shape,
):
    part = pl.program_id(0)
    rows = unit_ref.shape[0]
    channels, segment = x_ref.shape[1:]
    first_row, last_row = place_ref[0] == 0, place_ref[0] == mesh_shape[0] - 1
    first_col, last_col = place_ref[1] == 0, place_ref[1] == mesh_shape[1] - 1
    odd = place_ref[1] % 2 == 1
    above = first_row & (part == 0) & ends
    below = last_row & (part == pl.num_programs(0) - 1) & ends
    d1, d2 = FIRST_DILATION, SECOND_DILATION
    all_rows = rows + 2 * REACH
    hidden_rows = rows + 2 * d2
    steps = edge_ref.shape[0]
    groups = segment // SLOT
    lanes = lane_iota((channels, segment))
    in_slot = lanes % SLOT
    half = SLOT // 2
    rhs = (rhs0_ref, rhs1_ref)
    width = rhs0_ref.shape[1] // segment

    def stack(taps_ref):
        for a in range(3):
            for b in range(3):
                w_ref[a * channels : (a + 1) * channels, b * channels : (b + 1) * channels] = taps_ref[3 * a + b]

    for q in range(steps):
        own = own_ref[q]
        partner = partner_ref[q]
        cross = cross_ref[q]
        left = jnp.where(odd, partner, cross)
        right = jnp.where(odd, cross, partner)
        shift = half - REACH
        lower = pltpu.roll(jnp.where(in_slot < half, left, own), segment - shift, 1)
        upper = pltpu.roll(jnp.where(in_slot < half, own, right), shift, 1)
        edge_ref[q] = jnp.where(in_slot < half, lower, upper)
        side_ref[q] = pltpu.roll(jnp.where(in_slot < half, left, right), segment - shift, 1)

    def shifted(main, side, slot, amount):
        aligned = pltpu.roll(side, segment - REACH - slot * SLOT, 1)
        before = pltpu.roll(jnp.where(lanes >= segment - amount, aligned, main), amount, 1)
        after = pltpu.roll(jnp.where(lanes < amount, aligned, main), segment - amount, 1)
        return before, after

    def put(target, j, main, before, after):
        lo = j * segment
        target[0:channels, lo : lo + segment] = before
        target[channels : 2 * channels, lo : lo + segment] = main
        target[2 * channels :, lo : lo + segment] = after

    def multiply(source, product_ref, base):
        product = jnp.dot(w_ref[...], source[...], preferred_element_type=jnp.float32)
        for j in range(width):
            product_ref[base + j] = product[:, j * segment : (j + 1) * segment]

    def conv(source_ref, skip, sides_ref, product_ref, total, amount):
        def build(t, target):
            for j in range(width):
                row = jnp.minimum(t * width + j, total - 1)
                slot = jnp.minimum(row // spacing, groups - 1)
                main = source_ref[row + skip]
                put(target, j, main, *shifted(main, sides_ref[row - slot * spacing], slot, amount))

        build(0, rhs0_ref)

        def body(u, _):
            build(2 * u + 1, rhs1_ref)
            multiply(rhs0_ref, product_ref, 2 * u * width)
            build(2 * u + 2, rhs0_ref)
            multiply(rhs1_ref, product_ref, (2 * u + 1) * width)
            return 0

        lax.fori_loop(0, pl.cdiv(total, 2 * width), body, 0)

    stack(w1_ref)
    conv(x_ref, offset, side_ref, p1_ref, all_rows, d1)

    for t in range(pl.cdiv(steps, width)):
        target = rhs[t % 2]
        for j in range(width):
            main = edge_ref[min(t * width + j, steps - 1)]
            put(target, j, main, pltpu.roll(main, d1, 1), pltpu.roll(main, segment - d1, 1))
        multiply(target, p1e_ref, t * width)

    def three(product_ref, row, apart):
        return (
            product_ref[row, 0:channels]
            + product_ref[row + apart, channels : 2 * channels]
            + product_ref[row + 2 * apart, 2 * channels :]
        )

    def silu(v):
        return v / (1.0 + jnp.exp(-v))

    def hidden(t, _):
        for j in range(8):
            row = 8 * t + j
            outside = ((row < d2) & above) | ((row >= d2 + rows) & below)
            value = silu(three(p1_ref, row, d1))
            hid_ref[row] = jnp.where(outside, 0.0, value).astype(jnp.bfloat16)
        return 0

    lax.fori_loop(0, hidden_rows // 8, hidden, 0)

    left_out = (in_slot < REACH) & first_col
    right_out = (in_slot >= half + 2) & last_col
    for q in range(spacing):
        row = (lanes // SLOT) * spacing + q
        outside = ((row < d2) & above) | ((row >= d2 + rows) & below) | left_out | right_out
        value = silu(three(p1e_ref, q, d1))
        value = jnp.where(outside, 0.0, value).astype(jnp.bfloat16)
        gap = half + 2 - REACH
        hide_ref[q] = jnp.where(in_slot < REACH, value, pltpu.roll(value, segment - gap, 1))

    stack(w2_ref)
    conv(hid_ref, 0, hide_ref, p2_ref, hidden_rows, d2)

    def finish(t, _):
        for j in range(8):
            row = 8 * t + j
            total = x_ref[row + offset + REACH].astype(jnp.float32) + three(p2_ref, row, d2)
            feature = total.astype(jnp.bfloat16).astype(jnp.float32)
            mean = jnp.sum(feature * feature, axis=0, keepdims=True) * (1.0 / channels)
            unit_ref[row] = (feature * lax.rsqrt(mean + epsilon)).astype(jnp.bfloat16)
        return 0

    lax.fori_loop(0, rows // 8, finish, 0)


def unit_features(place, x, rows, offset, ends, edges, w1, w2, mesh_shape):
    parts, _, channels, segment = x.shape
    all_rows = rows + 2 * REACH
    hidden_rows = rows + 2 * SECOND_DILATION
    spacing, steps = edge_steps(rows, segment)
    width = 8

    def part_of(a):
        return pl.BlockSpec((None,) + a.shape[1:], lambda i: (i, 0, 0, 0))

    def whole(a):
        return pl.BlockSpec(a.shape, lambda i: (0,) * a.ndim)

    def up_to(n, m):
        return pl.cdiv(n, m) * m

    products = (3 * channels, segment)
    return pl.pallas_call(
        functools.partial(
            feature_kernel, spacing=spacing, offset=offset, ends=ends, mesh_shape=mesh_shape
        ),
        out_shape=jax.ShapeDtypeStruct((parts, rows, channels, segment), jnp.bfloat16),
        grid=(parts,),
        in_specs=[pl.BlockSpec(memory_space=pltpu.SMEM)]
        + [part_of(a) for a in (x, *edges)]
        + [whole(w1), whole(w2)],
        out_specs=pl.BlockSpec((None, rows, channels, segment), lambda i: (i, 0, 0, 0)),
        scratch_shapes=[
            pltpu.VMEM((3 * channels, 3 * channels), jnp.bfloat16),
            pltpu.VMEM((steps, channels, segment), jnp.bfloat16),
            pltpu.VMEM((steps, channels, segment), jnp.bfloat16),
            pltpu.VMEM((up_to(all_rows, 2 * width),) + products, jnp.float32),
            pltpu.VMEM((up_to(steps, width),) + products, jnp.float32),
            pltpu.VMEM((hidden_rows, channels, segment), jnp.bfloat16),
            pltpu.VMEM((spacing, channels, segment), jnp.bfloat16),
            pltpu.VMEM((up_to(hidden_rows, 2 * width),) + products, jnp.float32),
            pltpu.VMEM((3 * channels, width * segment), jnp.bfloat16),
            pltpu.VMEM((3 * channels, width * segment), jnp.bfloat16),
        ],
        compiler_params=pltpu.CompilerParams(vmem_limit_bytes=VMEM_LIMIT),
        cost_estimate=cost(parts * rows * 0.2),
    )(place, x, *edges, w1, w2)


def add_step(place_ref, range_ref, group, step, left_ref, mine_ref, theirs_ref, acc_ref, bias_ref):
    _, channels, segment = left_ref.shape
    block = place_ref[1]
    low = segment * range_ref[0, group]
    high = low + segment * range_ref[1, group]
    odd = block % 2
    base = segment * (block - 2 * (block // 2 - step))
    active = (base + segment - 1 >= low) & (base - 2 * segment + 1 < high) & (block // 2 >= step)
    scale = sharpness_divisor / channels * LOG2E

    def key_column(shape):
        column = lane_iota(shape)
        own = column < segment
        return column % segment + segment * jnp.where(own, odd, 1 - odd)

    @pl.when(active)
    def _():
        wide = (segment, 2 * segment)
        offsets = base + lax.broadcasted_iota(jnp.int32, wide, 0) - key_column(wide)
        inside = (offsets >= low) & (offsets < high)
        bias_ref[...] = jnp.where(inside, 0.0, -1e30)
        kind = lax.broadcasted_iota(jnp.int32, (16, 2 * segment), 0)
        column = key_column((16, 2 * segment))
        extra = jnp.where(kind == 0, 1, jnp.where(kind == 1, column, jnp.where(kind == 2, step, 0)))
        extra = extra.astype(jnp.float32).astype(jnp.bfloat16)
        for r in range(left_ref.shape[0]):
            keys = jnp.concatenate([mine_ref[r], theirs_ref[r]], axis=1)
            scores = lax.dot_general(
                left_ref[r], keys, (((0,), (0,)), ((), ())), preferred_element_type=jnp.float32
            )
            weights = jnp.exp2(scores * scale + bias_ref[...]).astype(jnp.bfloat16)
            extended = jnp.concatenate([keys, extra], axis=0)
            acc_ref[r, :, 0 : channels + 16] += lax.dot_general(
                weights, extended, (((1,), (1,)), ((), ())), preferred_element_type=jnp.float32
            )


def group_of(i, inner, groups):
    return i + 1 if inner else i * (groups - 1)


def gather_kernel(place_ref, range_ref, left_ref, *refs, inner, groups):
    keys, (acc_ref, bias_ref) = refs[:-2], refs[-2:]
    group = group_of(pl.program_id(0), inner, groups)
    acc_ref[...] = jnp.zeros_like(acc_ref)
    for step in range(len(keys) // 2):
        add_step(
            place_ref, range_ref, group, step, left_ref, keys[2 * step], keys[2 * step + 1],
            acc_ref, bias_ref,
        )


def finish_kernel(
    place_ref, range_ref, left_ref, mine_ref, theirs_ref, acc_in_ref, *refs, inner, groups, step
):
    matched_ref, disparity_ref, acc_ref, bias_ref, rows_ref = refs[-5:]
    group = group_of(pl.program_id(0), inner, groups)
    rows, channels, segment = left_ref.shape
    acc_ref[...] = acc_in_ref[...]
    add_step(
        place_ref, range_ref, group, step, left_ref, mine_ref, theirs_ref, acc_ref, bias_ref
    )
    block = place_ref[1]
    low = segment * range_ref[0, group]
    high = low + segment * range_ref[1, group]
    x = block * segment + lane_iota((1, segment))
    from_chip = (x - 2 * segment * (block // 2)).astype(jnp.float32)
    start = jnp.maximum(low, x + 1)
    beyond = jnp.maximum(high - start, 0)
    beyond_sum = ((start + high - 1) * beyond).astype(jnp.float32) * 0.5
    beyond = beyond.astype(jnp.float32)
    for r in range(rows):
        turned = acc_ref[r].T
        near = turned[channels : channels + 1]
        column = turned[channels + 1 : channels + 2]
        passed = turned[channels + 2 : channels + 3]
        inverse = 1.0 / (near + beyond)
        shift = from_chip * near - column + (2 * segment) * passed + beyond_sum
        rows_ref[r] = turned[:channels] * inverse
        disparity_ref[r : r + 1, :] = shift * inverse * (1.0 / segment)
    matched_ref[...] = jnp.swapaxes(rows_ref[...].astype(jnp.bfloat16), 0, 1)


def correlate(place, ranges, left, keys, inner):
    rows, channels, segment = left.shape
    groups = rows // RG
    own_groups = keys[0][0].shape[0] // RG
    block = (RG, channels, segment)
    smem = pl.BlockSpec(memory_space=pltpu.SMEM)
    return pl.pallas_call(
        functools.partial(gather_kernel, inner=inner, groups=groups),
        out_shape=jax.ShapeDtypeStruct((own_groups * RG, segment, 128), jnp.float32),
        grid=(own_groups,),
        in_specs=[smem, smem, pl.BlockSpec(block, lambda i: (group_of(i, inner, groups), 0, 0))]
        + [pl.BlockSpec(block, lambda i: (i, 0, 0))] * (2 * len(keys)),
        out_specs=pl.BlockSpec((RG, segment, 128), lambda i: (i, 0, 0)),
        scratch_shapes=[pltpu.VMEM((segment, 2 * segment), jnp.float32)],
        compiler_params=pltpu.CompilerParams(vmem_limit_bytes=VMEM_LIMIT),
        cost_estimate=cost(1.5 * own_groups),
    )(place, ranges, left, *[a for pair in keys for a in pair])


def finish(place, ranges, left, pair, acc, outs, inner, step):
    rows, channels, segment = left.shape
    groups = rows // RG
    own_groups = acc.shape[0] // RG
    block = (RG, channels, segment)
    smem = pl.BlockSpec(memory_space=pltpu.SMEM)

    def group(i):
        return group_of(i, inner, groups)

    given = () if outs is None else tuple(outs)
    return pl.pallas_call(
        functools.partial(finish_kernel, inner=inner, groups=groups, step=step),
        out_shape=(
            jax.ShapeDtypeStruct((channels, rows, segment), jnp.bfloat16),
            jax.ShapeDtypeStruct((rows, segment), jnp.float32),
        ),
        grid=(own_groups,),
        in_specs=[
            smem,
            smem,
            pl.BlockSpec(block, lambda i: (group(i), 0, 0)),
            pl.BlockSpec(block, lambda i: (i, 0, 0)),
            pl.BlockSpec(block, lambda i: (i, 0, 0)),
            pl.BlockSpec((RG, segment, 128), lambda i: (i, 0, 0)),
        ]
        + [pl.BlockSpec(memory_space=pl.ANY)] * len(given),
        out_specs=(
            pl.BlockSpec((channels, RG, segment), lambda i: (0, group(i), 0)),
            pl.BlockSpec((RG, segment), lambda i: (group(i), 0)),
        ),
        scratch_shapes=[
            pltpu.VMEM((RG, segment, 128), jnp.float32),
            pltpu.VMEM((segment, 2 * segment), jnp.float32),
            pltpu.VMEM((RG, channels, segment), jnp.float32),
        ],
        input_output_aliases={6: 0, 7: 1} if given else {},
        compiler_params=pltpu.CompilerParams(vmem_limit_bytes=VMEM_LIMIT),
        cost_estimate=cost(own_groups),
    )(place, ranges, left, *pair, acc, *given)


def both_ways(pairs):
    return pairs + [(b, a) for a, b in pairs]


def program(images, first_weight, second_weight, search_ranges):
    row_count = lax.axis_size("rows")
    col_count = lax.axis_size("cols")
    col = lax.axis_index("cols")
    channels, rows, segment = images.shape[1:]
    place = jnp.stack([lax.axis_index("rows"), col]).astype(jnp.int32)
    ranges = search_ranges.reshape(2, rows // RG)

    swap = [(i, i ^ 1) for i in range(col_count)]
    across = both_ways([(i, i + 1) for i in range(1, col_count - 1, 2)])
    hop = [(i, (i + 2) % col_count) for i in range(col_count)]
    down = [(i, i + 1) for i in range(row_count - 1)]
    up = [(b, a) for a, b in down]

    def exchanged(x, count, offset):
        own = pack_edges(x, count, offset)
        cross = lax.ppermute(own, "cols", across)
        partner = lax.ppermute(own, "cols", swap)
        return own, partner, cross

    def features(x, count, offset, ends, edges):
        return unit_features(
            place, x, count, offset, ends, edges, first_weight, second_weight,
            (row_count, col_count),
        )

    inner = rows - 2 * RG
    right_rows = images[1].transpose(1, 0, 2)
    edges_a = exchanged(right_rows[None], inner, RG - REACH)

    later, edges_a = lax.optimization_barrier((images, edges_a[0])), edges_a
    later = later[0]
    top = lax.ppermute(later[:, :, rows - REACH :].transpose(0, 2, 1, 3), "rows", down)
    bottom = lax.ppermute(later[:, :, :REACH].transpose(0, 2, 1, 3), "rows", up)
    right_a = features(right_rows[None], inner, RG - REACH, False, edges_a)[0]

    top, bottom, _ = lax.optimization_barrier((top, bottom, right_a[:1, :8]))
    outer = jnp.stack(
        [
            jnp.concatenate([top[1], right_rows[: RG + REACH]]),
            jnp.concatenate([right_rows[rows - RG - REACH :], bottom[1]]),
        ]
    )
    edges_b = exchanged(outer, RG, 0)
    right_b = features(outer, RG, 0, True, edges_b).reshape(2 * RG, channels, segment)

    left_rows = jnp.concatenate([top[0], later[0].transpose(1, 0, 2), bottom[0]])[None]
    edges_l = exchanged(left_rows, rows, 0)
    left = features(left_rows, rows, 0, True, edges_l)[0]

    steps = min(col_count // 2 - 1, HOPS // 2)

    def pair(mine):
        return mine, lax.ppermute(mine, "cols", swap)

    def chain(mine):
        pairs = [pair(mine)]
        for _ in range(1, steps + 1):
            mine = lax.ppermute(mine, "cols", hop)
            pairs.append(pair(mine))
        return pairs

    keys_a, keys_b = chain(right_a), chain(right_b)
    acc_a = correlate(place, ranges, left, keys_a[:-1], True)
    acc_b = correlate(place, ranges, left, keys_b[:-1], False)
    outs = finish(place, ranges, left, keys_a[-1], acc_a, None, True, steps)
    return finish(place, ranges, left, keys_b[-1], acc_b, outs, False, steps)


def solution(mesh):
    placed = (P(None, None, "rows", "cols"), P(), P(), P(None, "rows", "cols"))
    return jax.shard_map(
        program,
        mesh=mesh,
        in_specs=placed,
        out_specs=(P(None, "rows", "cols"), P("rows", "cols")),
        check_vma=False,
    )
```

```python
import functools

import jax
import jax.numpy as jnp
from jax import lax
from jax.experimental import pallas as pl
from jax.experimental.pallas import tpu as pltpu
from jax.sharding import PartitionSpec as P


RG = 8
FIRST_DILATION = 2
SECOND_DILATION = 4
HOPS = 18
REACH = FIRST_DILATION + SECOND_DILATION
SLOT = 16

sharpness_divisor = 10.0
epsilon = 1e-05
VMEM_LIMIT = 64 << 20
LOG2E = 1.4426950408889634


def lane_iota(shape):
    return lax.broadcasted_iota(jnp.int32, shape, len(shape) - 1)


def cost(microseconds):
    return pl.CostEstimate(
        flops=int(microseconds * 1e9), transcendentals=0, bytes_accessed=int(microseconds * 3e6)
    )


def cost(microseconds):
    return pl.CostEstimate(
        flops=int(microseconds * 1e9), transcendentals=0, bytes_accessed=int(microseconds * 3e6)
    )


def rows_kernel(place_ref, image_ref, above_ref, below_ref, x_ref, *, last_row):
    rows = image_ref.shape[1]
    held = above_ref.shape[1]
    inside_above = (place_ref[0] > 0).astype(jnp.float32)
    inside_below = (place_ref[0] < last_row).astype(jnp.float32)

    def turned(piece, keep):
        piece = jnp.swapaxes(piece, 0, 1)
        return (piece.astype(jnp.float32) * keep).astype(jnp.bfloat16)

    x_ref[0:REACH] = turned(above_ref[...], inside_above)[held - REACH :]
    for start in range(0, rows, 16):
        x_ref[REACH + start : REACH + start + 16] = jnp.swapaxes(image_ref[:, start : start + 16], 0, 1)
    x_ref[REACH + rows :] = turned(below_ref[...], inside_below)[:REACH]


def with_rows(place, images, above, below, row_count):
    count, channels, rows, segment = images.shape
    held = above.shape[2]

    def image_of(extent):
        return pl.BlockSpec((None, channels, extent, segment), lambda n: (n, 0, 0, 0))

    all_rows = rows + 2 * REACH
    return pl.pallas_call(
        functools.partial(rows_kernel, last_row=row_count - 1),
        out_shape=jax.ShapeDtypeStruct((count, all_rows, channels, segment), jnp.bfloat16),
        grid=(count,),
        in_specs=[pl.BlockSpec(memory_space=pltpu.SMEM), image_of(rows), image_of(held), image_of(held)],
        out_specs=pl.BlockSpec((None, all_rows, channels, segment), lambda n: (n, 0, 0, 0)),
        compiler_params=pltpu.CompilerParams(vmem_limit_bytes=VMEM_LIMIT),
        cost_estimate=cost(3),
        name="with_rows",
    )(place, images, above, below)


def pack_into(x_ref, edge_ref, base, rows, first):
    channels, segment = x_ref.shape[1:]
    slot_of = lane_iota((channels, segment)) // SLOT
    spacing, steps = edge_steps(rows, segment)
    for q in range(steps):
        packed = None
        for g in range(segment // SLOT):
            shift = (SLOT * g + SLOT // 2) % segment
            moved = pltpu.roll(x_ref[first + g * spacing + q], shift, 1)
            packed = moved if packed is None else jnp.where(slot_of == g, moved, packed)
        edge_ref[base + q] = packed


def edge_steps(rows, segment):
    spacing = (rows + 2 * SECOND_DILATION) // (segment // SLOT)
    return spacing, spacing + 2 * FIRST_DILATION


def pack_kernel(*refs, chunks):
    edge_ref = refs[-1]
    base = 0
    for index, rows, first in chunks:
        pack_into(refs[index], edge_ref, base, rows, first)
        base += edge_steps(rows, edge_ref.shape[2])[1]


def pack_edges(sources, chunks):
    channels, segment = sources[0][0].shape[2:]
    total = sum(edge_steps(rows, segment)[1] for _, rows, _ in chunks)

    def image_of(a, n):
        return pl.BlockSpec((None,) + a.shape[1:], lambda i: (n, 0, 0, 0))

    return pl.pallas_call(
        functools.partial(pack_kernel, chunks=chunks),
        out_shape=jax.ShapeDtypeStruct((total, channels, segment), jnp.bfloat16),
        grid=(1,),
        in_specs=[image_of(a, n) for a, n in sources],
        out_specs=pl.BlockSpec((total, channels, segment), lambda i: (0, 0, 0)),
        compiler_params=pltpu.CompilerParams(vmem_limit_bytes=VMEM_LIMIT),
        cost_estimate=cost(2),
    )(*[a for a, _ in sources])


def feature_kernel(
    place_ref, x_ref, own_ref, partner_ref, cross_ref, w1_ref, w2_ref, unit_ref,
    w_ref, edge_ref, side_ref, p1_ref, p1e_ref, hid_ref, hide_ref, p2_ref, rhs0_ref, rhs1_ref,
    *, spacing, offset, apart, ends, mesh_shape,
):
    part = pl.program_id(0)
    offset = offset + part * apart
    rows = unit_ref.shape[0]
    channels, segment = x_ref.shape[1:]
    first_row, last_row = place_ref[0] == 0, place_ref[0] == mesh_shape[0] - 1
    first_col, last_col = place_ref[1] == 0, place_ref[1] == mesh_shape[1] - 1
    odd = place_ref[1] % 2 == 1
    above = first_row & (part == 0) & ends
    below = last_row & (part == pl.num_programs(0) - 1) & ends
    d1, d2 = FIRST_DILATION, SECOND_DILATION
    all_rows = rows + 2 * REACH
    hidden_rows = rows + 2 * d2
    steps = edge_ref.shape[0]
    groups = segment // SLOT
    lanes = lane_iota((channels, segment))
    in_slot = lanes % SLOT
    half = SLOT // 2
    rhs = (rhs0_ref, rhs1_ref)
    width = rhs0_ref.shape[1] // segment

    def stack(taps_ref):
        for a in range(3):
            for b in range(3):
                w_ref[a * channels : (a + 1) * channels, b * channels : (b + 1) * channels] = taps_ref[3 * a + b]

    for q in range(steps):
        own = own_ref[q]
        partner = partner_ref[q]
        cross = cross_ref[q]
        left = jnp.where(odd, partner, cross)
        right = jnp.where(odd, cross, partner)
        shift = half - REACH
        lower = pltpu.roll(jnp.where(in_slot < half, left, own), segment - shift, 1)
        upper = pltpu.roll(jnp.where(in_slot < half, own, right), shift, 1)
        edge_ref[q] = jnp.where(in_slot < half, lower, upper)
        side_ref[q] = pltpu.roll(jnp.where(in_slot < half, left, right), segment - shift, 1)

    def shifted(main, side, slot, amount):
        aligned = pltpu.roll(side, segment - REACH - slot * SLOT, 1)
        before = pltpu.roll(jnp.where(lanes >= segment - amount, aligned, main), amount, 1)
        after = pltpu.roll(jnp.where(lanes < amount, aligned, main), segment - amount, 1)
        return before, after

    def put(target, j, main, before, after):
        lo = j * segment
        target[0:channels, lo : lo + segment] = before
        target[channels : 2 * channels, lo : lo + segment] = main
        target[2 * channels :, lo : lo + segment] = after

    def multiply(source, product_ref, base):
        product = jnp.dot(w_ref[...], source[...], preferred_element_type=jnp.float32)
        for j in range(width):
            product_ref[base + j] = product[:, j * segment : (j + 1) * segment]

    def conv(source_ref, skip, sides_ref, product_ref, total, amount):
        def build(t, target):
            for j in range(width):
                row = jnp.minimum(t * width + j, total - 1)
                slot = jnp.minimum(row // spacing, groups - 1)
                main = source_ref[row + skip]
                put(target, j, main, *shifted(main, sides_ref[row - slot * spacing], slot, amount))

        build(0, rhs0_ref)

        def body(u, _):
            build(2 * u + 1, rhs1_ref)
            multiply(rhs0_ref, product_ref, 2 * u * width)
            build(2 * u + 2, rhs0_ref)
            multiply(rhs1_ref, product_ref, (2 * u + 1) * width)
            return 0

        lax.fori_loop(0, pl.cdiv(total, 2 * width), body, 0)

    stack(w1_ref)
    conv(x_ref, offset, side_ref, p1_ref, all_rows, d1)

    for t in range(pl.cdiv(steps, width)):
        target = rhs[t % 2]
        for j in range(width):
            main = edge_ref[min(t * width + j, steps - 1)]
            put(target, j, main, pltpu.roll(main, d1, 1), pltpu.roll(main, segment - d1, 1))
        multiply(target, p1e_ref, t * width)

    def three(product_ref, row, apart):
        return (
            product_ref[row, 0:channels]
            + product_ref[row + apart, channels : 2 * channels]
            + product_ref[row + 2 * apart, 2 * channels :]
        )

    def silu(v):
        return v / (1.0 + jnp.exp(-v))

    def hidden(t, _):
        for j in range(8):
            row = 8 * t + j
            outside = ((row < d2) & above) | ((row >= d2 + rows) & below)
            value = silu(three(p1_ref, row, d1))
            hid_ref[row] = jnp.where(outside, 0.0, value).astype(jnp.bfloat16)
        return 0

    lax.fori_loop(0, hidden_rows // 8, hidden, 0)

    left_out = (in_slot < REACH) & first_col
    right_out = (in_slot >= half + 2) & last_col
    for q in range(spacing):
        row = (lanes // SLOT) * spacing + q
        outside = ((row < d2) & above) | ((row >= d2 + rows) & below) | left_out | right_out
        value = silu(three(p1e_ref, q, d1))
        value = jnp.where(outside, 0.0, value).astype(jnp.bfloat16)
        gap = half + 2 - REACH
        hide_ref[q] = jnp.where(in_slot < REACH, value, pltpu.roll(value, segment - gap, 1))

    stack(w2_ref)
    conv(hid_ref, 0, hide_ref, p2_ref, hidden_rows, d2)

    def finish(t, _):
        for j in range(8):
            row = 8 * t + j
            total = x_ref[row + offset + REACH].astype(jnp.float32) + three(p2_ref, row, d2)
            feature = total.astype(jnp.bfloat16).astype(jnp.float32)
            mean = jnp.sum(feature * feature, axis=0, keepdims=True) * (1.0 / channels)
            unit_ref[row] = (feature * lax.rsqrt(mean + epsilon)).astype(jnp.bfloat16)
        return 0

    lax.fori_loop(0, rows // 8, finish, 0)


def unit_features(place, x, index, parts, rows, offset, apart, ends, edges, edge_block, w1, w2, mesh_shape):
    _, held, channels, segment = x.shape
    all_rows = rows + 2 * REACH
    hidden_rows = rows + 2 * SECOND_DILATION
    spacing, steps = edge_steps(rows, segment)
    width = 8

    def whole(a):
        return pl.BlockSpec(a.shape, lambda i: (0,) * a.ndim)

    def up_to(n, m):
        return pl.cdiv(n, m) * m

    products = (3 * channels, segment)
    return pl.pallas_call(
        functools.partial(
            feature_kernel, spacing=spacing, offset=offset, apart=apart, ends=ends, mesh_shape=mesh_shape
        ),
        out_shape=jax.ShapeDtypeStruct((parts * rows, channels, segment), jnp.bfloat16),
        grid=(parts,),
        in_specs=[
            pl.BlockSpec(memory_space=pltpu.SMEM),
            pl.BlockSpec((None, held, channels, segment), lambda i: (index, 0, 0, 0)),
        ]
        + [pl.BlockSpec((pl.Element(steps), pl.Element(channels), pl.Element(segment)), lambda i: (edge_block + i * steps, 0, 0)) for _ in edges]
        + [whole(w1), whole(w2)],
        out_specs=pl.BlockSpec((rows, channels, segment), lambda i: (i, 0, 0)),
        scratch_shapes=[
            pltpu.VMEM((3 * channels, 3 * channels), jnp.bfloat16),
            pltpu.VMEM((steps, channels, segment), jnp.bfloat16),
            pltpu.VMEM((steps, channels, segment), jnp.bfloat16),
            pltpu.VMEM((up_to(all_rows, 2 * width),) + products, jnp.float32),
            pltpu.VMEM((up_to(steps, width),) + products, jnp.float32),
            pltpu.VMEM((hidden_rows, channels, segment), jnp.bfloat16),
            pltpu.VMEM((spacing, channels, segment), jnp.bfloat16),
            pltpu.VMEM((up_to(hidden_rows, 2 * width),) + products, jnp.float32),
            pltpu.VMEM((3 * channels, width * segment), jnp.bfloat16),
            pltpu.VMEM((3 * channels, width * segment), jnp.bfloat16),
        ],
        compiler_params=pltpu.CompilerParams(vmem_limit_bytes=VMEM_LIMIT),
        cost_estimate=cost(parts * rows * 0.2),
    )(place, x, *edges, w1, w2)


def add_step(place_ref, range_ref, group, step, left_ref, mine_ref, theirs_ref, acc_ref, bias_ref):
    _, channels, segment = left_ref.shape
    block = place_ref[1]
    low = segment * range_ref[0, group]
    high = low + segment * range_ref[1, group]
    odd = block % 2
    base = segment * (block - 2 * (block // 2 - step))
    active = (base + segment - 1 >= low) & (base - 2 * segment + 1 < high) & (block // 2 >= step)
    scale = sharpness_divisor / channels * LOG2E

    def key_column(shape):
        column = lane_iota(shape)
        own = column < segment
        return column % segment + segment * jnp.where(own, odd, 1 - odd)

    @pl.when(active)
    def _():
        wide = (segment, 2 * segment)
        offsets = base + lax.broadcasted_iota(jnp.int32, wide, 0) - key_column(wide)
        inside = (offsets >= low) & (offsets < high)
        bias_ref[...] = jnp.where(inside, 0.0, -1e30)
        kind = lax.broadcasted_iota(jnp.int32, (16, 2 * segment), 0)
        column = key_column((16, 2 * segment))
        extra = jnp.where(kind == 0, 1, jnp.where(kind == 1, column, jnp.where(kind == 2, step, 0)))
        extra = extra.astype(jnp.float32).astype(jnp.bfloat16)
        for r in range(left_ref.shape[0]):
            keys = jnp.concatenate([mine_ref[r], theirs_ref[r]], axis=1)
            scores = lax.dot_general(
                left_ref[r], keys, (((0,), (0,)), ((), ())), preferred_element_type=jnp.float32
            )
            weights = jnp.exp2(scores * scale + bias_ref[...]).astype(jnp.bfloat16)
            extended = jnp.concatenate([keys, extra], axis=0)
            acc_ref[r, :, 0 : channels + 16] += lax.dot_general(
                weights, extended, (((1,), (1,)), ((), ())), preferred_element_type=jnp.float32
            )


def group_of(i, inner, groups):
    return i + 1 if inner else i * (groups - 1)


def gather_kernel(place_ref, range_ref, left_ref, *refs, inner, groups):
    keys, (acc_ref, bias_ref) = refs[:-2], refs[-2:]
    group = group_of(pl.program_id(0), inner, groups)
    acc_ref[...] = jnp.zeros_like(acc_ref)
    for step in range(len(keys) // 2):
        add_step(
            place_ref, range_ref, group, step, left_ref, keys[2 * step], keys[2 * step + 1],
            acc_ref, bias_ref,
        )


def finish_kernel(
    place_ref, range_ref, left_ref, mine_ref, theirs_ref, acc_in_ref, *refs, inner, groups, step
):
    matched_ref, disparity_ref, acc_ref, bias_ref, rows_ref = refs[-5:]
    group = group_of(pl.program_id(0), inner, groups)
    rows, channels, segment = left_ref.shape
    acc_ref[...] = acc_in_ref[...]
    add_step(
        place_ref, range_ref, group, step, left_ref, mine_ref, theirs_ref, acc_ref, bias_ref
    )
    block = place_ref[1]
    low = segment * range_ref[0, group]
    high = low + segment * range_ref[1, group]
    x = block * segment + lane_iota((1, segment))
    from_chip = (x - 2 * segment * (block // 2)).astype(jnp.float32)
    start = jnp.maximum(low, x + 1)
    beyond = jnp.maximum(high - start, 0)
    beyond_sum = ((start + high - 1) * beyond).astype(jnp.float32) * 0.5
    beyond = beyond.astype(jnp.float32)
    for r in range(rows):
        turned = acc_ref[r].T
        near = turned[channels : channels + 1]
        column = turned[channels + 1 : channels + 2]
        passed = turned[channels + 2 : channels + 3]
        inverse = 1.0 / (near + beyond)
        shift = from_chip * near - column + (2 * segment) * passed + beyond_sum
        rows_ref[r] = turned[:channels] * inverse
        disparity_ref[r : r + 1, :] = shift * inverse * (1.0 / segment)
    matched_ref[...] = jnp.swapaxes(rows_ref[...].astype(jnp.bfloat16), 0, 1)


def correlate(place, ranges, left, keys, inner):
    rows, channels, segment = left.shape
    groups = rows // RG
    own_groups = keys[0][0].shape[0] // RG
    block = (RG, channels, segment)
    smem = pl.BlockSpec(memory_space=pltpu.SMEM)
    return pl.pallas_call(
        functools.partial(gather_kernel, inner=inner, groups=groups),
        out_shape=jax.ShapeDtypeStruct((own_groups * RG, segment, 128), jnp.float32),
        grid=(own_groups,),
        in_specs=[smem, smem, pl.BlockSpec(block, lambda i: (group_of(i, inner, groups), 0, 0))]
        + [pl.BlockSpec(block, lambda i: (i, 0, 0))] * (2 * len(keys)),
        out_specs=pl.BlockSpec((RG, segment, 128), lambda i: (i, 0, 0)),
        scratch_shapes=[pltpu.VMEM((segment, 2 * segment), jnp.float32)],
        compiler_params=pltpu.CompilerParams(vmem_limit_bytes=VMEM_LIMIT),
        cost_estimate=cost(1.5 * own_groups),
    )(place, ranges, left, *[a for pair in keys for a in pair])


def finish(place, ranges, left, pair, acc, outs, inner, step):
    rows, channels, segment = left.shape
    groups = rows // RG
    own_groups = acc.shape[0] // RG
    block = (RG, channels, segment)
    smem = pl.BlockSpec(memory_space=pltpu.SMEM)

    def group(i):
        return group_of(i, inner, groups)

    given = () if outs is None else tuple(outs)
    return pl.pallas_call(
        functools.partial(finish_kernel, inner=inner, groups=groups, step=step),
        out_shape=(
            jax.ShapeDtypeStruct((channels, rows, segment), jnp.bfloat16),
            jax.ShapeDtypeStruct((rows, segment), jnp.float32),
        ),
        grid=(own_groups,),
        in_specs=[
            smem,
            smem,
            pl.BlockSpec(block, lambda i: (group(i), 0, 0)),
            pl.BlockSpec(block, lambda i: (i, 0, 0)),
            pl.BlockSpec(block, lambda i: (i, 0, 0)),
            pl.BlockSpec((RG, segment, 128), lambda i: (i, 0, 0)),
        ]
        + [pl.BlockSpec(memory_space=pl.ANY)] * len(given),
        out_specs=(
            pl.BlockSpec((channels, RG, segment), lambda i: (0, group(i), 0)),
            pl.BlockSpec((RG, segment), lambda i: (group(i), 0)),
        ),
        scratch_shapes=[
            pltpu.VMEM((RG, segment, 128), jnp.float32),
            pltpu.VMEM((segment, 2 * segment), jnp.float32),
            pltpu.VMEM((RG, channels, segment), jnp.float32),
        ],
        input_output_aliases={6: 0, 7: 1} if given else {},
        compiler_params=pltpu.CompilerParams(vmem_limit_bytes=VMEM_LIMIT),
        cost_estimate=cost(own_groups),
    )(place, ranges, left, *pair, acc, *given)


def both_ways(pairs):
    return pairs + [(b, a) for a, b in pairs]


def program(images, first_weight, second_weight, search_ranges):
    row_count = lax.axis_size("rows")
    col_count = lax.axis_size("cols")
    col = lax.axis_index("cols")
    _, rows, segment = images.shape[1:]
    place = jnp.stack([lax.axis_index("rows"), col]).astype(jnp.int32)
    ranges = search_ranges.reshape(2, rows // RG)

    swap = [(i, i ^ 1) for i in range(col_count)]
    across = both_ways([(i, i + 1) for i in range(1, col_count - 1, 2)])
    hop = [(i, (i + 2) % col_count) for i in range(col_count)]
    down = [(i, (i + 1) % row_count) for i in range(row_count)]
    up = [(b, a) for a, b in down]

    def exchanged(sources, chunks):
        own = pack_edges(sources, chunks)
        cross = lax.ppermute(own, "cols", across)
        partner = lax.ppermute(own, "cols", swap)
        return own, partner, cross

    def features(x, index, parts, count, offset, apart, ends, edges, edge_block):
        return unit_features(
            place, x, index, parts, count, offset, apart, ends, edges, edge_block,
            first_weight, second_weight, (row_count, col_count),
        )

    above = lax.ppermute(images[:, :, rows - RG :], "rows", down)
    below = lax.ppermute(images[:, :, :RG], "rows", up)

    inner = rows - 2 * RG
    right_rows = images[1].transpose(1, 0, 2)[None]
    edges_a = exchanged([(right_rows, 0)], ((0, inner, RG - REACH),))
    x = with_rows(place, images, above, below, row_count)
    chunks = ((0, RG, 0), (0, RG, rows - RG), (1, rows, 0))
    edges_r = exchanged([(x, 1), (x, 0)], chunks)

    right_a = features(right_rows, 0, 1, inner, RG - REACH, 0, False, edges_a, 0)
    right_b = features(x, 1, 2, RG, 0, rows - RG, True, edges_r, 0)
    left = features(x, 0, 1, rows, 0, 0, True, edges_r, 2 * edge_steps(RG, segment)[1])

    steps = min(col_count // 2 - 1, HOPS // 2)

    def pair(mine):
        return mine, lax.ppermute(mine, "cols", swap)

    def chain(mine):
        pairs = [pair(mine)]
        for _ in range(1, steps + 1):
            mine = lax.ppermute(mine, "cols", hop)
            pairs.append(pair(mine))
        return pairs

    keys_a, keys_b = chain(right_a), chain(right_b)
    acc_a = correlate(place, ranges, left, keys_a[:-1], True)
    acc_b = correlate(place, ranges, left, keys_b[:-1], False)
    outs = finish(place, ranges, left, keys_a[-1], acc_a, None, True, steps)
    return finish(place, ranges, left, keys_b[-1], acc_b, outs, False, steps)


def solution(mesh):
    placed = (P(None, None, "rows", "cols"), P(), P(), P(None, "rows", "cols"))
    return jax.shard_map(
        program,
        mesh=mesh,
        in_specs=placed,
        out_specs=(P(None, "rows", "cols"), P("rows", "cols")),
        check_vma=False,
    )
```

```python
import functools

import jax
import jax.numpy as jnp
from jax import lax
from jax.experimental import pallas as pl
from jax.experimental.pallas import tpu as pltpu
from jax.sharding import PartitionSpec as P


RG = 8
FIRST_DILATION = 2
SECOND_DILATION = 4
HOPS = 18
REACH = FIRST_DILATION + SECOND_DILATION
SLOT = 16

sharpness_divisor = 10.0
epsilon = 1e-05
VMEM_LIMIT = 64 << 20
LOG2E = 1.4426950408889634


def lane_iota(shape):
    return lax.broadcasted_iota(jnp.int32, shape, len(shape) - 1)


def cost(microseconds):
    return pl.CostEstimate(
        flops=int(microseconds * 1e9), transcendentals=0, bytes_accessed=int(microseconds * 3e6)
    )


def cost(microseconds):
    return pl.CostEstimate(
        flops=int(microseconds * 1e9), transcendentals=0, bytes_accessed=int(microseconds * 3e6)
    )


def rows_kernel(place_ref, image_ref, above_ref, below_ref, x_ref, *, last_row):
    rows = image_ref.shape[1]
    held = above_ref.shape[1]
    inside_above = (place_ref[0] > 0).astype(jnp.float32)
    inside_below = (place_ref[0] < last_row).astype(jnp.float32)

    def turned(piece, keep):
        piece = jnp.swapaxes(piece, 0, 1)
        return (piece.astype(jnp.float32) * keep).astype(jnp.bfloat16)

    x_ref[0:REACH] = turned(above_ref[...], inside_above)[held - REACH :]
    for start in range(0, rows, 16):
        x_ref[REACH + start : REACH + start + 16] = jnp.swapaxes(image_ref[:, start : start + 16], 0, 1)
    x_ref[REACH + rows :] = turned(below_ref[...], inside_below)[:REACH]


def with_rows(place, images, index, above, below, row_count):
    _, channels, rows, segment = images.shape
    held = above.shape[2]

    def image_of(extent, first):
        return pl.BlockSpec((None, channels, extent, segment), lambda n: (first, 0, 0, 0))

    all_rows = rows + 2 * REACH
    return pl.pallas_call(
        functools.partial(rows_kernel, last_row=row_count - 1),
        out_shape=jax.ShapeDtypeStruct((1, all_rows, channels, segment), jnp.bfloat16),
        grid=(1,),
        in_specs=[
            pl.BlockSpec(memory_space=pltpu.SMEM),
            image_of(rows, index),
            image_of(held, 0),
            image_of(held, 0),
        ],
        out_specs=pl.BlockSpec((None, all_rows, channels, segment), lambda n: (0, 0, 0, 0)),
        compiler_params=pltpu.CompilerParams(vmem_limit_bytes=VMEM_LIMIT),
        cost_estimate=cost(2),
    )(place, images, above, below)


def pack_into(x_ref, edge_ref, base, rows, first):
    channels, segment = x_ref.shape[1:]
    slot_of = lane_iota((channels, segment)) // SLOT
    spacing, steps = edge_steps(rows, segment)
    for q in range(steps):
        packed = None
        for g in range(segment // SLOT):
            shift = (SLOT * g + SLOT // 2) % segment
            moved = pltpu.roll(x_ref[first + g * spacing + q], shift, 1)
            packed = moved if packed is None else jnp.where(slot_of == g, moved, packed)
        edge_ref[base + q] = packed


def edge_steps(rows, segment):
    spacing = (rows + 2 * SECOND_DILATION) // (segment // SLOT)
    return spacing, spacing + 2 * FIRST_DILATION


def pack_kernel(*refs, chunks):
    edge_ref = refs[-1]
    base = 0
    for index, rows, first in chunks:
        pack_into(refs[index], edge_ref, base, rows, first)
        base += edge_steps(rows, edge_ref.shape[2])[1]


def pack_edges(sources, chunks):
    channels, segment = sources[0][0].shape[2:]
    total = sum(edge_steps(rows, segment)[1] for _, rows, _ in chunks)

    def image_of(a, n):
        return pl.BlockSpec((None,) + a.shape[1:], lambda i: (n, 0, 0, 0))

    return pl.pallas_call(
        functools.partial(pack_kernel, chunks=chunks),
        out_shape=jax.ShapeDtypeStruct((total, channels, segment), jnp.bfloat16),
        grid=(1,),
        in_specs=[image_of(a, n) for a, n in sources],
        out_specs=pl.BlockSpec((total, channels, segment), lambda i: (0, 0, 0)),
        compiler_params=pltpu.CompilerParams(vmem_limit_bytes=VMEM_LIMIT),
        cost_estimate=cost(2),
    )(*[a for a, _ in sources])


def feature_kernel(
    place_ref, x_ref, own_ref, partner_ref, cross_ref, w1_ref, w2_ref, unit_ref,
    w_ref, edge_ref, side_ref, p1_ref, p1e_ref, hid_ref, hide_ref, p2_ref, rhs0_ref, rhs1_ref,
    *, spacing, offset, apart, ends, mesh_shape,
):
    part = pl.program_id(0)
    offset = offset + part * apart
    rows = unit_ref.shape[0]
    channels, segment = x_ref.shape[1:]
    first_row, last_row = place_ref[0] == 0, place_ref[0] == mesh_shape[0] - 1
    first_col, last_col = place_ref[1] == 0, place_ref[1] == mesh_shape[1] - 1
    odd = place_ref[1] % 2 == 1
    above = first_row & (part == 0) & ends
    below = last_row & (part == pl.num_programs(0) - 1) & ends
    d1, d2 = FIRST_DILATION, SECOND_DILATION
    all_rows = rows + 2 * REACH
    hidden_rows = rows + 2 * d2
    steps = edge_ref.shape[0]
    groups = segment // SLOT
    lanes = lane_iota((channels, segment))
    in_slot = lanes % SLOT
    half = SLOT // 2
    rhs = (rhs0_ref, rhs1_ref)
    width = rhs0_ref.shape[1] // segment

    def stack(taps_ref):
        for a in range(3):
            for b in range(3):
                w_ref[a * channels : (a + 1) * channels, b * channels : (b + 1) * channels] = taps_ref[3 * a + b]

    for q in range(steps):
        own = own_ref[q]
        partner = partner_ref[q]
        cross = cross_ref[q]
        left = jnp.where(odd, partner, cross)
        right = jnp.where(odd, cross, partner)
        shift = half - REACH
        lower = pltpu.roll(jnp.where(in_slot < half, left, own), segment - shift, 1)
        upper = pltpu.roll(jnp.where(in_slot < half, own, right), shift, 1)
        edge_ref[q] = jnp.where(in_slot < half, lower, upper)
        side_ref[q] = pltpu.roll(jnp.where(in_slot < half, left, right), segment - shift, 1)

    def shifted(main, side, slot, amount):
        to_start = segment - REACH - slot * SLOT
        before = jnp.where(
            lanes < amount,
            pltpu.roll(side, lax.rem(to_start + amount, segment), 1),
            pltpu.roll(main, amount, 1),
        )
        after = jnp.where(
            lanes >= segment - amount,
            pltpu.roll(side, lax.rem(to_start + segment - amount, segment), 1),
            pltpu.roll(main, segment - amount, 1),
        )
        return before, after

    def put(target, j, main, before, after):
        lo = j * segment
        target[0:channels, lo : lo + segment] = before
        target[channels : 2 * channels, lo : lo + segment] = main
        target[2 * channels :, lo : lo + segment] = after

    def multiply(source, product_ref, base):
        product = jnp.dot(w_ref[...], source[...], preferred_element_type=jnp.float32)
        for j in range(width):
            product_ref[base + j] = product[:, j * segment : (j + 1) * segment]

    def conv(source_ref, skip, sides_ref, product_ref, total, amount):
        def build(t, target):
            for j in range(width):
                row = jnp.minimum(t * width + j, total - 1)
                slot = jnp.minimum(row // spacing, groups - 1)
                main = source_ref[row + skip]
                put(target, j, main, *shifted(main, sides_ref[row - slot * spacing], slot, amount))

        build(0, rhs0_ref)

        def body(u, _):
            build(2 * u + 1, rhs1_ref)
            multiply(rhs0_ref, product_ref, 2 * u * width)
            build(2 * u + 2, rhs0_ref)
            multiply(rhs1_ref, product_ref, (2 * u + 1) * width)
            return 0

        lax.fori_loop(0, pl.cdiv(total, 2 * width), body, 0)

    stack(w1_ref)
    conv(x_ref, offset, side_ref, p1_ref, all_rows, d1)

    for t in range(pl.cdiv(steps, width)):
        target = rhs[t % 2]
        for j in range(width):
            main = edge_ref[min(t * width + j, steps - 1)]
            put(target, j, main, pltpu.roll(main, d1, 1), pltpu.roll(main, segment - d1, 1))
        multiply(target, p1e_ref, t * width)

    def three(product_ref, row, apart):
        return (
            product_ref[row, 0:channels]
            + product_ref[row + apart, channels : 2 * channels]
            + product_ref[row + 2 * apart, 2 * channels :]
        )

    def silu(v):
        return v / (1.0 + jnp.exp(-v))

    def hidden(t, _):
        for j in range(8):
            row = 8 * t + j
            outside = ((row < d2) & above) | ((row >= d2 + rows) & below)
            value = silu(three(p1_ref, row, d1))
            hid_ref[row] = jnp.where(outside, 0.0, value).astype(jnp.bfloat16)
        return 0

    lax.fori_loop(0, hidden_rows // 8, hidden, 0)

    left_out = (in_slot < REACH) & first_col
    right_out = (in_slot >= half + 2) & last_col
    for q in range(spacing):
        row = (lanes // SLOT) * spacing + q
        outside = ((row < d2) & above) | ((row >= d2 + rows) & below) | left_out | right_out
        value = silu(three(p1e_ref, q, d1))
        value = jnp.where(outside, 0.0, value).astype(jnp.bfloat16)
        gap = half + 2 - REACH
        hide_ref[q] = jnp.where(in_slot < REACH, value, pltpu.roll(value, segment - gap, 1))

    stack(w2_ref)
    conv(hid_ref, 0, hide_ref, p2_ref, hidden_rows, d2)

    def finish(t, _):
        for j in range(8):
            row = 8 * t + j
            total = x_ref[row + offset + REACH].astype(jnp.float32) + three(p2_ref, row, d2)
            feature = total.astype(jnp.bfloat16).astype(jnp.float32)
            mean = jnp.sum(feature * feature, axis=0, keepdims=True) * (1.0 / channels)
            unit_ref[row] = (feature * lax.rsqrt(mean + epsilon)).astype(jnp.bfloat16)
        return 0

    lax.fori_loop(0, rows // 8, finish, 0)


def unit_features(place, x, index, parts, rows, offset, apart, ends, edges, edge_block, w1, w2, mesh_shape):
    _, held, channels, segment = x.shape
    all_rows = rows + 2 * REACH
    hidden_rows = rows + 2 * SECOND_DILATION
    spacing, steps = edge_steps(rows, segment)
    width = 8

    def whole(a):
        return pl.BlockSpec(a.shape, lambda i: (0,) * a.ndim)

    def up_to(n, m):
        return pl.cdiv(n, m) * m

    products = (3 * channels, segment)
    return pl.pallas_call(
        functools.partial(
            feature_kernel, spacing=spacing, offset=offset, apart=apart, ends=ends, mesh_shape=mesh_shape
        ),
        out_shape=jax.ShapeDtypeStruct((parts * rows, channels, segment), jnp.bfloat16),
        grid=(parts,),
        in_specs=[
            pl.BlockSpec(memory_space=pltpu.SMEM),
            pl.BlockSpec((None, held, channels, segment), lambda i: (index, 0, 0, 0)),
        ]
        + [pl.BlockSpec((pl.Element(steps), pl.Element(channels), pl.Element(segment)), lambda i: (edge_block + i * steps, 0, 0)) for _ in edges]
        + [whole(w1), whole(w2)],
        out_specs=pl.BlockSpec((rows, channels, segment), lambda i: (i, 0, 0)),
        scratch_shapes=[
            pltpu.VMEM((3 * channels, 3 * channels), jnp.bfloat16),
            pltpu.VMEM((steps, channels, segment), jnp.bfloat16),
            pltpu.VMEM((steps, channels, segment), jnp.bfloat16),
            pltpu.VMEM((up_to(all_rows, 2 * width),) + products, jnp.float32),
            pltpu.VMEM((up_to(steps, width),) + products, jnp.float32),
            pltpu.VMEM((hidden_rows, channels, segment), jnp.bfloat16),
            pltpu.VMEM((spacing, channels, segment), jnp.bfloat16),
            pltpu.VMEM((up_to(hidden_rows, 2 * width),) + products, jnp.float32),
            pltpu.VMEM((3 * channels, width * segment), jnp.bfloat16),
            pltpu.VMEM((3 * channels, width * segment), jnp.bfloat16),
        ],
        compiler_params=pltpu.CompilerParams(vmem_limit_bytes=VMEM_LIMIT),
        cost_estimate=cost(parts * rows * 0.2),
    )(place, x, *edges, w1, w2)


def add_step(place_ref, range_ref, group, step, left_ref, mine_ref, theirs_ref, acc_ref, bias_ref):
    _, channels, segment = left_ref.shape
    block = place_ref[1]
    low = segment * range_ref[0, group]
    high = low + segment * range_ref[1, group]
    odd = block % 2
    base = segment * (block - 2 * (block // 2 - step))
    active = (base + segment - 1 >= low) & (base - 2 * segment + 1 < high) & (block // 2 >= step)
    scale = sharpness_divisor / channels * LOG2E

    def key_column(shape):
        column = lane_iota(shape)
        own = column < segment
        return column % segment + segment * jnp.where(own, odd, 1 - odd)

    @pl.when(active)
    def _():
        wide = (segment, 2 * segment)
        offsets = base + lax.broadcasted_iota(jnp.int32, wide, 0) - key_column(wide)
        inside = (offsets >= low) & (offsets < high)
        bias_ref[...] = jnp.where(inside, 0.0, -1e30)
        kind = lax.broadcasted_iota(jnp.int32, (16, 2 * segment), 0)
        column = key_column((16, 2 * segment))
        extra = jnp.where(kind == 0, 1, jnp.where(kind == 1, column, jnp.where(kind == 2, step, 0)))
        extra = extra.astype(jnp.float32).astype(jnp.bfloat16)

        def score(r):
            keys = jnp.concatenate([mine_ref[r], theirs_ref[r]], axis=1)
            return keys, lax.dot_general(
                left_ref[r], keys, (((0,), (0,)), ((), ())), preferred_element_type=jnp.float32
            )

        rows = left_ref.shape[0]
        upcoming = score(0)
        for r in range(rows):
            keys, scores = upcoming
            if r + 1 < rows:
                upcoming = score(r + 1)
            weights = jnp.exp2(scores * scale + bias_ref[...]).astype(jnp.bfloat16)
            extended = jnp.concatenate([keys, extra], axis=0)
            acc_ref[r, :, 0 : channels + 16] += lax.dot_general(
                weights, extended, (((1,), (1,)), ((), ())), preferred_element_type=jnp.float32
            )


def group_of(i, inner, groups):
    return i + 1 if inner else i * (groups - 1)


def gather_kernel(place_ref, range_ref, left_ref, *refs, inner, groups):
    keys, (acc_ref, bias_ref) = refs[:-2], refs[-2:]
    group = group_of(pl.program_id(0), inner, groups)
    acc_ref[...] = jnp.zeros_like(acc_ref)
    for step in range(len(keys) // 2):
        add_step(
            place_ref, range_ref, group, step, left_ref, keys[2 * step], keys[2 * step + 1],
            acc_ref, bias_ref,
        )


def finish_kernel(
    place_ref, range_ref, left_ref, mine_ref, theirs_ref, acc_in_ref, *refs, first, inner, groups, step
):
    matched_ref, disparity_ref, acc_ref, bias_ref, rows_ref = refs[-5:]
    group = group_of(first + pl.program_id(0), inner, groups)
    rows, channels, segment = left_ref.shape
    acc_ref[...] = acc_in_ref[...]
    add_step(
        place_ref, range_ref, group, step, left_ref, mine_ref, theirs_ref, acc_ref, bias_ref
    )
    block = place_ref[1]
    low = segment * range_ref[0, group]
    high = low + segment * range_ref[1, group]
    x = block * segment + lane_iota((1, segment))
    from_chip = (x - 2 * segment * (block // 2)).astype(jnp.float32)
    start = jnp.maximum(low, x + 1)
    beyond = jnp.maximum(high - start, 0)
    beyond_sum = ((start + high - 1) * beyond).astype(jnp.float32) * 0.5
    beyond = beyond.astype(jnp.float32)
    for r in range(rows):
        turned = acc_ref[r].T
        near = turned[channels : channels + 1]
        column = turned[channels + 1 : channels + 2]
        passed = turned[channels + 2 : channels + 3]
        inverse = 1.0 / (near + beyond)
        shift = from_chip * near - column + (2 * segment) * passed + beyond_sum
        rows_ref[r] = turned[:channels] * inverse
        disparity_ref[r : r + 1, :] = shift * inverse * (1.0 / segment)
    matched_ref[...] = jnp.swapaxes(rows_ref[...].astype(jnp.bfloat16), 0, 1)


def correlate(place, ranges, left, keys, inner):
    rows, channels, segment = left.shape
    groups = rows // RG
    own_groups = keys[0][0].shape[0] // RG
    block = (RG, channels, segment)
    smem = pl.BlockSpec(memory_space=pltpu.SMEM)
    return pl.pallas_call(
        functools.partial(gather_kernel, inner=inner, groups=groups),
        out_shape=jax.ShapeDtypeStruct((own_groups * RG, segment, 128), jnp.float32),
        grid=(own_groups,),
        in_specs=[smem, smem, pl.BlockSpec(block, lambda i: (group_of(i, inner, groups), 0, 0))]
        + [pl.BlockSpec(block, lambda i: (i, 0, 0))] * (2 * len(keys)),
        out_specs=pl.BlockSpec((RG, segment, 128), lambda i: (i, 0, 0)),
        scratch_shapes=[pltpu.VMEM((segment, 2 * segment), jnp.float32)],
        compiler_params=pltpu.CompilerParams(vmem_limit_bytes=VMEM_LIMIT),
        cost_estimate=cost(1.5 * own_groups),
    )(place, ranges, left, *[a for pair in keys for a in pair])


def finish(place, ranges, left, pair, acc, piece, outs, inner, step):
    rows, channels, segment = left.shape
    groups = rows // RG
    own_groups = pair[0].shape[0] // RG
    first = piece * own_groups
    block = (RG, channels, segment)
    smem = pl.BlockSpec(memory_space=pltpu.SMEM)

    def group(i):
        return group_of(first + i, inner, groups)

    given = () if outs is None else tuple(outs)
    return pl.pallas_call(
        functools.partial(finish_kernel, first=first, inner=inner, groups=groups, step=step),
        out_shape=(
            jax.ShapeDtypeStruct((channels, rows, segment), jnp.bfloat16),
            jax.ShapeDtypeStruct((rows, segment), jnp.float32),
        ),
        grid=(own_groups,),
        in_specs=[
            smem,
            smem,
            pl.BlockSpec(block, lambda i: (group(i), 0, 0)),
            pl.BlockSpec(block, lambda i: (i, 0, 0)),
            pl.BlockSpec(block, lambda i: (i, 0, 0)),
            pl.BlockSpec((RG, segment, 128), lambda i: (first + i, 0, 0)),
        ]
        + [pl.BlockSpec(memory_space=pl.ANY)] * len(given),
        out_specs=(
            pl.BlockSpec((channels, RG, segment), lambda i: (0, group(i), 0)),
            pl.BlockSpec((RG, segment), lambda i: (group(i), 0)),
        ),
        scratch_shapes=[
            pltpu.VMEM((RG, segment, 128), jnp.float32),
            pltpu.VMEM((segment, 2 * segment), jnp.float32),
            pltpu.VMEM((RG, channels, segment), jnp.float32),
        ],
        input_output_aliases={6: 0, 7: 1} if given else {},
        compiler_params=pltpu.CompilerParams(vmem_limit_bytes=VMEM_LIMIT),
        cost_estimate=cost(own_groups),
    )(place, ranges, left, *pair, acc, *given)


def both_ways(pairs):
    return pairs + [(b, a) for a, b in pairs]


def program(images, first_weight, second_weight, search_ranges):
    row_count = lax.axis_size("rows")
    col_count = lax.axis_size("cols")
    col = lax.axis_index("cols")
    _, rows, _ = images.shape[1:]
    place = jnp.stack([lax.axis_index("rows"), col]).astype(jnp.int32)
    ranges = search_ranges.reshape(2, rows // RG)

    swap = [(i, i ^ 1) for i in range(col_count)]
    across = both_ways([(i, i + 1) for i in range(1, col_count - 1, 2)])
    hop = [(i, (i + 2) % col_count) for i in range(col_count)]
    down = [(i, (i + 1) % row_count) for i in range(row_count)]
    up = [(b, a) for a, b in down]

    def exchanged(sources, chunks):
        own = pack_edges(sources, chunks)
        cross = lax.ppermute(own, "cols", across)
        partner = lax.ppermute(own, "cols", swap)
        return own, partner, cross

    def features(x, index, parts, count, offset, apart, ends, edges, edge_block):
        return unit_features(
            place, x, index, parts, count, offset, apart, ends, edges, edge_block,
            first_weight, second_weight, (row_count, col_count),
        )

    def rows_around(images, index):
        image = images[index : index + 1]
        above = lax.ppermute(image[:, :, rows - RG :], "rows", down)
        below = lax.ppermute(image[:, :, :RG], "rows", up)
        return with_rows(place, images, index, above, below, row_count)

    inner = rows - 2 * RG
    right_rows = images[1].transpose(1, 0, 2)[None]
    edges_a = exchanged([(right_rows, 0)], ((0, inner, RG - REACH),))
    right_x = rows_around(images, 1)
    edges_b = exchanged([(right_x, 0)], ((0, RG, 0), (0, RG, rows - RG)))
    right_a = features(right_rows, 0, 1, inner, RG - REACH, 0, False, edges_a, 0)
    right_b = features(right_x, 0, 2, RG, 0, rows - RG, True, edges_b, 0)

    later, _ = lax.optimization_barrier((images, right_a[:1, :8]))
    left_x = rows_around(later, 0)
    edges_l = exchanged([(left_x, 0)], ((0, rows, 0),))
    left = features(left_x, 0, 1, rows, 0, 0, True, edges_l, 0)

    steps = min(col_count // 2 - 1, HOPS // 2)

    def pair(mine):
        return mine, lax.ppermute(mine, "cols", swap)

    def chain(mine, pieces):
        pairs = [pair(mine)]
        for _ in range(1, steps):
            mine = lax.ppermute(mine, "cols", hop)
            pairs.append(pair(mine))
        last = []
        for piece in range(pieces):
            extent = mine.shape[0] // pieces
            part = lax.slice_in_dim(mine, piece * extent, (piece + 1) * extent)
            part = lax.ppermute(part, "cols", hop)
            last.append(pair(part))
        return pairs, last

    keys_a, last_a = chain(right_a, 2)
    keys_b, last_b = chain(right_b, 1)
    acc_a = correlate(place, ranges, left, keys_a, True)
    acc_b = correlate(place, ranges, left, keys_b, False)
    outs = None
    for piece, keys in enumerate(last_a):
        outs = finish(place, ranges, left, keys, acc_a, piece, outs, True, steps)
    return finish(place, ranges, left, last_b[0], acc_b, 0, outs, False, steps)


def solution(mesh):
    placed = (P(None, None, "rows", "cols"), P(), P(), P(None, "rows", "cols"))
    return jax.shard_map(
        program,
        mesh=mesh,
        in_specs=placed,
        out_specs=(P(None, "rows", "cols"), P("rows", "cols")),
        check_vma=False,
    )
```

```python
import functools

import jax
import jax.numpy as jnp
from jax import lax
from jax.experimental import pallas as pl
from jax.experimental.pallas import tpu as pltpu
from jax.sharding import PartitionSpec as P


RG = 8
FIRST_DILATION = 2
SECOND_DILATION = 4
HOPS = 18
REACH = FIRST_DILATION + SECOND_DILATION
SLOT = 16

sharpness_divisor = 10.0
epsilon = 1e-05
VMEM_LIMIT = 64 << 20
LOG2E = 1.4426950408889634


def lane_iota(shape):
    return lax.broadcasted_iota(jnp.int32, shape, len(shape) - 1)


def cost(microseconds):
    return pl.CostEstimate(
        flops=int(microseconds * 1e9), transcendentals=0, bytes_accessed=int(microseconds * 3e6)
    )


def cost(microseconds):
    return pl.CostEstimate(
        flops=int(microseconds * 1e9), transcendentals=0, bytes_accessed=int(microseconds * 3e6)
    )


def turn_kernel(image_ref, mid_ref, first_ref, last_ref):
    piece = jnp.swapaxes(image_ref[...], 0, 1)
    mid_ref[...] = piece

    @pl.when(pl.program_id(0) == 0)
    def _():
        first_ref[...] = piece[:REACH]

    @pl.when(pl.program_id(0) == pl.num_programs(0) - 1)
    def _():
        last_ref[...] = piece[piece.shape[0] - REACH :]


def turned(images, index):
    _, channels, rows, segment = images.shape
    step = 2 * RG
    edge = jax.ShapeDtypeStruct((REACH, channels, segment), jnp.bfloat16)
    return pl.pallas_call(
        turn_kernel,
        out_shape=(jax.ShapeDtypeStruct((rows, channels, segment), jnp.bfloat16), edge, edge),
        grid=(rows // step,),
        in_specs=[pl.BlockSpec((None, channels, step, segment), lambda i: (index, 0, i, 0))],
        out_specs=(
            pl.BlockSpec((step, channels, segment), lambda i: (i, 0, 0)),
            whole(edge),
            whole(edge),
        ),
        compiler_params=pltpu.CompilerParams(vmem_limit_bytes=VMEM_LIMIT),
        cost_estimate=cost(2),
    )(images)


def edge_steps(rows, segment):
    spacing = (rows + 2 * SECOND_DILATION) // (segment // SLOT)
    return spacing, spacing + 2 * FIRST_DILATION


def kept(piece, inside):
    return jnp.where(inside, piece, jnp.zeros_like(piece))


def pack_kernel(place_ref, *refs, chunks, last_row):
    mid_ref, edge_ref = refs[0], refs[-1]
    rows, channels, segment = mid_ref.shape
    slot_of = lane_iota((channels, segment)) // SLOT

    def row_at(row):
        if row < 0:
            return kept(refs[1][row + REACH], place_ref[0] > 0)
        if row >= rows:
            return kept(refs[2][row - rows], place_ref[0] < last_row)
        return mid_ref[row]

    base = 0
    for count, first in chunks:
        spacing, steps = edge_steps(count, segment)
        for q in range(steps):
            packed = None
            for g in range(segment // SLOT):
                shift = (SLOT * g + SLOT // 2) % segment
                moved = pltpu.roll(row_at(first - REACH + g * spacing + q), shift, 1)
                packed = moved if packed is None else jnp.where(slot_of == g, moved, packed)
            edge_ref[base + q] = packed
        base += steps


def whole(a):
    return pl.BlockSpec(a.shape, lambda i: (0,) * a.ndim)


def pack_edges(place, pieces, chunks, row_count):
    _, channels, segment = pieces[0].shape
    total = sum(edge_steps(count, segment)[1] for count, _ in chunks)
    return pl.pallas_call(
        functools.partial(pack_kernel, chunks=chunks, last_row=row_count - 1),
        out_shape=jax.ShapeDtypeStruct((total, channels, segment), jnp.bfloat16),
        grid=(1,),
        in_specs=[pl.BlockSpec(memory_space=pltpu.SMEM)] + [whole(a) for a in pieces],
        out_specs=pl.BlockSpec((total, channels, segment), lambda i: (0, 0, 0)),
        compiler_params=pltpu.CompilerParams(vmem_limit_bytes=VMEM_LIMIT),
        cost_estimate=cost(2),
    )(place, *pieces)


def feature_kernel(place_ref, *refs, spacing, offset, mesh_shape):
    (
        own_ref, partner_ref, cross_ref, w1_ref, w2_ref, unit_ref,
        w_ref, edge_ref, side_ref, p1_ref, p1e_ref, hid_ref, hide_ref, p2_ref, rhs0_ref, rhs1_ref, x_ref,
    ) = refs[-17:]
    part = pl.program_id(0)
    ends = len(refs) == 20
    mid_ref = refs[0]
    held, channels, segment = mid_ref.shape
    rows = unit_ref.shape[0]
    first_row, last_row = place_ref[0] == 0, place_ref[0] == mesh_shape[0] - 1
    first_col, last_col = place_ref[1] == 0, place_ref[1] == mesh_shape[1] - 1
    odd = place_ref[1] % 2 == 1
    above = first_row & (part == 0) & ends
    below = last_row & (part == pl.num_programs(0) - 1) & ends
    d1, d2 = FIRST_DILATION, SECOND_DILATION
    all_rows = rows + 2 * REACH
    hidden_rows = rows + 2 * d2
    steps = edge_ref.shape[0]
    groups = segment // SLOT
    lanes = lane_iota((channels, segment))
    in_slot = lanes % SLOT
    half = SLOT // 2
    rhs = (rhs0_ref, rhs1_ref)
    width = rhs0_ref.shape[1] // segment

    def stack(taps_ref):
        for a in range(3):
            for b in range(3):
                w_ref[a * channels : (a + 1) * channels, b * channels : (b + 1) * channels] = taps_ref[3 * a + b]

    for q in range(steps):
        own = own_ref[q]
        partner = partner_ref[q]
        cross = cross_ref[q]
        left = jnp.where(odd, partner, cross)
        right = jnp.where(odd, cross, partner)
        shift = half - REACH
        lower = pltpu.roll(jnp.where(in_slot < half, left, own), segment - shift, 1)
        upper = pltpu.roll(jnp.where(in_slot < half, own, right), shift, 1)
        edge_ref[q] = jnp.where(in_slot < half, lower, upper)
        side_ref[q] = pltpu.roll(jnp.where(in_slot < half, left, right), segment - shift, 1)

    def shifted(main, side, slot, amount):
        to_start = segment - REACH - slot * SLOT
        before = jnp.where(
            lanes < amount,
            pltpu.roll(side, lax.rem(to_start + amount, segment), 1),
            pltpu.roll(main, amount, 1),
        )
        after = jnp.where(
            lanes >= segment - amount,
            pltpu.roll(side, lax.rem(to_start + segment - amount, segment), 1),
            pltpu.roll(main, segment - amount, 1),
        )
        return before, after

    def put(target, j, main, before, after):
        lo = j * segment
        target[0:channels, lo : lo + segment] = before
        target[channels : 2 * channels, lo : lo + segment] = main
        target[2 * channels :, lo : lo + segment] = after

    def multiply(source, product_ref, base):
        product = jnp.dot(w_ref[...], source[...], preferred_element_type=jnp.float32)
        for j in range(width):
            product_ref[base + j] = product[:, j * segment : (j + 1) * segment]

    def conv(source_ref, skip, sides_ref, product_ref, total, amount):
        def build(t, target):
            for j in range(width):
                row = jnp.minimum(t * width + j, total - 1)
                slot = jnp.minimum(row // spacing, groups - 1)
                main = source_ref[row + skip]
                put(target, j, main, *shifted(main, sides_ref[row - slot * spacing], slot, amount))

        build(0, rhs0_ref)

        def body(u, _):
            build(2 * u + 1, rhs1_ref)
            multiply(rhs0_ref, product_ref, 2 * u * width)
            build(2 * u + 2, rhs0_ref)
            multiply(rhs1_ref, product_ref, (2 * u + 1) * width)
            return 0

        lax.fori_loop(0, pl.cdiv(total, 2 * width), body, 0)

    if ends:
        top = kept(refs[1][...], ~first_row)
        bottom = kept(refs[2][...], ~last_row)
        if rows == held:
            x_ref[0:REACH] = top
            x_ref[REACH : REACH + rows] = mid_ref[...]
            x_ref[REACH + rows :] = bottom
        else:

            @pl.when(part == 0)
            def _():
                x_ref[0:REACH] = top
                x_ref[REACH:] = mid_ref[: rows + REACH]

            @pl.when(part == 1)
            def _():
                x_ref[: rows + REACH] = mid_ref[held - rows - REACH :]
                x_ref[rows + REACH :] = bottom

    else:
        x_ref = mid_ref

    stack(w1_ref)
    conv(x_ref, offset, side_ref, p1_ref, all_rows, d1)

    for t in range(pl.cdiv(steps, width)):
        target = rhs[t % 2]
        for j in range(width):
            main = edge_ref[min(t * width + j, steps - 1)]
            put(target, j, main, pltpu.roll(main, d1, 1), pltpu.roll(main, segment - d1, 1))
        multiply(target, p1e_ref, t * width)

    def three(product_ref, row, apart):
        return (
            product_ref[row, 0:channels]
            + product_ref[row + apart, channels : 2 * channels]
            + product_ref[row + 2 * apart, 2 * channels :]
        )

    def silu(v):
        return v / (1.0 + jnp.exp(-v))

    def hidden(t, _):
        for j in range(8):
            row = 8 * t + j
            outside = ((row < d2) & above) | ((row >= d2 + rows) & below)
            value = silu(three(p1_ref, row, d1))
            hid_ref[row] = jnp.where(outside, 0.0, value).astype(jnp.bfloat16)
        return 0

    lax.fori_loop(0, hidden_rows // 8, hidden, 0)

    left_out = (in_slot < REACH) & first_col
    right_out = (in_slot >= half + 2) & last_col
    for q in range(spacing):
        row = (lanes // SLOT) * spacing + q
        outside = ((row < d2) & above) | ((row >= d2 + rows) & below) | left_out | right_out
        value = silu(three(p1e_ref, q, d1))
        value = jnp.where(outside, 0.0, value).astype(jnp.bfloat16)
        gap = half + 2 - REACH
        hide_ref[q] = jnp.where(in_slot < REACH, value, pltpu.roll(value, segment - gap, 1))

    stack(w2_ref)
    conv(hid_ref, 0, hide_ref, p2_ref, hidden_rows, d2)

    def finish(t, _):
        for j in range(8):
            row = 8 * t + j
            total = x_ref[row + offset + REACH].astype(jnp.float32) + three(p2_ref, row, d2)
            feature = total.astype(jnp.bfloat16).astype(jnp.float32)
            mean = jnp.sum(feature * feature, axis=0, keepdims=True) * (1.0 / channels)
            unit_ref[row] = (feature * lax.rsqrt(mean + epsilon)).astype(jnp.bfloat16)
        return 0

    lax.fori_loop(0, rows // 8, finish, 0)


def unit_features(place, pieces, parts, rows, offset, edges, w1, w2, mesh_shape):
    _, channels, segment = pieces[0].shape
    all_rows = rows + 2 * REACH
    hidden_rows = rows + 2 * SECOND_DILATION
    spacing, steps = edge_steps(rows, segment)
    width = 8

    def up_to(n, m):
        return pl.cdiv(n, m) * m

    products = (3 * channels, segment)
    assembled = all_rows if len(pieces) == 3 else 1
    return pl.pallas_call(
        functools.partial(feature_kernel, spacing=spacing, offset=offset, mesh_shape=mesh_shape),
        out_shape=jax.ShapeDtypeStruct((parts * rows, channels, segment), jnp.bfloat16),
        grid=(parts,),
        in_specs=[pl.BlockSpec(memory_space=pltpu.SMEM)]
        + [whole(a) for a in pieces]
        + [pl.BlockSpec((steps, channels, segment), lambda i: (i, 0, 0)) for _ in edges]
        + [whole(w1), whole(w2)],
        out_specs=pl.BlockSpec((rows, channels, segment), lambda i: (i, 0, 0)),
        scratch_shapes=[
            pltpu.VMEM((3 * channels, 3 * channels), jnp.bfloat16),
            pltpu.VMEM((steps, channels, segment), jnp.bfloat16),
            pltpu.VMEM((steps, channels, segment), jnp.bfloat16),
            pltpu.VMEM((up_to(all_rows, 2 * width),) + products, jnp.float32),
            pltpu.VMEM((up_to(steps, width),) + products, jnp.float32),
            pltpu.VMEM((hidden_rows, channels, segment), jnp.bfloat16),
            pltpu.VMEM((spacing, channels, segment), jnp.bfloat16),
            pltpu.VMEM((up_to(hidden_rows, 2 * width),) + products, jnp.float32),
            pltpu.VMEM((3 * channels, width * segment), jnp.bfloat16),
            pltpu.VMEM((3 * channels, width * segment), jnp.bfloat16),
            pltpu.VMEM((assembled, channels, segment), jnp.bfloat16),
        ],
        compiler_params=pltpu.CompilerParams(vmem_limit_bytes=VMEM_LIMIT),
        cost_estimate=cost(parts * rows * 0.2),
    )(place, *pieces, *edges, w1, w2)


def add_step(place_ref, range_ref, group, step, left_ref, mine_ref, theirs_ref, acc_ref, bias_ref):
    _, channels, segment = left_ref.shape
    block = place_ref[1]
    low = segment * range_ref[0, group]
    high = low + segment * range_ref[1, group]
    odd = block % 2
    base = segment * (block - 2 * (block // 2 - step))
    active = (base + segment - 1 >= low) & (base - 2 * segment + 1 < high) & (block // 2 >= step)
    scale = sharpness_divisor / channels * LOG2E

    def key_column(shape):
        column = lane_iota(shape)
        own = column < segment
        return column % segment + segment * jnp.where(own, odd, 1 - odd)

    @pl.when(active)
    def _():
        wide = (segment, 2 * segment)
        offsets = base + lax.broadcasted_iota(jnp.int32, wide, 0) - key_column(wide)
        inside = (offsets >= low) & (offsets < high)
        bias_ref[...] = jnp.where(inside, 0.0, -1e30)
        kind = lax.broadcasted_iota(jnp.int32, (16, 2 * segment), 0)
        column = key_column((16, 2 * segment))
        extra = jnp.where(kind == 0, 1, jnp.where(kind == 1, column, jnp.where(kind == 2, step, 0)))
        extra = extra.astype(jnp.float32).astype(jnp.bfloat16)

        def score(r):
            keys = jnp.concatenate([mine_ref[r], theirs_ref[r]], axis=1)
            return keys, lax.dot_general(
                left_ref[r], keys, (((0,), (0,)), ((), ())), preferred_element_type=jnp.float32
            )

        rows = left_ref.shape[0]
        upcoming = score(0)
        for r in range(rows):
            keys, scores = upcoming
            if r + 1 < rows:
                upcoming = score(r + 1)
            weights = jnp.exp2(scores * scale + bias_ref[...]).astype(jnp.bfloat16)
            extended = jnp.concatenate([keys, extra], axis=0)
            acc_ref[r, :, 0 : channels + 16] += lax.dot_general(
                weights, extended, (((1,), (1,)), ((), ())), preferred_element_type=jnp.float32
            )


def group_of(i, inner, groups):
    return i + 1 if inner else i * (groups - 1)


def gather_kernel(place_ref, range_ref, left_ref, *refs, inner, groups, start, count):
    keys, (acc_ref, bias_ref) = refs[: 2 * count], refs[-2:]
    group = group_of(pl.program_id(0), inner, groups)
    acc_ref[...] = refs[2 * count][...] if start else jnp.zeros_like(acc_ref)
    for index in range(count):
        add_step(
            place_ref, range_ref, group, start + index, left_ref, keys[2 * index], keys[2 * index + 1],
            acc_ref, bias_ref,
        )


def finish_kernel(
    place_ref, range_ref, left_ref, mine_ref, theirs_ref, acc_in_ref, *refs, first, inner, groups, step
):
    matched_ref, disparity_ref, acc_ref, bias_ref, rows_ref = refs[-5:]
    group = group_of(first + pl.program_id(0), inner, groups)
    rows, channels, segment = left_ref.shape
    acc_ref[...] = acc_in_ref[...]
    add_step(
        place_ref, range_ref, group, step, left_ref, mine_ref, theirs_ref, acc_ref, bias_ref
    )
    block = place_ref[1]
    low = segment * range_ref[0, group]
    high = low + segment * range_ref[1, group]
    x = block * segment + lane_iota((1, segment))
    from_chip = (x - 2 * segment * (block // 2)).astype(jnp.float32)
    start = jnp.maximum(low, x + 1)
    beyond = jnp.maximum(high - start, 0)
    beyond_sum = ((start + high - 1) * beyond).astype(jnp.float32) * 0.5
    beyond = beyond.astype(jnp.float32)
    for r in range(rows):
        turned = acc_ref[r].T
        near = turned[channels : channels + 1]
        column = turned[channels + 1 : channels + 2]
        passed = turned[channels + 2 : channels + 3]
        inverse = 1.0 / (near + beyond)
        shift = from_chip * near - column + (2 * segment) * passed + beyond_sum
        rows_ref[r] = turned[:channels] * inverse
        disparity_ref[r : r + 1, :] = shift * inverse * (1.0 / segment)
    matched_ref[...] = jnp.swapaxes(rows_ref[...].astype(jnp.bfloat16), 0, 1)


def correlate(place, ranges, left, keys, acc, start, inner):
    rows, channels, segment = left.shape
    groups = rows // RG
    own_groups = keys[0][0].shape[0] // RG
    block = (RG, channels, segment)
    smem = pl.BlockSpec(memory_space=pltpu.SMEM)
    acc_spec = pl.BlockSpec((RG, segment, 128), lambda i: (i, 0, 0))
    given = (acc,) if start else ()
    return pl.pallas_call(
        functools.partial(gather_kernel, inner=inner, groups=groups, start=start, count=len(keys)),
        out_shape=jax.ShapeDtypeStruct((own_groups * RG, segment, 128), jnp.float32),
        grid=(own_groups,),
        in_specs=[smem, smem, pl.BlockSpec(block, lambda i: (group_of(i, inner, groups), 0, 0))]
        + [pl.BlockSpec(block, lambda i: (i, 0, 0))] * (2 * len(keys))
        + [acc_spec] * len(given),
        out_specs=acc_spec,
        scratch_shapes=[pltpu.VMEM((segment, 2 * segment), jnp.float32)],
        input_output_aliases={3 + 2 * len(keys): 0} if given else {},
        compiler_params=pltpu.CompilerParams(vmem_limit_bytes=VMEM_LIMIT),
        cost_estimate=cost(1.5 * own_groups),
    )(place, ranges, left, *[a for pair in keys for a in pair], *given)


def finish(place, ranges, left, pair, acc, piece, outs, inner, step):
    rows, channels, segment = left.shape
    groups = rows // RG
    own_groups = pair[0].shape[0] // RG
    first = piece * own_groups
    block = (RG, channels, segment)
    smem = pl.BlockSpec(memory_space=pltpu.SMEM)

    def group(i):
        return group_of(first + i, inner, groups)

    given = () if outs is None else tuple(outs)
    return pl.pallas_call(
        functools.partial(finish_kernel, first=first, inner=inner, groups=groups, step=step),
        out_shape=(
            jax.ShapeDtypeStruct((channels, rows, segment), jnp.bfloat16),
            jax.ShapeDtypeStruct((rows, segment), jnp.float32),
        ),
        grid=(own_groups,),
        in_specs=[
            smem,
            smem,
            pl.BlockSpec(block, lambda i: (group(i), 0, 0)),
            pl.BlockSpec(block, lambda i: (i, 0, 0)),
            pl.BlockSpec(block, lambda i: (i, 0, 0)),
            pl.BlockSpec((RG, segment, 128), lambda i: (first + i, 0, 0)),
        ]
        + [pl.BlockSpec(memory_space=pl.ANY)] * len(given),
        out_specs=(
            pl.BlockSpec((channels, RG, segment), lambda i: (0, group(i), 0)),
            pl.BlockSpec((RG, segment), lambda i: (group(i), 0)),
        ),
        scratch_shapes=[
            pltpu.VMEM((RG, segment, 128), jnp.float32),
            pltpu.VMEM((segment, 2 * segment), jnp.float32),
            pltpu.VMEM((RG, channels, segment), jnp.float32),
        ],
        input_output_aliases={6: 0, 7: 1} if given else {},
        compiler_params=pltpu.CompilerParams(vmem_limit_bytes=VMEM_LIMIT),
        cost_estimate=cost(own_groups),
    )(place, ranges, left, *pair, acc, *given)


def both_ways(pairs):
    return pairs + [(b, a) for a, b in pairs]


def program(images, first_weight, second_weight, search_ranges):
    row_count = lax.axis_size("rows")
    col_count = lax.axis_size("cols")
    col = lax.axis_index("cols")
    _, rows, _ = images.shape[1:]
    place = jnp.stack([lax.axis_index("rows"), col]).astype(jnp.int32)
    ranges = search_ranges.reshape(2, rows // RG)

    swap = [(i, i ^ 1) for i in range(col_count)]
    across = both_ways([(i, i + 1) for i in range(1, col_count - 1, 2)])
    hop = [(i, (i + 2) % col_count) for i in range(col_count)]
    down = [(i, (i + 1) % row_count) for i in range(row_count)]
    up = [(b, a) for a, b in down]

    def exchanged(pieces, chunks):
        own = pack_edges(place, pieces, chunks, row_count)
        cross = lax.ppermute(own, "cols", across)
        partner = lax.ppermute(own, "cols", swap)
        return own, partner, cross

    def features(pieces, parts, count, offset, edges):
        return unit_features(
            place, pieces, parts, count, offset, edges, first_weight, second_weight,
            (row_count, col_count),
        )

    def rows_of(index):
        mid, first, last = turned(images, index)
        above = lax.ppermute(last, "rows", down)
        below = lax.ppermute(first, "rows", up)
        return mid, above, below

    inner = rows - 2 * RG
    right_rows = rows_of(1)
    edges_a = exchanged(right_rows[:1], ((inner, RG),))
    edges_b = exchanged(right_rows, ((RG, 0), (RG, rows - RG)))
    right_a = features(right_rows[:1], 1, inner, RG - REACH, edges_a)
    right_b = features(right_rows, 2, RG, 0, edges_b)

    left_rows = rows_of(0)
    edges_l = exchanged(left_rows, ((rows, 0),))
    left = features(left_rows, 1, rows, 0, edges_l)

    steps = min(col_count // 2 - 1, HOPS // 2)

    def pair(mine):
        return mine, lax.ppermute(mine, "cols", swap)

    def chain(mine, pieces):
        pairs = [pair(mine)]
        for _ in range(1, steps):
            mine = lax.ppermute(mine, "cols", hop)
            pairs.append(pair(mine))
        last = []
        for piece in range(pieces):
            extent = mine.shape[0] // pieces
            part = lax.slice_in_dim(mine, piece * extent, (piece + 1) * extent)
            part = lax.ppermute(part, "cols", hop)
            last.append(pair(part))
        return pairs, last

    keys_a, last_a = chain(right_a, 2)
    keys_b, last_b = chain(right_b, 1)
    early = max(steps - 1, 1)

    def totals(keys, inside):
        acc = correlate(place, ranges, left, keys[:early], None, 0, inside)
        if early == steps:
            return acc
        return correlate(place, ranges, left, keys[early:], acc, early, inside)

    acc_a, acc_b = totals(keys_a, True), totals(keys_b, False)
    outs = None
    for piece, keys in enumerate(last_a):
        outs = finish(place, ranges, left, keys, acc_a, piece, outs, True, steps)
    return finish(place, ranges, left, last_b[0], acc_b, 0, outs, False, steps)


def solution(mesh):
    placed = (P(None, None, "rows", "cols"), P(), P(), P(None, "rows", "cols"))
    return jax.shard_map(
        program,
        mesh=mesh,
        in_specs=placed,
        out_specs=(P(None, "rows", "cols"), P("rows", "cols")),
        check_vma=False,
    )
```

```python
import functools

import jax
import jax.numpy as jnp
from jax import lax
from jax.experimental import pallas as pl
from jax.experimental.pallas import tpu as pltpu
from jax.sharding import PartitionSpec as P


RG = 8
FIRST_DILATION = 2
SECOND_DILATION = 4
HOPS = 18
REACH = FIRST_DILATION + SECOND_DILATION
SLOT = 16

sharpness_divisor = 10.0
epsilon = 1e-05
VMEM_LIMIT = 64 << 20
LOG2E = 1.4426950408889634


def lane_iota(shape):
    return lax.broadcasted_iota(jnp.int32, shape, len(shape) - 1)


def cost(microseconds):
    return pl.CostEstimate(
        flops=int(microseconds * 1e9), transcendentals=0, bytes_accessed=int(microseconds * 3e6)
    )


def cost(microseconds):
    return pl.CostEstimate(
        flops=int(microseconds * 1e9), transcendentals=0, bytes_accessed=int(microseconds * 3e6)
    )


def edge_steps(rows, segment):
    spacing = (rows + 2 * SECOND_DILATION) // (segment // SLOT)
    return spacing, spacing + 2 * FIRST_DILATION


def kept(piece, inside):
    return jnp.where(inside, piece, jnp.zeros_like(piece))


def pack_kernel(place_ref, *refs, images, last_row):
    edge_ref = refs[-1]
    per_image = (len(refs) - 1) // len(images)
    base = 0
    for n, chunks in enumerate(images):
        mid_ref = refs[n * per_image]
        around = refs[n * per_image + 1 : (n + 1) * per_image]
        rows, channels, segment = mid_ref.shape
        slot_of = lane_iota((channels, segment)) // SLOT

        def row_at(row):
            if row < 0:
                return kept(around[0][row + REACH], place_ref[0] > 0)
            if row >= rows:
                return kept(around[1][row - rows], place_ref[0] < last_row)
            return mid_ref[row]

        for count, first in chunks:
            spacing, steps = edge_steps(count, segment)
            for q in range(steps):
                packed = None
                for g in range(segment // SLOT):
                    shift = (SLOT * g + SLOT // 2) % segment
                    moved = pltpu.roll(row_at(first - REACH + g * spacing + q), shift, 1)
                    packed = moved if packed is None else jnp.where(slot_of == g, moved, packed)
                edge_ref[base + q] = packed
            base += steps


def whole(a):
    return pl.BlockSpec(a.shape, lambda i: (0,) * a.ndim)


def image_of(a, index):
    return pl.BlockSpec((None,) + a.shape[1:], lambda i: (index, 0, 0, 0))


def pack_edges(place, pieces, images, row_count):
    channels, segment = pieces[0].shape[2:]
    total = sum(edge_steps(count, segment)[1] for _, chunks in images for count, _ in chunks)
    return pl.pallas_call(
        functools.partial(
            pack_kernel, images=tuple(chunks for _, chunks in images), last_row=row_count - 1
        ),
        out_shape=jax.ShapeDtypeStruct((total, channels, segment), jnp.bfloat16),
        grid=(1,),
        in_specs=[pl.BlockSpec(memory_space=pltpu.SMEM)]
        + [image_of(a, index) for index, _ in images for a in pieces],
        out_specs=pl.BlockSpec((total, channels, segment), lambda i: (0, 0, 0)),
        compiler_params=pltpu.CompilerParams(vmem_limit_bytes=VMEM_LIMIT),
        cost_estimate=cost(2),
    )(place, *(list(pieces) * len(images)))


def feature_kernel(place_ref, *refs, spacing, offset, mesh_shape):
    (
        own_ref, partner_ref, cross_ref, w1_ref, w2_ref, unit_ref,
        w_ref, edge_ref, side_ref, p1_ref, p1e_ref, hid_ref, hide_ref, p2_ref, rhs0_ref, rhs1_ref, x_ref,
    ) = refs[-17:]
    part = pl.program_id(0)
    ends = len(refs) == 20
    mid_ref = refs[0]
    held, channels, segment = mid_ref.shape
    rows = unit_ref.shape[0]
    first_row, last_row = place_ref[0] == 0, place_ref[0] == mesh_shape[0] - 1
    first_col, last_col = place_ref[1] == 0, place_ref[1] == mesh_shape[1] - 1
    odd = place_ref[1] % 2 == 1
    above = first_row & (part == 0) & ends
    below = last_row & (part == pl.num_programs(0) - 1) & ends
    d1, d2 = FIRST_DILATION, SECOND_DILATION
    all_rows = rows + 2 * REACH
    hidden_rows = rows + 2 * d2
    steps = edge_ref.shape[0]
    groups = segment // SLOT
    lanes = lane_iota((channels, segment))
    in_slot = lanes % SLOT
    half = SLOT // 2
    rhs = (rhs0_ref, rhs1_ref)
    width = rhs0_ref.shape[1] // segment

    def stack(taps_ref):
        for a in range(3):
            for b in range(3):
                w_ref[a * channels : (a + 1) * channels, b * channels : (b + 1) * channels] = taps_ref[3 * a + b]

    for q in range(steps):
        own = own_ref[q]
        partner = partner_ref[q]
        cross = cross_ref[q]
        left = jnp.where(odd, partner, cross)
        right = jnp.where(odd, cross, partner)
        shift = half - REACH
        lower = pltpu.roll(jnp.where(in_slot < half, left, own), segment - shift, 1)
        upper = pltpu.roll(jnp.where(in_slot < half, own, right), shift, 1)
        edge_ref[q] = jnp.where(in_slot < half, lower, upper)
        side_ref[q] = pltpu.roll(jnp.where(in_slot < half, left, right), segment - shift, 1)

    def shifted(main, side, slot, amount):
        to_start = segment - REACH - slot * SLOT
        before = jnp.where(
            lanes < amount,
            pltpu.roll(side, lax.rem(to_start + amount, segment), 1),
            pltpu.roll(main, amount, 1),
        )
        after = jnp.where(
            lanes >= segment - amount,
            pltpu.roll(side, lax.rem(to_start + segment - amount, segment), 1),
            pltpu.roll(main, segment - amount, 1),
        )
        return before, after

    def put(target, j, main, before, after):
        lo = j * segment
        target[0:channels, lo : lo + segment] = before
        target[channels : 2 * channels, lo : lo + segment] = main
        target[2 * channels :, lo : lo + segment] = after

    def multiply(source, product_ref, base):
        product = jnp.dot(w_ref[...], source[...], preferred_element_type=jnp.float32)
        for j in range(width):
            product_ref[base + j] = product[:, j * segment : (j + 1) * segment]

    def conv(source_ref, skip, sides_ref, product_ref, total, amount):
        def build(t, target):
            for j in range(width):
                row = jnp.minimum(t * width + j, total - 1)
                slot = jnp.minimum(row // spacing, groups - 1)
                main = source_ref[row + skip]
                put(target, j, main, *shifted(main, sides_ref[row - slot * spacing], slot, amount))

        build(0, rhs0_ref)

        def body(u, _):
            build(2 * u + 1, rhs1_ref)
            multiply(rhs0_ref, product_ref, 2 * u * width)
            build(2 * u + 2, rhs0_ref)
            multiply(rhs1_ref, product_ref, (2 * u + 1) * width)
            return 0

        lax.fori_loop(0, pl.cdiv(total, 2 * width), body, 0)

    if ends:
        top = kept(refs[1][...], ~first_row)
        bottom = kept(refs[2][...], ~last_row)
        if rows == held:
            x_ref[0:REACH] = top
            x_ref[REACH : REACH + rows] = mid_ref[...]
            x_ref[REACH + rows :] = bottom
        else:

            @pl.when(part == 0)
            def _():
                x_ref[0:REACH] = top
                x_ref[REACH:] = mid_ref[: rows + REACH]

            @pl.when(part == 1)
            def _():
                x_ref[: rows + REACH] = mid_ref[held - rows - REACH :]
                x_ref[rows + REACH :] = bottom

    else:
        x_ref = mid_ref

    stack(w1_ref)
    conv(x_ref, offset, side_ref, p1_ref, all_rows, d1)

    for t in range(pl.cdiv(steps, width)):
        target = rhs[t % 2]
        for j in range(width):
            main = edge_ref[min(t * width + j, steps - 1)]
            put(target, j, main, pltpu.roll(main, d1, 1), pltpu.roll(main, segment - d1, 1))
        multiply(target, p1e_ref, t * width)

    def three(product_ref, row, apart):
        return (
            product_ref[row, 0:channels]
            + product_ref[row + apart, channels : 2 * channels]
            + product_ref[row + 2 * apart, 2 * channels :]
        )

    def silu(v):
        return v / (1.0 + jnp.exp(-v))

    def hidden(t, _):
        for j in range(8):
            row = 8 * t + j
            outside = ((row < d2) & above) | ((row >= d2 + rows) & below)
            value = silu(three(p1_ref, row, d1))
            hid_ref[row] = jnp.where(outside, 0.0, value).astype(jnp.bfloat16)
        return 0

    lax.fori_loop(0, hidden_rows // 8, hidden, 0)

    left_out = (in_slot < REACH) & first_col
    right_out = (in_slot >= half + 2) & last_col
    for q in range(spacing):
        row = (lanes // SLOT) * spacing + q
        outside = ((row < d2) & above) | ((row >= d2 + rows) & below) | left_out | right_out
        value = silu(three(p1e_ref, q, d1))
        value = jnp.where(outside, 0.0, value).astype(jnp.bfloat16)
        gap = half + 2 - REACH
        hide_ref[q] = jnp.where(in_slot < REACH, value, pltpu.roll(value, segment - gap, 1))

    stack(w2_ref)
    conv(hid_ref, 0, hide_ref, p2_ref, hidden_rows, d2)

    def finish(t, _):
        for j in range(8):
            row = 8 * t + j
            total = x_ref[row + offset + REACH].astype(jnp.float32) + three(p2_ref, row, d2)
            feature = total.astype(jnp.bfloat16).astype(jnp.float32)
            mean = jnp.sum(feature * feature, axis=0, keepdims=True) * (1.0 / channels)
            unit_ref[row] = (feature * lax.rsqrt(mean + epsilon)).astype(jnp.bfloat16)
        return 0

    lax.fori_loop(0, rows // 8, finish, 0)


def unit_features(place, pieces, index, parts, rows, offset, edges, base, w1, w2, mesh_shape):
    channels, segment = pieces[0].shape[2:]
    all_rows = rows + 2 * REACH
    hidden_rows = rows + 2 * SECOND_DILATION
    spacing, steps = edge_steps(rows, segment)
    width = 8

    def up_to(n, m):
        return pl.cdiv(n, m) * m

    products = (3 * channels, segment)
    assembled = all_rows if len(pieces) == 3 else 1
    return pl.pallas_call(
        functools.partial(feature_kernel, spacing=spacing, offset=offset, mesh_shape=mesh_shape),
        out_shape=jax.ShapeDtypeStruct((parts * rows, channels, segment), jnp.bfloat16),
        grid=(parts,),
        in_specs=[pl.BlockSpec(memory_space=pltpu.SMEM)]
        + [image_of(a, index) for a in pieces]
        + [
            pl.BlockSpec(
                (pl.Element(steps), pl.Element(channels), pl.Element(segment)),
                lambda i: (base + i * steps, 0, 0),
            )
            for _ in edges
        ]
        + [whole(w1), whole(w2)],
        out_specs=pl.BlockSpec((rows, channels, segment), lambda i: (i, 0, 0)),
        scratch_shapes=[
            pltpu.VMEM((3 * channels, 3 * channels), jnp.bfloat16),
            pltpu.VMEM((steps, channels, segment), jnp.bfloat16),
            pltpu.VMEM((steps, channels, segment), jnp.bfloat16),
            pltpu.VMEM((up_to(all_rows, 2 * width),) + products, jnp.float32),
            pltpu.VMEM((up_to(steps, width),) + products, jnp.float32),
            pltpu.VMEM((hidden_rows, channels, segment), jnp.bfloat16),
            pltpu.VMEM((spacing, channels, segment), jnp.bfloat16),
            pltpu.VMEM((up_to(hidden_rows, 2 * width),) + products, jnp.float32),
            pltpu.VMEM((3 * channels, width * segment), jnp.bfloat16),
            pltpu.VMEM((3 * channels, width * segment), jnp.bfloat16),
            pltpu.VMEM((assembled, channels, segment), jnp.bfloat16),
        ],
        compiler_params=pltpu.CompilerParams(vmem_limit_bytes=VMEM_LIMIT),
        cost_estimate=cost(parts * rows * 0.2),
    )(place, *pieces, *edges, w1, w2)


def add_step(place_ref, range_ref, group, step, left_ref, mine_ref, theirs_ref, acc_ref, bias_ref):
    _, channels, segment = left_ref.shape
    block = place_ref[1]
    low = segment * range_ref[0, group]
    high = low + segment * range_ref[1, group]
    odd = block % 2
    base = segment * (block - 2 * (block // 2 - step))
    active = (base + segment - 1 >= low) & (base - 2 * segment + 1 < high) & (block // 2 >= step)
    scale = sharpness_divisor / channels * LOG2E

    def key_column(shape):
        column = lane_iota(shape)
        own = column < segment
        return column % segment + segment * jnp.where(own, odd, 1 - odd)

    @pl.when(active)
    def _():
        wide = (segment, 2 * segment)
        offsets = base + lax.broadcasted_iota(jnp.int32, wide, 0) - key_column(wide)
        inside = (offsets >= low) & (offsets < high)
        bias_ref[...] = jnp.where(inside, 0.0, -1e30)
        kind = lax.broadcasted_iota(jnp.int32, (16, 2 * segment), 0)
        column = key_column((16, 2 * segment))
        extra = jnp.where(kind == 0, 1, jnp.where(kind == 1, column, jnp.where(kind == 2, step, 0)))
        extra = extra.astype(jnp.float32).astype(jnp.bfloat16)

        def score(r):
            keys = jnp.concatenate([mine_ref[r], theirs_ref[r]], axis=1)
            return keys, lax.dot_general(
                left_ref[r], keys, (((0,), (0,)), ((), ())), preferred_element_type=jnp.float32
            )

        rows = left_ref.shape[0]
        upcoming = score(0)
        for r in range(rows):
            keys, scores = upcoming
            if r + 1 < rows:
                upcoming = score(r + 1)
            weights = jnp.exp2(scores * scale + bias_ref[...]).astype(jnp.bfloat16)
            extended = jnp.concatenate([keys, extra], axis=0)
            acc_ref[r, :, 0 : channels + 16] += lax.dot_general(
                weights, extended, (((1,), (1,)), ((), ())), preferred_element_type=jnp.float32
            )


def group_of(i, inner, groups):
    return i + 1 if inner else i * (groups - 1)


def gather_kernel(place_ref, range_ref, left_ref, *refs, inner, groups, start, count):
    keys, (acc_ref, bias_ref) = refs[: 2 * count], refs[-2:]
    group = group_of(pl.program_id(0), inner, groups)
    acc_ref[...] = refs[2 * count][...] if start else jnp.zeros_like(acc_ref)
    for index in range(count):
        add_step(
            place_ref, range_ref, group, start + index, left_ref, keys[2 * index], keys[2 * index + 1],
            acc_ref, bias_ref,
        )


def finish_kernel(
    place_ref, range_ref, left_ref, mine_ref, theirs_ref, acc_in_ref, *refs, first, inner, groups, step
):
    matched_ref, disparity_ref, acc_ref, bias_ref, rows_ref = refs[-5:]
    group = group_of(first + pl.program_id(0), inner, groups)
    rows, channels, segment = left_ref.shape
    acc_ref[...] = acc_in_ref[...]
    add_step(
        place_ref, range_ref, group, step, left_ref, mine_ref, theirs_ref, acc_ref, bias_ref
    )
    block = place_ref[1]
    low = segment * range_ref[0, group]
    high = low + segment * range_ref[1, group]
    x = block * segment + lane_iota((1, segment))
    from_chip = (x - 2 * segment * (block // 2)).astype(jnp.float32)
    start = jnp.maximum(low, x + 1)
    beyond = jnp.maximum(high - start, 0)
    beyond_sum = ((start + high - 1) * beyond).astype(jnp.float32) * 0.5
    beyond = beyond.astype(jnp.float32)
    for r in range(rows):
        turned = acc_ref[r].T
        near = turned[channels : channels + 1]
        column = turned[channels + 1 : channels + 2]
        passed = turned[channels + 2 : channels + 3]
        inverse = 1.0 / (near + beyond)
        shift = from_chip * near - column + (2 * segment) * passed + beyond_sum
        rows_ref[r] = turned[:channels] * inverse
        disparity_ref[r : r + 1, :] = shift * inverse * (1.0 / segment)
    matched_ref[...] = jnp.swapaxes(rows_ref[...].astype(jnp.bfloat16), 0, 1)


def correlate(place, ranges, left, keys, acc, start, inner):
    rows, channels, segment = left.shape
    groups = rows // RG
    own_groups = keys[0][0].shape[0] // RG
    block = (RG, channels, segment)
    smem = pl.BlockSpec(memory_space=pltpu.SMEM)
    acc_spec = pl.BlockSpec((RG, segment, 128), lambda i: (i, 0, 0))
    given = (acc,) if start else ()
    return pl.pallas_call(
        functools.partial(gather_kernel, inner=inner, groups=groups, start=start, count=len(keys)),
        out_shape=jax.ShapeDtypeStruct((own_groups * RG, segment, 128), jnp.float32),
        grid=(own_groups,),
        in_specs=[smem, smem, pl.BlockSpec(block, lambda i: (group_of(i, inner, groups), 0, 0))]
        + [pl.BlockSpec(block, lambda i: (i, 0, 0))] * (2 * len(keys))
        + [acc_spec] * len(given),
        out_specs=acc_spec,
        scratch_shapes=[pltpu.VMEM((segment, 2 * segment), jnp.float32)],
        input_output_aliases={3 + 2 * len(keys): 0} if given else {},
        compiler_params=pltpu.CompilerParams(vmem_limit_bytes=VMEM_LIMIT),
        cost_estimate=cost(1.5 * own_groups),
    )(place, ranges, left, *[a for pair in keys for a in pair], *given)


def finish(place, ranges, left, pair, acc, piece, outs, inner, step):
    rows, channels, segment = left.shape
    groups = rows // RG
    own_groups = pair[0].shape[0] // RG
    first = piece * own_groups
    block = (RG, channels, segment)
    smem = pl.BlockSpec(memory_space=pltpu.SMEM)

    def group(i):
        return group_of(first + i, inner, groups)

    given = () if outs is None else tuple(outs)
    return pl.pallas_call(
        functools.partial(finish_kernel, first=first, inner=inner, groups=groups, step=step),
        out_shape=(
            jax.ShapeDtypeStruct((channels, rows, segment), jnp.bfloat16),
            jax.ShapeDtypeStruct((rows, segment), jnp.float32),
        ),
        grid=(own_groups,),
        in_specs=[
            smem,
            smem,
            pl.BlockSpec(block, lambda i: (group(i), 0, 0)),
            pl.BlockSpec(block, lambda i: (i, 0, 0)),
            pl.BlockSpec(block, lambda i: (i, 0, 0)),
            pl.BlockSpec((RG, segment, 128), lambda i: (first + i, 0, 0)),
        ]
        + [pl.BlockSpec(memory_space=pl.ANY)] * len(given),
        out_specs=(
            pl.BlockSpec((channels, RG, segment), lambda i: (0, group(i), 0)),
            pl.BlockSpec((RG, segment), lambda i: (group(i), 0)),
        ),
        scratch_shapes=[
            pltpu.VMEM((RG, segment, 128), jnp.float32),
            pltpu.VMEM((segment, 2 * segment), jnp.float32),
            pltpu.VMEM((RG, channels, segment), jnp.float32),
        ],
        input_output_aliases={6: 0, 7: 1} if given else {},
        compiler_params=pltpu.CompilerParams(vmem_limit_bytes=VMEM_LIMIT),
        cost_estimate=cost(own_groups),
    )(place, ranges, left, *pair, acc, *given)


def both_ways(pairs):
    return pairs + [(b, a) for a, b in pairs]


def program(images, first_weight, second_weight, search_ranges):
    row_count = lax.axis_size("rows")
    col_count = lax.axis_size("cols")
    col = lax.axis_index("cols")
    _, rows, segment = images.shape[1:]
    place = jnp.stack([lax.axis_index("rows"), col]).astype(jnp.int32)
    ranges = search_ranges.reshape(2, rows // RG)

    swap = [(i, i ^ 1) for i in range(col_count)]
    across = both_ways([(i, i + 1) for i in range(1, col_count - 1, 2)])
    hop = [(i, (i + 2) % col_count) for i in range(col_count)]
    down = [(i, (i + 1) % row_count) for i in range(row_count)]
    up = [(b, a) for a, b in down]

    def exchanged(pieces, chunks):
        own = pack_edges(place, pieces, chunks, row_count)
        cross = lax.ppermute(own, "cols", across)
        partner = lax.ppermute(own, "cols", swap)
        return own, partner, cross

    def features(pieces, index, parts, count, offset, edges, base):
        return unit_features(
            place, pieces, index, parts, count, offset, edges, base,
            first_weight, second_weight, (row_count, col_count),
        )

    mid = images.transpose(0, 2, 1, 3)
    above = lax.ppermute(mid[:, rows - REACH :], "rows", down)
    below = lax.ppermute(mid[:, :REACH], "rows", up)

    inner = rows - 2 * RG
    around = (mid, above, below)
    edges_a = exchanged((mid,), ((1, ((inner, RG),)),))
    edges_r = exchanged(around, ((1, ((RG, 0), (RG, rows - RG))), (0, ((rows, 0),))))
    right_a = features((mid,), 1, 1, inner, RG - REACH, edges_a, 0)
    right_b = features(around, 1, 2, RG, 0, edges_r, 0)
    left = features(around, 0, 1, rows, 0, edges_r, 2 * edge_steps(RG, segment)[1])

    steps = min(col_count // 2 - 1, HOPS // 2)

    def pair(mine):
        return mine, lax.ppermute(mine, "cols", swap)

    def chain(mine, pieces):
        pairs = [pair(mine)]
        for _ in range(1, steps):
            mine = lax.ppermute(mine, "cols", hop)
            pairs.append(pair(mine))
        last = []
        for piece in range(pieces):
            extent = mine.shape[0] // pieces
            part = lax.slice_in_dim(mine, piece * extent, (piece + 1) * extent)
            part = lax.ppermute(part, "cols", hop)
            last.append(pair(part))
        return pairs, last

    keys_a, last_a = chain(right_a, 2)
    keys_b, last_b = chain(right_b, 1)
    early = max(steps - 1, 1)

    def totals(keys, inside):
        acc = correlate(place, ranges, left, keys[:early], None, 0, inside)
        if early == steps:
            return acc
        return correlate(place, ranges, left, keys[early:], acc, early, inside)

    acc_a, acc_b = totals(keys_a, True), totals(keys_b, False)
    outs = None
    for piece, keys in enumerate(last_a):
        outs = finish(place, ranges, left, keys, acc_a, piece, outs, True, steps)
    return finish(place, ranges, left, last_b[0], acc_b, 0, outs, False, steps)


def solution(mesh):
    placed = (P(None, None, "rows", "cols"), P(), P(), P(None, "rows", "cols"))
    return jax.shard_map(
        program,
        mesh=mesh,
        in_specs=placed,
        out_specs=(P(None, "rows", "cols"), P("rows", "cols")),
        check_vma=False,
    )
```

```python
import functools

import jax
import jax.numpy as jnp
from jax import lax
from jax.experimental import pallas as pl
from jax.experimental.pallas import tpu as pltpu
from jax.sharding import PartitionSpec as P


RG = 8
FIRST_DILATION = 2
SECOND_DILATION = 4
HOPS = 18
REACH = FIRST_DILATION + SECOND_DILATION
SLOT = 16

EXTRA = 16

sharpness_divisor = 10.0
epsilon = 1e-05
VMEM_LIMIT = 64 << 20
LOG2E = 1.4426950408889634


def lane_iota(shape):
    return lax.broadcasted_iota(jnp.int32, shape, len(shape) - 1)


def cost(microseconds):
    return pl.CostEstimate(
        flops=int(microseconds * 1e9), transcendentals=0, bytes_accessed=int(microseconds * 3e6)
    )


def cost(microseconds):
    return pl.CostEstimate(
        flops=int(microseconds * 1e9), transcendentals=0, bytes_accessed=int(microseconds * 3e6)
    )


def edge_steps(rows, segment):
    spacing = (rows + 2 * SECOND_DILATION) // (segment // SLOT)
    return spacing, spacing + 2 * FIRST_DILATION


def kept(piece, inside):
    return jnp.where(inside, piece, jnp.zeros_like(piece))


def pack_kernel(*refs, images, last_row):
    edge_ref = refs[-1]
    alone = len(refs) == 2
    place_ref = None if alone else refs[0]
    refs = refs[:-1] if alone else refs[1:-1]
    per_image = len(refs) // len(images)
    base = 0
    for n, chunks in enumerate(images):
        mid_ref = refs[n * per_image]
        around = refs[n * per_image + 1 : (n + 1) * per_image]
        rows, channels, segment = mid_ref.shape
        slot_of = lane_iota((channels, segment)) // SLOT

        def row_at(row):
            if row < 0:
                return kept(around[0][row + REACH], place_ref[0] > 0)
            if row >= rows:
                return kept(around[1][row - rows], place_ref[0] < last_row)
            return mid_ref[row]

        for count, first in chunks:
            spacing, steps = edge_steps(count, segment)
            for q in range(steps):
                packed = None
                for g in range(segment // SLOT):
                    shift = (SLOT * g + SLOT // 2) % segment
                    moved = pltpu.roll(row_at(first - REACH + g * spacing + q), shift, 1)
                    packed = moved if packed is None else jnp.where(slot_of == g, moved, packed)
                edge_ref[base + q] = packed
            base += steps


def whole(a):
    return pl.BlockSpec(a.shape, lambda i: (0,) * a.ndim)


def image_of(a, index):
    return pl.BlockSpec((None,) + a.shape[1:], lambda i: (index, 0, 0, 0))


def pack_edges(place, pieces, images, row_count):
    channels, segment = pieces[0].shape[2:]
    total = sum(edge_steps(count, segment)[1] for _, chunks in images for count, _ in chunks)
    given = () if len(pieces) == 1 else (place,)
    scalars = [pl.BlockSpec(memory_space=pltpu.SMEM)] * len(given)
    return pl.pallas_call(
        functools.partial(
            pack_kernel, images=tuple(chunks for _, chunks in images), last_row=row_count - 1
        ),
        out_shape=jax.ShapeDtypeStruct((total, channels, segment), jnp.bfloat16),
        grid=(1,),
        in_specs=scalars + [image_of(a, index) for index, _ in images for a in pieces],
        out_specs=pl.BlockSpec((total, channels, segment), lambda i: (0, 0, 0)),
        compiler_params=pltpu.CompilerParams(vmem_limit_bytes=VMEM_LIMIT),
        cost_estimate=cost(2),
    )(*given, *(list(pieces) * len(images)))


def feature_kernel(place_ref, *refs, spacing, offset, mesh_shape):
    (
        own_ref, partner_ref, cross_ref, w1_ref, w2_ref, unit_ref,
        w_ref, edge_ref, side_ref, p1_ref, p1e_ref, hid_ref, hide_ref, p2_ref, rhs0_ref, rhs1_ref, x_ref,
    ) = refs[-17:]
    part = pl.program_id(0)
    ends = len(refs) == 20
    mid_ref = refs[0]
    held, channels, segment = mid_ref.shape
    rows = unit_ref.shape[0]
    first_row, last_row = place_ref[0] == 0, place_ref[0] == mesh_shape[0] - 1
    first_col, last_col = place_ref[1] == 0, place_ref[1] == mesh_shape[1] - 1
    odd = place_ref[1] % 2 == 1
    above = first_row & (part == 0) & ends
    below = last_row & (part == pl.num_programs(0) - 1) & ends
    d1, d2 = FIRST_DILATION, SECOND_DILATION
    all_rows = rows + 2 * REACH
    hidden_rows = rows + 2 * d2
    steps = edge_ref.shape[0]
    groups = segment // SLOT
    lanes = lane_iota((channels, segment))
    in_slot = lanes % SLOT
    half = SLOT // 2
    rhs = (rhs0_ref, rhs1_ref)
    width = rhs0_ref.shape[1] // segment

    def stack(taps_ref):
        for a in range(3):
            for b in range(3):
                w_ref[a * channels : (a + 1) * channels, b * channels : (b + 1) * channels] = taps_ref[3 * a + b]

    for q in range(steps):
        own = own_ref[q]
        partner = partner_ref[q]
        cross = cross_ref[q]
        left = jnp.where(odd, partner, cross)
        right = jnp.where(odd, cross, partner)
        shift = half - REACH
        lower = pltpu.roll(jnp.where(in_slot < half, left, own), segment - shift, 1)
        upper = pltpu.roll(jnp.where(in_slot < half, own, right), shift, 1)
        edge_ref[q] = jnp.where(in_slot < half, lower, upper)
        side_ref[q] = pltpu.roll(jnp.where(in_slot < half, left, right), segment - shift, 1)

    def shifted(main, side, slot, amount):
        to_start = segment - REACH - slot * SLOT
        before = jnp.where(
            lanes < amount,
            pltpu.roll(side, lax.rem(to_start + amount, segment), 1),
            pltpu.roll(main, amount, 1),
        )
        after = jnp.where(
            lanes >= segment - amount,
            pltpu.roll(side, lax.rem(to_start + segment - amount, segment), 1),
            pltpu.roll(main, segment - amount, 1),
        )
        return before, after

    def put(target, j, main, before, after):
        lo = j * segment
        target[0:channels, lo : lo + segment] = before
        target[channels : 2 * channels, lo : lo + segment] = main
        target[2 * channels :, lo : lo + segment] = after

    def conv(source_ref, skip, sides_ref, product_ref, amount):
        def build(q, target):
            q = jnp.minimum(q, spacing - 1)
            side = sides_ref[q]
            for slot in range(groups):
                main = source_ref[slot * spacing + q + skip]
                put(target, slot, main, *shifted(main, side, slot, amount))

        def multiply_rows(q, source):
            product = jnp.dot(w_ref[...], source[...], preferred_element_type=jnp.float32)
            for slot in range(groups):
                product_ref[slot * spacing + q] = product[:, slot * segment : (slot + 1) * segment]

        build(0, rhs0_ref)

        def body(u, _):
            build(2 * u + 1, rhs1_ref)
            multiply_rows(2 * u, rhs0_ref)
            build(2 * u + 2, rhs0_ref)
            multiply_rows(2 * u + 1, rhs1_ref)
            return 0

        lax.fori_loop(0, spacing // 2, body, 0)
        if spacing % 2:
            multiply_rows(spacing - 1, rhs0_ref)

    if ends:
        top = kept(refs[1][...], ~first_row)
        bottom = kept(refs[2][...], ~last_row)
        if rows == held:
            x_ref[0:REACH] = top
            x_ref[REACH : REACH + rows] = mid_ref[...]
            x_ref[REACH + rows :] = bottom
        else:

            @pl.when(part == 0)
            def _():
                x_ref[0:REACH] = top
                x_ref[REACH:] = mid_ref[: rows + REACH]

            @pl.when(part == 1)
            def _():
                x_ref[: rows + REACH] = mid_ref[held - rows - REACH :]
                x_ref[rows + REACH :] = bottom

    else:
        x_ref = mid_ref

    stack(w1_ref)
    conv(x_ref, offset, side_ref, p1_ref, d1)

    pending = [
        (p1_ref, row, x_ref[row + offset], groups - 1, row - (groups - 1) * spacing)
        for row in range(groups * spacing, all_rows)
    ]
    pending += [(p1e_ref, q, edge_ref[q], None, None) for q in range(steps)]
    for t in range(pl.cdiv(len(pending), width)):
        target = rhs[t % 2]
        batch = pending[t * width : (t + 1) * width]
        for j, (_, _, main, slot, q) in enumerate(batch):
            if slot is None:
                moved = pltpu.roll(main, d1, 1), pltpu.roll(main, segment - d1, 1)
            else:
                moved = shifted(main, side_ref[q], slot, d1)
            put(target, j, main, *moved)
        product = jnp.dot(
            w_ref[...], target[:, : len(batch) * segment], preferred_element_type=jnp.float32
        )
        for j, (product_ref, row, _, _, _) in enumerate(batch):
            product_ref[row] = product[:, j * segment : (j + 1) * segment]

    def three(product_ref, row, apart):
        return (
            product_ref[row, 0:channels]
            + product_ref[row + apart, channels : 2 * channels]
            + product_ref[row + 2 * apart, 2 * channels :]
        )

    def silu(v):
        return v / (1.0 + jnp.exp(-v))

    def hidden(t, _):
        for j in range(8):
            row = 8 * t + j
            outside = ((row < d2) & above) | ((row >= d2 + rows) & below)
            value = silu(three(p1_ref, row, d1))
            hid_ref[row] = jnp.where(outside, 0.0, value).astype(jnp.bfloat16)
        return 0

    lax.fori_loop(0, hidden_rows // 8, hidden, 0)

    left_out = (in_slot < REACH) & first_col
    right_out = (in_slot >= half + 2) & last_col
    for q in range(spacing):
        row = (lanes // SLOT) * spacing + q
        outside = ((row < d2) & above) | ((row >= d2 + rows) & below) | left_out | right_out
        value = silu(three(p1e_ref, q, d1))
        value = jnp.where(outside, 0.0, value).astype(jnp.bfloat16)
        gap = half + 2 - REACH
        hide_ref[q] = jnp.where(in_slot < REACH, value, pltpu.roll(value, segment - gap, 1))

    stack(w2_ref)
    conv(hid_ref, 0, hide_ref, p2_ref, d2)

    def finish(t, _):
        for j in range(8):
            row = 8 * t + j
            total = x_ref[row + offset + REACH].astype(jnp.float32) + three(p2_ref, row, d2)
            feature = total.astype(jnp.bfloat16).astype(jnp.float32)
            mean = jnp.sum(feature * feature, axis=0, keepdims=True) * (1.0 / channels)
            unit_ref[row] = (feature * lax.rsqrt(mean + epsilon)).astype(jnp.bfloat16)
        return 0

    lax.fori_loop(0, rows // 8, finish, 0)


def unit_features(place, pieces, index, parts, rows, offset, edges, base, w1, w2, mesh_shape):
    channels, segment = pieces[0].shape[2:]
    all_rows = rows + 2 * REACH
    hidden_rows = rows + 2 * SECOND_DILATION
    spacing, steps = edge_steps(rows, segment)
    width = segment // SLOT
    products = (3 * channels, segment)
    assembled = all_rows if len(pieces) == 3 else 1
    return pl.pallas_call(
        functools.partial(feature_kernel, spacing=spacing, offset=offset, mesh_shape=mesh_shape),
        out_shape=jax.ShapeDtypeStruct((parts * rows, channels, segment), jnp.bfloat16),
        grid=(parts,),
        in_specs=[pl.BlockSpec(memory_space=pltpu.SMEM)]
        + [image_of(a, index) for a in pieces]
        + [
            pl.BlockSpec(
                (pl.Element(steps), pl.Element(channels), pl.Element(segment)),
                lambda i: (base + i * steps, 0, 0),
            )
            for _ in edges
        ]
        + [whole(w1), whole(w2)],
        out_specs=pl.BlockSpec((rows, channels, segment), lambda i: (i, 0, 0)),
        scratch_shapes=[
            pltpu.VMEM((3 * channels, 3 * channels), jnp.bfloat16),
            pltpu.VMEM((steps, channels, segment), jnp.bfloat16),
            pltpu.VMEM((steps, channels, segment), jnp.bfloat16),
            pltpu.VMEM((all_rows,) + products, jnp.float32),
            pltpu.VMEM((steps,) + products, jnp.float32),
            pltpu.VMEM((hidden_rows, channels, segment), jnp.bfloat16),
            pltpu.VMEM((spacing, channels, segment), jnp.bfloat16),
            pltpu.VMEM((hidden_rows,) + products, jnp.float32),
            pltpu.VMEM((3 * channels, width * segment), jnp.bfloat16),
            pltpu.VMEM((3 * channels, width * segment), jnp.bfloat16),
            pltpu.VMEM((assembled, channels, segment), jnp.bfloat16),
        ],
        compiler_params=pltpu.CompilerParams(vmem_limit_bytes=VMEM_LIMIT),
        cost_estimate=cost(parts * rows * 0.2),
    )(place, *pieces, *edges, w1, w2)


def add_step(place_ref, range_ref, group, step, left_ref, mine_ref, theirs_ref, acc_ref, bias_ref, scores_ref):
    _, channels, segment = left_ref.shape
    block = place_ref[1]
    low = segment * range_ref[0, group]
    high = low + segment * range_ref[1, group]
    odd = block % 2
    base = segment * (block - 2 * (block // 2 - step))
    active = (base + segment - 1 >= low) & (base - 2 * segment + 1 < high) & (block // 2 >= step)
    scale = sharpness_divisor / channels * LOG2E

    def key_column(shape):
        column = lane_iota(shape)
        own = column < segment
        return column % segment + segment * jnp.where(own, odd, 1 - odd)

    @pl.when(active)
    def _():
        wide = (segment, 2 * segment)
        offsets = base + lax.broadcasted_iota(jnp.int32, wide, 0) - key_column(wide)
        inside = (offsets >= low) & (offsets < high)
        bias_ref[...] = jnp.where(inside, 0.0, -1e30)
        kind = lax.broadcasted_iota(jnp.int32, (EXTRA, 2 * segment), 0)
        column = key_column((EXTRA, 2 * segment))
        extra = jnp.where(kind == 0, 1, jnp.where(kind == 1, column, jnp.where(kind == 2, step, 0)))
        extra = extra.astype(jnp.float32).astype(jnp.bfloat16)
        rows = left_ref.shape[0]

        def score(r):
            keys = jnp.concatenate([mine_ref[r], theirs_ref[r]], axis=1)
            scores_ref[r % 2] = lax.dot_general(
                left_ref[r], keys, (((0,), (0,)), ((), ())), preferred_element_type=jnp.float32
            )

        score(0)
        for r in range(rows):
            if r + 1 < rows:
                score(r + 1)
            weights = jnp.exp2(scores_ref[r % 2] * scale + bias_ref[...]).astype(jnp.bfloat16)
            keys = jnp.concatenate([mine_ref[r], theirs_ref[r]], axis=1)
            extended = jnp.concatenate([keys, extra], axis=0)
            acc_ref[r] += lax.dot_general(
                extended, weights, (((1,), (1,)), ((), ())), preferred_element_type=jnp.float32
            )


def group_of(i, inner, groups):
    return i + 1 if inner else i * (groups - 1)


def gather_kernel(place_ref, range_ref, left_ref, *refs, inner, groups, start, count):
    keys, (acc_ref, bias_ref, scores_ref) = refs[: 2 * count], refs[-3:]
    group = group_of(pl.program_id(0), inner, groups)
    acc_ref[...] = refs[2 * count][...] if start else jnp.zeros_like(acc_ref)
    for index in range(count):
        add_step(
            place_ref, range_ref, group, start + index, left_ref, keys[2 * index], keys[2 * index + 1],
            acc_ref, bias_ref, scores_ref,
        )


def finish_kernel(
    place_ref, range_ref, left_ref, mine_ref, theirs_ref, acc_in_ref, *refs, first, inner, groups, step
):
    matched_ref, disparity_ref, acc_ref, bias_ref, scores_ref, rows_ref = refs[-6:]
    group = group_of(first + pl.program_id(0), inner, groups)
    rows, channels, segment = left_ref.shape
    acc_ref[...] = acc_in_ref[...]
    add_step(
        place_ref, range_ref, group, step, left_ref, mine_ref, theirs_ref, acc_ref, bias_ref, scores_ref
    )
    block = place_ref[1]
    low = segment * range_ref[0, group]
    high = low + segment * range_ref[1, group]
    x = block * segment + lane_iota((1, segment))
    from_chip = (x - 2 * segment * (block // 2)).astype(jnp.float32)
    start = jnp.maximum(low, x + 1)
    beyond = jnp.maximum(high - start, 0)
    beyond_sum = ((start + high - 1) * beyond).astype(jnp.float32) * 0.5
    beyond = beyond.astype(jnp.float32)
    for r in range(rows):
        turned = acc_ref[r]
        near = turned[channels : channels + 1]
        column = turned[channels + 1 : channels + 2]
        passed = turned[channels + 2 : channels + 3]
        inverse = 1.0 / (near + beyond)
        shift = from_chip * near - column + (2 * segment) * passed + beyond_sum
        rows_ref[r] = turned[:channels] * inverse
        disparity_ref[r : r + 1, :] = shift * inverse * (1.0 / segment)
    matched_ref[...] = jnp.swapaxes(rows_ref[...].astype(jnp.bfloat16), 0, 1)


def correlate(place, ranges, left, keys, acc, start, inner):
    rows, channels, segment = left.shape
    groups = rows // RG
    own_groups = keys[0][0].shape[0] // RG
    block = (RG, channels, segment)
    smem = pl.BlockSpec(memory_space=pltpu.SMEM)
    held = channels + EXTRA
    acc_spec = pl.BlockSpec((RG, held, segment), lambda i: (i, 0, 0))
    given = (acc,) if start else ()
    return pl.pallas_call(
        functools.partial(gather_kernel, inner=inner, groups=groups, start=start, count=len(keys)),
        out_shape=jax.ShapeDtypeStruct((own_groups * RG, held, segment), jnp.float32),
        grid=(own_groups,),
        in_specs=[smem, smem, pl.BlockSpec(block, lambda i: (group_of(i, inner, groups), 0, 0))]
        + [pl.BlockSpec(block, lambda i: (i, 0, 0))] * (2 * len(keys))
        + [acc_spec] * len(given),
        out_specs=acc_spec,
        scratch_shapes=[
            pltpu.VMEM((segment, 2 * segment), jnp.float32),
            pltpu.VMEM((2, segment, 2 * segment), jnp.float32),
        ],
        input_output_aliases={3 + 2 * len(keys): 0} if given else {},
        compiler_params=pltpu.CompilerParams(vmem_limit_bytes=VMEM_LIMIT),
        cost_estimate=cost(1.5 * own_groups),
    )(place, ranges, left, *[a for pair in keys for a in pair], *given)


def finish(place, ranges, left, pair, acc, piece, outs, inner, step):
    rows, channels, segment = left.shape
    groups = rows // RG
    own_groups = pair[0].shape[0] // RG
    first = piece * own_groups
    block = (RG, channels, segment)
    smem = pl.BlockSpec(memory_space=pltpu.SMEM)

    def group(i):
        return group_of(first + i, inner, groups)

    given = () if outs is None else tuple(outs)
    return pl.pallas_call(
        functools.partial(finish_kernel, first=first, inner=inner, groups=groups, step=step),
        out_shape=(
            jax.ShapeDtypeStruct((channels, rows, segment), jnp.bfloat16),
            jax.ShapeDtypeStruct((rows, segment), jnp.float32),
        ),
        grid=(own_groups,),
        in_specs=[
            smem,
            smem,
            pl.BlockSpec(block, lambda i: (group(i), 0, 0)),
            pl.BlockSpec(block, lambda i: (i, 0, 0)),
            pl.BlockSpec(block, lambda i: (i, 0, 0)),
            pl.BlockSpec((RG, channels + EXTRA, segment), lambda i: (first + i, 0, 0)),
        ]
        + [pl.BlockSpec(memory_space=pl.ANY)] * len(given),
        out_specs=(
            pl.BlockSpec((channels, RG, segment), lambda i: (0, group(i), 0)),
            pl.BlockSpec((RG, segment), lambda i: (group(i), 0)),
        ),
        scratch_shapes=[
            pltpu.VMEM((RG, channels + EXTRA, segment), jnp.float32),
            pltpu.VMEM((segment, 2 * segment), jnp.float32),
            pltpu.VMEM((2, segment, 2 * segment), jnp.float32),
            pltpu.VMEM((RG, channels, segment), jnp.float32),
        ],
        input_output_aliases={6: 0, 7: 1} if given else {},
        compiler_params=pltpu.CompilerParams(vmem_limit_bytes=VMEM_LIMIT),
        cost_estimate=cost(own_groups),
    )(place, ranges, left, *pair, acc, *given)


def both_ways(pairs):
    return pairs + [(b, a) for a, b in pairs]


def program(images, first_weight, second_weight, search_ranges):
    row_count = lax.axis_size("rows")
    col_count = lax.axis_size("cols")
    col = lax.axis_index("cols")
    _, rows, segment = images.shape[1:]
    place = jnp.stack([lax.axis_index("rows"), col]).astype(jnp.int32)
    ranges = search_ranges.reshape(2, rows // RG)

    swap = [(i, i ^ 1) for i in range(col_count)]
    across = both_ways([(i, i + 1) for i in range(1, col_count - 1, 2)])
    hop = [(i, (i + 2) % col_count) for i in range(col_count)]
    down = [(i, (i + 1) % row_count) for i in range(row_count)]
    up = [(b, a) for a, b in down]

    def exchanged(pieces, chunks):
        own = pack_edges(place, pieces, chunks, row_count)
        cross = lax.ppermute(own, "cols", across)
        partner = lax.ppermute(own, "cols", swap)
        return own, partner, cross

    def features(pieces, index, parts, count, offset, edges, base):
        return unit_features(
            place, pieces, index, parts, count, offset, edges, base,
            first_weight, second_weight, (row_count, col_count),
        )

    mid = images.transpose(0, 2, 1, 3)
    above = lax.ppermute(mid[:, rows - REACH :], "rows", down)
    below = lax.ppermute(mid[:, :REACH], "rows", up)

    inner = rows - 2 * RG
    around = (mid, above, below)
    edges_a = exchanged((mid,), ((1, ((inner, RG),)),))
    edges_r = exchanged(around, ((1, ((RG, 0), (RG, rows - RG))), (0, ((rows, 0),))))
    right_a = features((mid,), 1, 1, inner, RG - REACH, edges_a, 0)
    right_b = features(around, 1, 2, RG, 0, edges_r, 0)
    left = features(around, 0, 1, rows, 0, edges_r, 2 * edge_steps(RG, segment)[1])

    steps = min(col_count // 2 - 1, HOPS // 2)

    def pair(mine):
        return mine, lax.ppermute(mine, "cols", swap)

    def chain(mine, pieces):
        pairs = [pair(mine)]
        for _ in range(1, steps):
            mine = lax.ppermute(mine, "cols", hop)
            pairs.append(pair(mine))
        last = []
        for piece in range(pieces):
            extent = mine.shape[0] // pieces
            part = lax.slice_in_dim(mine, piece * extent, (piece + 1) * extent)
            part = lax.ppermute(part, "cols", hop)
            last.append(pair(part))
        return pairs, last

    keys_a, last_a = chain(right_a, 2)
    keys_b, last_b = chain(right_b, 1)
    early = max(steps - 1, 1)

    def totals(keys, inside):
        acc = correlate(place, ranges, left, keys[:early], None, 0, inside)
        if early == steps:
            return acc
        return correlate(place, ranges, left, keys[early:], acc, early, inside)

    acc_a, acc_b = totals(keys_a, True), totals(keys_b, False)
    outs = None
    for piece, keys in enumerate(last_a):
        outs = finish(place, ranges, left, keys, acc_a, piece, outs, True, steps)
    return finish(place, ranges, left, last_b[0], acc_b, 0, outs, False, steps)


def solution(mesh):
    placed = (P(None, None, "rows", "cols"), P(), P(), P(None, "rows", "cols"))
    return jax.shard_map(
        program,
        mesh=mesh,
        in_specs=placed,
        out_specs=(P(None, "rows", "cols"), P("rows", "cols")),
        check_vma=False,
    )
```

```python
import functools

import jax
import jax.numpy as jnp
from jax import lax
from jax.experimental import pallas as pl
from jax.experimental.pallas import tpu as pltpu
from jax.sharding import PartitionSpec as P


RG = 8
FIRST_DILATION = 2
SECOND_DILATION = 4
HOPS = 18
REACH = FIRST_DILATION + SECOND_DILATION
SLOT = 16

EXTRA = 16

sharpness_divisor = 10.0
epsilon = 1e-05
VMEM_LIMIT = 64 << 20
LOG2E = 1.4426950408889634


def lane_iota(shape):
    return lax.broadcasted_iota(jnp.int32, shape, len(shape) - 1)


def cost(microseconds):
    return pl.CostEstimate(
        flops=int(microseconds * 1e9), transcendentals=0, bytes_accessed=int(microseconds * 3e6)
    )


def cost(microseconds):
    return pl.CostEstimate(
        flops=int(microseconds * 1e9), transcendentals=0, bytes_accessed=int(microseconds * 3e6)
    )


def edge_steps(rows, segment):
    spacing = (rows + 2 * SECOND_DILATION) // (segment // SLOT)
    return spacing, spacing + 2 * FIRST_DILATION


def kept(piece, inside):
    return jnp.where(inside, piece, jnp.zeros_like(piece))


def pack_kernel(*refs, images, last_row):
    edge_ref = refs[-1]
    alone = len(refs) == 2
    place_ref = None if alone else refs[0]
    refs = refs[:-1] if alone else refs[1:-1]
    per_image = len(refs) // len(images)
    base = 0
    for n, chunks in enumerate(images):
        mid_ref = refs[n * per_image]
        around = refs[n * per_image + 1 : (n + 1) * per_image]
        rows, channels, segment = mid_ref.shape
        slot_of = lane_iota((channels, segment)) // SLOT

        def row_at(row):
            if row < 0:
                return kept(around[0][row + REACH], place_ref[0] > 0)
            if row >= rows:
                return kept(around[1][row - rows], place_ref[0] < last_row)
            return mid_ref[row]

        for count, first in chunks:
            spacing, steps = edge_steps(count, segment)
            for q in range(steps):
                packed = None
                for g in range(segment // SLOT):
                    shift = (SLOT * g + SLOT // 2) % segment
                    moved = pltpu.roll(row_at(first - REACH + g * spacing + q), shift, 1)
                    packed = moved if packed is None else jnp.where(slot_of == g, moved, packed)
                edge_ref[base + q] = packed
            base += steps


def whole(a):
    return pl.BlockSpec(a.shape, lambda i: (0,) * a.ndim)


def image_of(a, index):
    return pl.BlockSpec((None,) + a.shape[1:], lambda i: (index, 0, 0, 0))


def pack_edges(place, pieces, images, row_count):
    channels, segment = pieces[0].shape[2:]
    total = sum(edge_steps(count, segment)[1] for _, chunks in images for count, _ in chunks)
    given = () if len(pieces) == 1 else (place,)
    scalars = [pl.BlockSpec(memory_space=pltpu.SMEM)] * len(given)
    return pl.pallas_call(
        functools.partial(
            pack_kernel, images=tuple(chunks for _, chunks in images), last_row=row_count - 1
        ),
        out_shape=jax.ShapeDtypeStruct((total, channels, segment), jnp.bfloat16),
        grid=(1,),
        in_specs=scalars + [image_of(a, index) for index, _ in images for a in pieces],
        out_specs=pl.BlockSpec((total, channels, segment), lambda i: (0, 0, 0)),
        compiler_params=pltpu.CompilerParams(vmem_limit_bytes=VMEM_LIMIT),
        cost_estimate=cost(2),
    )(*given, *(list(pieces) * len(images)))


def feature_kernel(place_ref, *refs, spacing, offset, mesh_shape):
    (
        own_ref, partner_ref, cross_ref, w1_ref, w2_ref, unit_ref,
        w_ref, edge_ref, side_ref, p1_ref, p1e_ref, hid_ref, hide_ref, p2_ref, rhs0_ref, rhs1_ref, x_ref,
    ) = refs[-17:]
    part = pl.program_id(0)
    ends = len(refs) == 20
    mid_ref = refs[0]
    held, channels, segment = mid_ref.shape
    rows = unit_ref.shape[0]
    first_row, last_row = place_ref[0] == 0, place_ref[0] == mesh_shape[0] - 1
    first_col, last_col = place_ref[1] == 0, place_ref[1] == mesh_shape[1] - 1
    odd = place_ref[1] % 2 == 1
    above = first_row & (part == 0) & ends
    below = last_row & (part == pl.num_programs(0) - 1) & ends
    d1, d2 = FIRST_DILATION, SECOND_DILATION
    all_rows = rows + 2 * REACH
    hidden_rows = rows + 2 * d2
    steps = edge_ref.shape[0]
    groups = segment // SLOT
    lanes = lane_iota((channels, segment))
    in_slot = lanes % SLOT
    half = SLOT // 2
    rhs = (rhs0_ref, rhs1_ref)
    width = rhs0_ref.shape[1] // segment

    def stack(taps_ref):
        for a in range(3):
            for b in range(3):
                w_ref[a * channels : (a + 1) * channels, b * channels : (b + 1) * channels] = taps_ref[3 * a + b]

    for q in range(steps):
        own = own_ref[q]
        partner = partner_ref[q]
        cross = cross_ref[q]
        left = jnp.where(odd, partner, cross)
        right = jnp.where(odd, cross, partner)
        shift = half - REACH
        lower = pltpu.roll(jnp.where(in_slot < half, left, own), segment - shift, 1)
        upper = pltpu.roll(jnp.where(in_slot < half, own, right), shift, 1)
        edge_ref[q] = jnp.where(in_slot < half, lower, upper)
        side_ref[q] = pltpu.roll(jnp.where(in_slot < half, left, right), segment - shift, 1)

    def shifted(main, side, slot, amount):
        to_start = segment - REACH - slot * SLOT
        before = jnp.where(
            lanes < amount,
            pltpu.roll(side, lax.rem(to_start + amount, segment), 1),
            pltpu.roll(main, amount, 1),
        )
        after = jnp.where(
            lanes >= segment - amount,
            pltpu.roll(side, lax.rem(to_start + segment - amount, segment), 1),
            pltpu.roll(main, segment - amount, 1),
        )
        return before, after

    def put(target, j, main, before, after):
        lo = j * segment
        target[0:channels, lo : lo + segment] = before
        target[channels : 2 * channels, lo : lo + segment] = main
        target[2 * channels :, lo : lo + segment] = after

    def conv(source_ref, skip, sides_ref, product_ref, amount):
        def build(q, target):
            q = jnp.minimum(q, spacing - 1)
            side = sides_ref[q]
            for slot in range(groups):
                main = source_ref[slot * spacing + q + skip]
                put(target, slot, main, *shifted(main, side, slot, amount))

        def multiply_rows(q, source):
            product = jnp.dot(w_ref[...], source[...], preferred_element_type=jnp.float32)
            for slot in range(groups):
                product_ref[slot * spacing + q] = product[:, slot * segment : (slot + 1) * segment]

        build(0, rhs0_ref)

        def body(u, _):
            build(2 * u + 1, rhs1_ref)
            multiply_rows(2 * u, rhs0_ref)
            build(2 * u + 2, rhs0_ref)
            multiply_rows(2 * u + 1, rhs1_ref)
            return 0

        lax.fori_loop(0, spacing // 2, body, 0)
        if spacing % 2:
            multiply_rows(spacing - 1, rhs0_ref)

    if ends:
        top = kept(refs[1][...], ~first_row)
        bottom = kept(refs[2][...], ~last_row)
        if rows == held:
            x_ref[0:REACH] = top
            x_ref[REACH : REACH + rows] = mid_ref[...]
            x_ref[REACH + rows :] = bottom
        else:

            @pl.when(part == 0)
            def _():
                x_ref[0:REACH] = top
                x_ref[REACH:] = mid_ref[: rows + REACH]

            @pl.when(part == 1)
            def _():
                x_ref[: rows + REACH] = mid_ref[held - rows - REACH :]
                x_ref[rows + REACH :] = bottom

    else:
        x_ref = mid_ref

    stack(w1_ref)
    conv(x_ref, offset, side_ref, p1_ref, d1)

    pending = [
        (p1_ref, row, x_ref[row + offset], groups - 1, row - (groups - 1) * spacing)
        for row in range(groups * spacing, all_rows)
    ]
    pending += [(p1e_ref, q, edge_ref[q], None, None) for q in range(steps)]
    for t in range(pl.cdiv(len(pending), width)):
        target = rhs[t % 2]
        batch = pending[t * width : (t + 1) * width]
        for j, (_, _, main, slot, q) in enumerate(batch):
            if slot is None:
                moved = pltpu.roll(main, d1, 1), pltpu.roll(main, segment - d1, 1)
            else:
                moved = shifted(main, side_ref[q], slot, d1)
            put(target, j, main, *moved)
        product = jnp.dot(
            w_ref[...], target[:, : len(batch) * segment], preferred_element_type=jnp.float32
        )
        for j, (product_ref, row, _, _, _) in enumerate(batch):
            product_ref[row] = product[:, j * segment : (j + 1) * segment]

    def three(product_ref, row, apart):
        return (
            product_ref[row, 0:channels]
            + product_ref[row + apart, channels : 2 * channels]
            + product_ref[row + 2 * apart, 2 * channels :]
        )

    def silu(v):
        return v / (1.0 + jnp.exp(-v))

    def hidden(t, _):
        for j in range(8):
            row = 8 * t + j
            outside = ((row < d2) & above) | ((row >= d2 + rows) & below)
            value = silu(three(p1_ref, row, d1))
            hid_ref[row] = jnp.where(outside, 0.0, value).astype(jnp.bfloat16)
        return 0

    lax.fori_loop(0, hidden_rows // 8, hidden, 0)

    left_out = (in_slot < REACH) & first_col
    right_out = (in_slot >= half + 2) & last_col
    for q in range(spacing):
        row = (lanes // SLOT) * spacing + q
        outside = ((row < d2) & above) | ((row >= d2 + rows) & below) | left_out | right_out
        value = silu(three(p1e_ref, q, d1))
        value = jnp.where(outside, 0.0, value).astype(jnp.bfloat16)
        gap = half + 2 - REACH
        hide_ref[q] = jnp.where(in_slot < REACH, value, pltpu.roll(value, segment - gap, 1))

    stack(w2_ref)
    conv(hid_ref, 0, hide_ref, p2_ref, d2)

    def finish(t, _):
        for j in range(8):
            row = 8 * t + j
            total = x_ref[row + offset + REACH].astype(jnp.float32) + three(p2_ref, row, d2)
            feature = total.astype(jnp.bfloat16).astype(jnp.float32)
            mean = jnp.sum(feature * feature, axis=0, keepdims=True) * (1.0 / channels)
            unit_ref[row] = (feature * lax.rsqrt(mean + epsilon)).astype(jnp.bfloat16)
        return 0

    lax.fori_loop(0, rows // 8, finish, 0)


def unit_features(place, pieces, index, parts, rows, offset, edges, base, w1, w2, mesh_shape):
    channels, segment = pieces[0].shape[2:]
    all_rows = rows + 2 * REACH
    hidden_rows = rows + 2 * SECOND_DILATION
    spacing, steps = edge_steps(rows, segment)
    width = segment // SLOT
    products = (3 * channels, segment)
    assembled = all_rows if len(pieces) == 3 else 1
    return pl.pallas_call(
        functools.partial(feature_kernel, spacing=spacing, offset=offset, mesh_shape=mesh_shape),
        out_shape=jax.ShapeDtypeStruct((parts * rows, channels, segment), jnp.bfloat16),
        grid=(parts,),
        in_specs=[pl.BlockSpec(memory_space=pltpu.SMEM)]
        + [image_of(a, index) for a in pieces]
        + [
            pl.BlockSpec(
                (pl.Element(steps), pl.Element(channels), pl.Element(segment)),
                lambda i: (base + i * steps, 0, 0),
            )
            for _ in edges
        ]
        + [whole(w1), whole(w2)],
        out_specs=pl.BlockSpec((rows, channels, segment), lambda i: (i, 0, 0)),
        scratch_shapes=[
            pltpu.VMEM((3 * channels, 3 * channels), jnp.bfloat16),
            pltpu.VMEM((steps, channels, segment), jnp.bfloat16),
            pltpu.VMEM((steps, channels, segment), jnp.bfloat16),
            pltpu.VMEM((all_rows,) + products, jnp.float32),
            pltpu.VMEM((steps,) + products, jnp.float32),
            pltpu.VMEM((hidden_rows, channels, segment), jnp.bfloat16),
            pltpu.VMEM((spacing, channels, segment), jnp.bfloat16),
            pltpu.VMEM((hidden_rows,) + products, jnp.float32),
            pltpu.VMEM((3 * channels, width * segment), jnp.bfloat16),
            pltpu.VMEM((3 * channels, width * segment), jnp.bfloat16),
            pltpu.VMEM((assembled, channels, segment), jnp.bfloat16),
        ],
        compiler_params=pltpu.CompilerParams(vmem_limit_bytes=VMEM_LIMIT),
        cost_estimate=cost(parts * rows * 0.2),
    )(place, *pieces, *edges, w1, w2)


def add_step(place_ref, range_ref, group, step, left_ref, mine_ref, theirs_ref, acc_ref, bias_ref, scores_ref):
    _, channels, segment = left_ref.shape
    block = place_ref[1]
    low = segment * range_ref[0, group]
    high = low + segment * range_ref[1, group]
    odd = block % 2
    base = segment * (block - 2 * (block // 2 - step))
    active = (base + segment - 1 >= low) & (base - 2 * segment + 1 < high) & (block // 2 >= step)
    scale = sharpness_divisor / channels * LOG2E

    def key_column(shape):
        column = lane_iota(shape)
        own = column < segment
        return column % segment + segment * jnp.where(own, odd, 1 - odd)

    @pl.when(active)
    def _():
        wide = (segment, 2 * segment)
        offsets = base + lax.broadcasted_iota(jnp.int32, wide, 0) - key_column(wide)
        inside = (offsets >= low) & (offsets < high)
        bias_ref[...] = jnp.where(inside, 0.0, -1e30)
        kind = lax.broadcasted_iota(jnp.int32, (EXTRA, 2 * segment), 0)
        column = key_column((EXTRA, 2 * segment))
        extra = jnp.where(kind == 0, 1, jnp.where(kind == 1, column, jnp.where(kind == 2, step, 0)))
        extra = extra.astype(jnp.float32).astype(jnp.bfloat16)
        rows = left_ref.shape[0]

        def score(r):
            keys = jnp.concatenate([mine_ref[r], theirs_ref[r]], axis=1)
            scores_ref[r % 2] = lax.dot_general(
                left_ref[r], keys, (((0,), (0,)), ((), ())), preferred_element_type=jnp.float32
            )

        score(0)
        for r in range(rows):
            if r + 1 < rows:
                score(r + 1)
            weights = jnp.exp2(scores_ref[r % 2] * scale + bias_ref[...]).astype(jnp.bfloat16)
            keys = jnp.concatenate([mine_ref[r], theirs_ref[r]], axis=1)
            extended = jnp.concatenate([keys, extra], axis=0)
            acc_ref[r] += lax.dot_general(
                extended, weights, (((1,), (1,)), ((), ())), preferred_element_type=jnp.float32
            )


def group_of(i, inner, groups):
    quarter = groups // 4
    return i + quarter if inner else jnp.where(i < quarter, i, i + 2 * quarter)


def gather_kernel(place_ref, range_ref, left_ref, *refs, inner, groups, start, count):
    keys, (acc_ref, bias_ref, scores_ref) = refs[: 2 * count], refs[-3:]
    group = group_of(pl.program_id(0), inner, groups)
    acc_ref[...] = refs[2 * count][...] if start else jnp.zeros_like(acc_ref)
    for index in range(count):
        add_step(
            place_ref, range_ref, group, start + index, left_ref, keys[2 * index], keys[2 * index + 1],
            acc_ref, bias_ref, scores_ref,
        )


def finish_kernel(
    place_ref, range_ref, left_ref, mine_ref, theirs_ref, acc_in_ref, *refs, inner, groups, step
):
    matched_ref, disparity_ref, acc_ref, bias_ref, scores_ref, rows_ref = refs[-6:]
    group = group_of(pl.program_id(0), inner, groups)
    rows, channels, segment = left_ref.shape
    acc_ref[...] = acc_in_ref[...]
    add_step(
        place_ref, range_ref, group, step, left_ref, mine_ref, theirs_ref, acc_ref, bias_ref, scores_ref
    )
    block = place_ref[1]
    low = segment * range_ref[0, group]
    high = low + segment * range_ref[1, group]
    x = block * segment + lane_iota((1, segment))
    from_chip = (x - 2 * segment * (block // 2)).astype(jnp.float32)
    start = jnp.maximum(low, x + 1)
    beyond = jnp.maximum(high - start, 0)
    beyond_sum = ((start + high - 1) * beyond).astype(jnp.float32) * 0.5
    beyond = beyond.astype(jnp.float32)
    for r in range(rows):
        turned = acc_ref[r]
        near = turned[channels : channels + 1]
        column = turned[channels + 1 : channels + 2]
        passed = turned[channels + 2 : channels + 3]
        inverse = 1.0 / (near + beyond)
        shift = from_chip * near - column + (2 * segment) * passed + beyond_sum
        rows_ref[r] = turned[:channels] * inverse
        disparity_ref[r : r + 1, :] = shift * inverse * (1.0 / segment)
    matched_ref[...] = jnp.swapaxes(rows_ref[...].astype(jnp.bfloat16), 0, 1)


def correlate(place, ranges, left, keys, acc, start, inner):
    rows, channels, segment = left.shape
    groups = rows // RG
    own_groups = keys[0][0].shape[0] // RG
    block = (RG, channels, segment)
    smem = pl.BlockSpec(memory_space=pltpu.SMEM)
    held = channels + EXTRA
    acc_spec = pl.BlockSpec((RG, held, segment), lambda i: (i, 0, 0))
    given = (acc,) if start else ()
    return pl.pallas_call(
        functools.partial(gather_kernel, inner=inner, groups=groups, start=start, count=len(keys)),
        out_shape=jax.ShapeDtypeStruct((own_groups * RG, held, segment), jnp.float32),
        grid=(own_groups,),
        in_specs=[smem, smem, pl.BlockSpec(block, lambda i: (group_of(i, inner, groups), 0, 0))]
        + [pl.BlockSpec(block, lambda i: (i, 0, 0))] * (2 * len(keys))
        + [acc_spec] * len(given),
        out_specs=acc_spec,
        scratch_shapes=[
            pltpu.VMEM((segment, 2 * segment), jnp.float32),
            pltpu.VMEM((2, segment, 2 * segment), jnp.float32),
        ],
        input_output_aliases={3 + 2 * len(keys): 0} if given else {},
        compiler_params=pltpu.CompilerParams(vmem_limit_bytes=VMEM_LIMIT),
        cost_estimate=cost(1.5 * own_groups),
    )(place, ranges, left, *[a for pair in keys for a in pair], *given)


def finish(place, ranges, left, pair, acc, outs, inner, step):
    rows, channels, segment = left.shape
    groups = rows // RG
    own_groups = pair[0].shape[0] // RG
    block = (RG, channels, segment)
    smem = pl.BlockSpec(memory_space=pltpu.SMEM)

    def group(i):
        return group_of(i, inner, groups)

    given = () if outs is None else tuple(outs)
    return pl.pallas_call(
        functools.partial(finish_kernel, inner=inner, groups=groups, step=step),
        out_shape=(
            jax.ShapeDtypeStruct((channels, rows, segment), jnp.bfloat16),
            jax.ShapeDtypeStruct((rows, segment), jnp.float32),
        ),
        grid=(own_groups,),
        in_specs=[
            smem,
            smem,
            pl.BlockSpec(block, lambda i: (group(i), 0, 0)),
            pl.BlockSpec(block, lambda i: (i, 0, 0)),
            pl.BlockSpec(block, lambda i: (i, 0, 0)),
            pl.BlockSpec((RG, channels + EXTRA, segment), lambda i: (i, 0, 0)),
        ]
        + [pl.BlockSpec(memory_space=pl.ANY)] * len(given),
        out_specs=(
            pl.BlockSpec((channels, RG, segment), lambda i: (0, group(i), 0)),
            pl.BlockSpec((RG, segment), lambda i: (group(i), 0)),
        ),
        scratch_shapes=[
            pltpu.VMEM((RG, channels + EXTRA, segment), jnp.float32),
            pltpu.VMEM((segment, 2 * segment), jnp.float32),
            pltpu.VMEM((2, segment, 2 * segment), jnp.float32),
            pltpu.VMEM((RG, channels, segment), jnp.float32),
        ],
        input_output_aliases={6: 0, 7: 1} if given else {},
        compiler_params=pltpu.CompilerParams(vmem_limit_bytes=VMEM_LIMIT),
        cost_estimate=cost(own_groups),
    )(place, ranges, left, *pair, acc, *given)


def both_ways(pairs):
    return pairs + [(b, a) for a, b in pairs]


def program(images, first_weight, second_weight, search_ranges):
    row_count = lax.axis_size("rows")
    col_count = lax.axis_size("cols")
    col = lax.axis_index("cols")
    _, rows, segment = images.shape[1:]
    place = jnp.stack([lax.axis_index("rows"), col]).astype(jnp.int32)
    ranges = search_ranges.reshape(2, rows // RG)

    swap = [(i, i ^ 1) for i in range(col_count)]
    across = both_ways([(i, i + 1) for i in range(1, col_count - 1, 2)])
    hop = [(i, (i + 2) % col_count) for i in range(col_count)]
    down = [(i, (i + 1) % row_count) for i in range(row_count)]
    up = [(b, a) for a, b in down]

    def exchanged(pieces, chunks):
        own = pack_edges(place, pieces, chunks, row_count)
        cross = lax.ppermute(own, "cols", across)
        partner = lax.ppermute(own, "cols", swap)
        return own, partner, cross

    def features(pieces, index, parts, count, offset, edges, base):
        return unit_features(
            place, pieces, index, parts, count, offset, edges, base,
            first_weight, second_weight, (row_count, col_count),
        )

    mid = images.transpose(0, 2, 1, 3)
    above = lax.ppermute(mid[:, rows - REACH :], "rows", down)
    below = lax.ppermute(mid[:, :REACH], "rows", up)

    strip = rows // 4
    inner = rows - 2 * strip
    around = (mid, above, below)
    edges_a = exchanged((mid,), ((1, ((inner, strip),)),))
    edges_r = exchanged(around, ((1, ((strip, 0), (strip, rows - strip))), (0, ((rows, 0),))))
    right_a = features((mid,), 1, 1, inner, strip - REACH, edges_a, 0)
    right_b = features(around, 1, 2, strip, 0, edges_r, 0)
    left = features(around, 0, 1, rows, 0, edges_r, 2 * edge_steps(strip, segment)[1])

    steps = min(col_count // 2 - 1, HOPS // 2)
    early = max(steps - 1, 1)

    def chain(mine):
        pairs = []
        for step in range(steps + 1):
            if step:
                mine = lax.ppermute(mine, "cols", hop)
            pairs.append((mine, lax.ppermute(mine, "cols", swap)))
        return pairs

    def totals(keys, inside):
        acc = correlate(place, ranges, left, keys[:early], None, 0, inside)
        if early == steps:
            return acc
        return correlate(place, ranges, left, keys[early:steps], acc, early, inside)

    keys_a, keys_b = chain(right_a), chain(right_b)
    acc_a, acc_b = totals(keys_a, True), totals(keys_b, False)
    outs = finish(place, ranges, left, keys_a[steps], acc_a, None, True, steps)
    return finish(place, ranges, left, keys_b[steps], acc_b, outs, False, steps)


def solution(mesh):
    placed = (P(None, None, "rows", "cols"), P(), P(), P(None, "rows", "cols"))
    return jax.shard_map(
        program,
        mesh=mesh,
        in_specs=placed,
        out_specs=(P(None, "rows", "cols"), P("rows", "cols")),
        check_vma=False,
    )
```

```python
import functools

import jax
import jax.numpy as jnp
from jax import lax
from jax.experimental import pallas as pl
from jax.experimental.pallas import tpu as pltpu
from jax.sharding import PartitionSpec as P


RG = 8
FIRST_DILATION = 2
SECOND_DILATION = 4
HOPS = 18
REACH = FIRST_DILATION + SECOND_DILATION
SLOT = 16

EXTRA = 16

sharpness_divisor = 10.0
epsilon = 1e-05
VMEM_LIMIT = 64 << 20
LOG2E = 1.4426950408889634


def lane_iota(shape):
    return lax.broadcasted_iota(jnp.int32, shape, len(shape) - 1)


def cost(microseconds):
    return pl.CostEstimate(
        flops=int(microseconds * 1e9), transcendentals=0, bytes_accessed=int(microseconds * 3e6)
    )


def cost(microseconds):
    return pl.CostEstimate(
        flops=int(microseconds * 1e9), transcendentals=0, bytes_accessed=int(microseconds * 3e6)
    )


def edge_steps(rows, segment):
    spacing = (rows + 2 * SECOND_DILATION) // (segment // SLOT)
    return spacing, spacing + 2 * FIRST_DILATION


def kept(piece, inside):
    return jnp.where(inside, piece, jnp.zeros_like(piece))


def either_side(place_ref, near, far):
    odd = place_ref[0] % 2 == 1
    return jnp.where(odd, near, far), jnp.where(odd, far, near)


def pack_kernel(*refs, images, last_row):
    edge_ref = refs[-1]
    alone = len(refs) == 2
    place_ref = None if alone else refs[0]
    refs = refs[:-1] if alone else refs[1:-1]
    per_image = len(refs) // len(images)
    base = 0
    for n, chunks in enumerate(images):
        mid_ref = refs[n * per_image]
        around = refs[n * per_image + 1 : (n + 1) * per_image]
        rows, channels, segment = mid_ref.shape
        slot_of = lane_iota((channels, segment)) // SLOT

        def row_at(row):
            if 0 <= row < rows:
                return mid_ref[row]
            at = row + REACH if row < 0 else row - rows
            above, below = either_side(place_ref, around[0][at], around[1][at])
            return kept(above, place_ref[0] > 0) if row < 0 else kept(below, place_ref[0] < last_row)

        for count, first in chunks:
            spacing, steps = edge_steps(count, segment)
            for q in range(steps):
                packed = None
                for g in range(segment // SLOT):
                    shift = (SLOT * g + SLOT // 2) % segment
                    moved = pltpu.roll(row_at(first - REACH + g * spacing + q), shift, 1)
                    packed = moved if packed is None else jnp.where(slot_of == g, moved, packed)
                edge_ref[base + q] = packed
            base += steps


def whole(a):
    return pl.BlockSpec(a.shape, lambda i: (0,) * a.ndim)


def image_of(a, index):
    return pl.BlockSpec((None,) + a.shape[1:], lambda i: (index, 0, 0, 0))


def pack_edges(place, pieces, images, row_count):
    channels, segment = pieces[0].shape[2:]
    total = sum(edge_steps(count, segment)[1] for _, chunks in images for count, _ in chunks)
    given = () if len(pieces) == 1 else (place,)
    scalars = [pl.BlockSpec(memory_space=pltpu.SMEM)] * len(given)
    return pl.pallas_call(
        functools.partial(
            pack_kernel, images=tuple(chunks for _, chunks in images), last_row=row_count - 1
        ),
        out_shape=jax.ShapeDtypeStruct((total, channels, segment), jnp.bfloat16),
        grid=(1,),
        in_specs=scalars + [image_of(a, index) for index, _ in images for a in pieces],
        out_specs=pl.BlockSpec((total, channels, segment), lambda i: (0, 0, 0)),
        compiler_params=pltpu.CompilerParams(vmem_limit_bytes=VMEM_LIMIT),
        cost_estimate=cost(2),
    )(*given, *(list(pieces) * len(images)))


def feature_kernel(place_ref, *refs, spacing, offset, mesh_shape):
    (
        own_ref, partner_ref, cross_ref, w1_ref, w2_ref, unit_ref,
        w_ref, edge_ref, side_ref, p1_ref, p1e_ref, hid_ref, hide_ref, p2_ref, rhs0_ref, rhs1_ref, x_ref,
    ) = refs[-17:]
    part = pl.program_id(0)
    ends = len(refs) == 20
    mid_ref = refs[0]
    held, channels, segment = mid_ref.shape
    rows = unit_ref.shape[0]
    first_row, last_row = place_ref[0] == 0, place_ref[0] == mesh_shape[0] - 1
    first_col, last_col = place_ref[1] == 0, place_ref[1] == mesh_shape[1] - 1
    odd = place_ref[1] % 2 == 1
    above = first_row & (part == 0) & ends
    below = last_row & (part == pl.num_programs(0) - 1) & ends
    d1, d2 = FIRST_DILATION, SECOND_DILATION
    all_rows = rows + 2 * REACH
    hidden_rows = rows + 2 * d2
    steps = edge_ref.shape[0]
    groups = segment // SLOT
    lanes = lane_iota((channels, segment))
    in_slot = lanes % SLOT
    half = SLOT // 2
    rhs = (rhs0_ref, rhs1_ref)
    width = rhs0_ref.shape[1] // segment

    def stack(taps_ref):
        for a in range(3):
            for b in range(3):
                w_ref[a * channels : (a + 1) * channels, b * channels : (b + 1) * channels] = taps_ref[3 * a + b]

    for q in range(steps):
        own = own_ref[q]
        partner = partner_ref[q]
        cross = kept(cross_ref[q], ~(first_col | last_col))
        left = jnp.where(odd, partner, cross)
        right = jnp.where(odd, cross, partner)
        shift = half - REACH
        lower = pltpu.roll(jnp.where(in_slot < half, left, own), segment - shift, 1)
        upper = pltpu.roll(jnp.where(in_slot < half, own, right), shift, 1)
        edge_ref[q] = jnp.where(in_slot < half, lower, upper)
        side_ref[q] = pltpu.roll(jnp.where(in_slot < half, left, right), segment - shift, 1)

    def shifted(main, side, slot, amount):
        to_start = segment - REACH - slot * SLOT
        before = jnp.where(
            lanes < amount,
            pltpu.roll(side, lax.rem(to_start + amount, segment), 1),
            pltpu.roll(main, amount, 1),
        )
        after = jnp.where(
            lanes >= segment - amount,
            pltpu.roll(side, lax.rem(to_start + segment - amount, segment), 1),
            pltpu.roll(main, segment - amount, 1),
        )
        return before, after

    def put(target, j, main, before, after):
        lo = j * segment
        target[0:channels, lo : lo + segment] = before
        target[channels : 2 * channels, lo : lo + segment] = main
        target[2 * channels :, lo : lo + segment] = after

    def conv(source_ref, skip, sides_ref, product_ref, amount):
        def build(q, target):
            q = jnp.minimum(q, spacing - 1)
            side = sides_ref[q]
            for slot in range(groups):
                main = source_ref[slot * spacing + q + skip]
                put(target, slot, main, *shifted(main, side, slot, amount))

        def multiply_rows(q, source):
            product = jnp.dot(w_ref[...], source[...], preferred_element_type=jnp.float32)
            for slot in range(groups):
                product_ref[slot * spacing + q] = product[:, slot * segment : (slot + 1) * segment]

        build(0, rhs0_ref)

        def body(u, _):
            build(2 * u + 1, rhs1_ref)
            multiply_rows(2 * u, rhs0_ref)
            build(2 * u + 2, rhs0_ref)
            multiply_rows(2 * u + 1, rhs1_ref)
            return 0

        lax.fori_loop(0, spacing // 2, body, 0)
        if spacing % 2:
            multiply_rows(spacing - 1, rhs0_ref)

    if ends:
        top, bottom = either_side(place_ref, refs[1][...], refs[2][...])
        top, bottom = kept(top, ~first_row), kept(bottom, ~last_row)
        if rows == held:
            x_ref[0:REACH] = top
            x_ref[REACH : REACH + rows] = mid_ref[...]
            x_ref[REACH + rows :] = bottom
        else:

            @pl.when(part == 0)
            def _():
                x_ref[0:REACH] = top
                x_ref[REACH:] = mid_ref[: rows + REACH]

            @pl.when(part == 1)
            def _():
                x_ref[: rows + REACH] = mid_ref[held - rows - REACH :]
                x_ref[rows + REACH :] = bottom

    else:
        x_ref = mid_ref

    stack(w1_ref)
    conv(x_ref, offset, side_ref, p1_ref, d1)

    pending = [
        (p1_ref, row, x_ref[row + offset], groups - 1, row - (groups - 1) * spacing)
        for row in range(groups * spacing, all_rows)
    ]
    pending += [(p1e_ref, q, edge_ref[q], None, None) for q in range(steps)]
    for t in range(pl.cdiv(len(pending), width)):
        target = rhs[t % 2]
        batch = pending[t * width : (t + 1) * width]
        for j, (_, _, main, slot, q) in enumerate(batch):
            if slot is None:
                moved = pltpu.roll(main, d1, 1), pltpu.roll(main, segment - d1, 1)
            else:
                moved = shifted(main, side_ref[q], slot, d1)
            put(target, j, main, *moved)
        product = jnp.dot(
            w_ref[...], target[:, : len(batch) * segment], preferred_element_type=jnp.float32
        )
        for j, (product_ref, row, _, _, _) in enumerate(batch):
            product_ref[row] = product[:, j * segment : (j + 1) * segment]

    def three(product_ref, row, apart):
        return (
            product_ref[row, 0:channels]
            + product_ref[row + apart, channels : 2 * channels]
            + product_ref[row + 2 * apart, 2 * channels :]
        )

    def silu(v):
        return v / (1.0 + jnp.exp(-v))

    def hidden(t, _):
        for j in range(8):
            row = 8 * t + j
            outside = ((row < d2) & above) | ((row >= d2 + rows) & below)
            value = silu(three(p1_ref, row, d1))
            hid_ref[row] = jnp.where(outside, 0.0, value).astype(jnp.bfloat16)
        return 0

    lax.fori_loop(0, hidden_rows // 8, hidden, 0)

    left_out = (in_slot < REACH) & first_col
    right_out = (in_slot >= half + 2) & last_col
    for q in range(spacing):
        row = (lanes // SLOT) * spacing + q
        outside = ((row < d2) & above) | ((row >= d2 + rows) & below) | left_out | right_out
        value = silu(three(p1e_ref, q, d1))
        value = jnp.where(outside, 0.0, value).astype(jnp.bfloat16)
        gap = half + 2 - REACH
        hide_ref[q] = jnp.where(in_slot < REACH, value, pltpu.roll(value, segment - gap, 1))

    stack(w2_ref)
    conv(hid_ref, 0, hide_ref, p2_ref, d2)

    def finish(t, _):
        for j in range(8):
            row = 8 * t + j
            total = x_ref[row + offset + REACH].astype(jnp.float32) + three(p2_ref, row, d2)
            feature = total.astype(jnp.bfloat16).astype(jnp.float32)
            mean = jnp.sum(feature * feature, axis=0, keepdims=True) * (1.0 / channels)
            unit_ref[row] = (feature * lax.rsqrt(mean + epsilon)).astype(jnp.bfloat16)
        return 0

    lax.fori_loop(0, rows // 8, finish, 0)


def unit_features(place, pieces, index, parts, rows, offset, edges, base, w1, w2, mesh_shape):
    channels, segment = pieces[0].shape[2:]
    all_rows = rows + 2 * REACH
    hidden_rows = rows + 2 * SECOND_DILATION
    spacing, steps = edge_steps(rows, segment)
    width = segment // SLOT
    products = (3 * channels, segment)
    assembled = all_rows if len(pieces) == 3 else 1
    return pl.pallas_call(
        functools.partial(feature_kernel, spacing=spacing, offset=offset, mesh_shape=mesh_shape),
        out_shape=jax.ShapeDtypeStruct((parts * rows, channels, segment), jnp.bfloat16),
        grid=(parts,),
        in_specs=[pl.BlockSpec(memory_space=pltpu.SMEM)]
        + [image_of(a, index) for a in pieces]
        + [
            pl.BlockSpec(
                (pl.Element(steps), pl.Element(channels), pl.Element(segment)),
                lambda i: (base + i * steps, 0, 0),
            )
            for _ in edges
        ]
        + [whole(w1), whole(w2)],
        out_specs=pl.BlockSpec((rows, channels, segment), lambda i: (i, 0, 0)),
        scratch_shapes=[
            pltpu.VMEM((3 * channels, 3 * channels), jnp.bfloat16),
            pltpu.VMEM((steps, channels, segment), jnp.bfloat16),
            pltpu.VMEM((steps, channels, segment), jnp.bfloat16),
            pltpu.VMEM((all_rows,) + products, jnp.float32),
            pltpu.VMEM((steps,) + products, jnp.float32),
            pltpu.VMEM((hidden_rows, channels, segment), jnp.bfloat16),
            pltpu.VMEM((spacing, channels, segment), jnp.bfloat16),
            pltpu.VMEM((hidden_rows,) + products, jnp.float32),
            pltpu.VMEM((3 * channels, width * segment), jnp.bfloat16),
            pltpu.VMEM((3 * channels, width * segment), jnp.bfloat16),
            pltpu.VMEM((assembled, channels, segment), jnp.bfloat16),
        ],
        compiler_params=pltpu.CompilerParams(vmem_limit_bytes=VMEM_LIMIT),
        cost_estimate=cost(parts * rows * 0.2),
    )(place, *pieces, *edges, w1, w2)


def add_step(place_ref, range_ref, group, step, left_ref, mine_ref, theirs_ref, acc_ref, bias_ref, scores_ref):
    _, channels, segment = left_ref.shape
    block = place_ref[1]
    low = segment * range_ref[0, group]
    high = low + segment * range_ref[1, group]
    odd = block % 2
    base = segment * (block - 2 * (block // 2 - step))
    active = (base + segment - 1 >= low) & (base - 2 * segment + 1 < high) & (block // 2 >= step)
    scale = sharpness_divisor / channels * LOG2E

    def key_column(shape):
        column = lane_iota(shape)
        own = column < segment
        return column % segment + segment * jnp.where(own, odd, 1 - odd)

    @pl.when(active)
    def _():
        wide = (segment, 2 * segment)
        offsets = base + lax.broadcasted_iota(jnp.int32, wide, 0) - key_column(wide)
        inside = (offsets >= low) & (offsets < high)
        bias_ref[...] = jnp.where(inside, 0.0, -1e30)
        kind = lax.broadcasted_iota(jnp.int32, (EXTRA, 2 * segment), 0)
        column = key_column((EXTRA, 2 * segment))
        extra = jnp.where(kind == 0, 1, jnp.where(kind == 1, column, jnp.where(kind == 2, step, 0)))
        extra = extra.astype(jnp.float32).astype(jnp.bfloat16)
        rows = left_ref.shape[0]

        def score(r):
            keys = jnp.concatenate([mine_ref[r], theirs_ref[r]], axis=1)
            scores_ref[r % 2] = lax.dot_general(
                left_ref[r], keys, (((0,), (0,)), ((), ())), preferred_element_type=jnp.float32
            )

        score(0)
        for r in range(rows):
            if r + 1 < rows:
                score(r + 1)
            weights = jnp.exp2(scores_ref[r % 2] * scale + bias_ref[...]).astype(jnp.bfloat16)
            keys = jnp.concatenate([mine_ref[r], theirs_ref[r]], axis=1)
            extended = jnp.concatenate([keys, extra], axis=0)
            acc_ref[r] += lax.dot_general(
                extended, weights, (((1,), (1,)), ((), ())), preferred_element_type=jnp.float32
            )


def group_of(i, inner, groups):
    quarter = groups // 4
    return i + quarter if inner else jnp.where(i < quarter, i, i + 2 * quarter)


def gather_kernel(place_ref, range_ref, left_ref, *refs, inner, groups, start, count):
    keys, (acc_ref, bias_ref, scores_ref) = refs[: 2 * count], refs[-3:]
    group = group_of(pl.program_id(0), inner, groups)
    acc_ref[...] = refs[2 * count][...] if start else jnp.zeros_like(acc_ref)
    for index in range(count):
        add_step(
            place_ref, range_ref, group, start + index, left_ref, keys[2 * index], keys[2 * index + 1],
            acc_ref, bias_ref, scores_ref,
        )


def finish_kernel(
    place_ref, range_ref, left_ref, mine_ref, theirs_ref, acc_in_ref, *refs, inner, groups, step
):
    matched_ref, disparity_ref, acc_ref, bias_ref, scores_ref, rows_ref = refs[-6:]
    group = group_of(pl.program_id(0), inner, groups)
    rows, channels, segment = left_ref.shape
    acc_ref[...] = acc_in_ref[...]
    add_step(
        place_ref, range_ref, group, step, left_ref, mine_ref, theirs_ref, acc_ref, bias_ref, scores_ref
    )
    block = place_ref[1]
    low = segment * range_ref[0, group]
    high = low + segment * range_ref[1, group]
    x = block * segment + lane_iota((1, segment))
    from_chip = (x - 2 * segment * (block // 2)).astype(jnp.float32)
    start = jnp.maximum(low, x + 1)
    beyond = jnp.maximum(high - start, 0)
    beyond_sum = ((start + high - 1) * beyond).astype(jnp.float32) * 0.5
    beyond = beyond.astype(jnp.float32)
    for r in range(rows):
        turned = acc_ref[r]
        near = turned[channels : channels + 1]
        column = turned[channels + 1 : channels + 2]
        passed = turned[channels + 2 : channels + 3]
        inverse = 1.0 / (near + beyond)
        shift = from_chip * near - column + (2 * segment) * passed + beyond_sum
        rows_ref[r] = turned[:channels] * inverse
        disparity_ref[r : r + 1, :] = shift * inverse * (1.0 / segment)
    matched_ref[...] = jnp.swapaxes(rows_ref[...].astype(jnp.bfloat16), 0, 1)


def correlate(place, ranges, left, keys, acc, start, inner):
    rows, channels, segment = left.shape
    groups = rows // RG
    own_groups = keys[0][0].shape[0] // RG
    block = (RG, channels, segment)
    smem = pl.BlockSpec(memory_space=pltpu.SMEM)
    held = channels + EXTRA
    acc_spec = pl.BlockSpec((RG, held, segment), lambda i: (i, 0, 0))
    given = (acc,) if start else ()
    return pl.pallas_call(
        functools.partial(gather_kernel, inner=inner, groups=groups, start=start, count=len(keys)),
        out_shape=jax.ShapeDtypeStruct((own_groups * RG, held, segment), jnp.float32),
        grid=(own_groups,),
        in_specs=[smem, smem, pl.BlockSpec(block, lambda i: (group_of(i, inner, groups), 0, 0))]
        + [pl.BlockSpec(block, lambda i: (i, 0, 0))] * (2 * len(keys))
        + [acc_spec] * len(given),
        out_specs=acc_spec,
        scratch_shapes=[
            pltpu.VMEM((segment, 2 * segment), jnp.float32),
            pltpu.VMEM((2, segment, 2 * segment), jnp.float32),
        ],
        input_output_aliases={3 + 2 * len(keys): 0} if given else {},
        compiler_params=pltpu.CompilerParams(vmem_limit_bytes=VMEM_LIMIT),
        cost_estimate=cost(1.5 * own_groups),
    )(place, ranges, left, *[a for pair in keys for a in pair], *given)


def finish(place, ranges, left, pair, acc, outs, inner, step):
    rows, channels, segment = left.shape
    groups = rows // RG
    own_groups = pair[0].shape[0] // RG
    block = (RG, channels, segment)
    smem = pl.BlockSpec(memory_space=pltpu.SMEM)

    def group(i):
        return group_of(i, inner, groups)

    given = () if outs is None else tuple(outs)
    return pl.pallas_call(
        functools.partial(finish_kernel, inner=inner, groups=groups, step=step),
        out_shape=(
            jax.ShapeDtypeStruct((channels, rows, segment), jnp.bfloat16),
            jax.ShapeDtypeStruct((rows, segment), jnp.float32),
        ),
        grid=(own_groups,),
        in_specs=[
            smem,
            smem,
            pl.BlockSpec(block, lambda i: (group(i), 0, 0)),
            pl.BlockSpec(block, lambda i: (i, 0, 0)),
            pl.BlockSpec(block, lambda i: (i, 0, 0)),
            pl.BlockSpec((RG, channels + EXTRA, segment), lambda i: (i, 0, 0)),
        ]
        + [pl.BlockSpec(memory_space=pl.ANY)] * len(given),
        out_specs=(
            pl.BlockSpec((channels, RG, segment), lambda i: (0, group(i), 0)),
            pl.BlockSpec((RG, segment), lambda i: (group(i), 0)),
        ),
        scratch_shapes=[
            pltpu.VMEM((RG, channels + EXTRA, segment), jnp.float32),
            pltpu.VMEM((segment, 2 * segment), jnp.float32),
            pltpu.VMEM((2, segment, 2 * segment), jnp.float32),
            pltpu.VMEM((RG, channels, segment), jnp.float32),
        ],
        input_output_aliases={6: 0, 7: 1} if given else {},
        compiler_params=pltpu.CompilerParams(vmem_limit_bytes=VMEM_LIMIT),
        cost_estimate=cost(own_groups),
    )(place, ranges, left, *pair, acc, *given)


def both_ways(pairs):
    return pairs + [(b, a) for a, b in pairs]


def program(images, first_weight, second_weight, search_ranges):
    row_count = lax.axis_size("rows")
    col_count = lax.axis_size("cols")
    col = lax.axis_index("cols")
    _, rows, segment = images.shape[1:]
    place = jnp.stack([lax.axis_index("rows"), col]).astype(jnp.int32)
    ranges = search_ranges.reshape(2, rows // RG)

    swap = [(i, i ^ 1) for i in range(col_count)]
    across = both_ways([(i, (i + 1) % col_count) for i in range(1, col_count, 2)])
    hop = [(i, (i + 2) % col_count) for i in range(col_count)]
    near_pairs = both_ways([(i, i + 1) for i in range(0, row_count, 2)])
    far_pairs = both_ways([(i, (i + 1) % row_count) for i in range(1, row_count, 2)])

    def exchanged(pieces, chunks):
        own = pack_edges(place, pieces, chunks, row_count)
        cross = lax.ppermute(own, "cols", across)
        partner = lax.ppermute(own, "cols", swap)
        return own, partner, cross

    def features(pieces, index, parts, count, offset, edges, base):
        return unit_features(
            place, pieces, index, parts, count, offset, edges, base,
            first_weight, second_weight, (row_count, col_count),
        )

    mid = images.transpose(0, 2, 1, 3)
    odd_row = lax.axis_index("rows") % 2 == 1
    first_rows, last_rows = mid[:, :REACH], mid[:, rows - REACH :]
    near = lax.ppermute(jnp.where(odd_row, first_rows, last_rows), "rows", near_pairs)
    far = lax.ppermute(jnp.where(odd_row, last_rows, first_rows), "rows", far_pairs)

    strip = rows // 4
    inner = rows - 2 * strip
    around = (mid, near, far)
    edges_a = exchanged((mid,), ((1, ((inner, strip),)),))
    edges_r = exchanged(around, ((1, ((strip, 0), (strip, rows - strip))), (0, ((rows, 0),))))
    right_a = features((mid,), 1, 1, inner, strip - REACH, edges_a, 0)
    right_b = features(around, 1, 2, strip, 0, edges_r, 0)
    left = features(around, 0, 1, rows, 0, edges_r, 2 * edge_steps(strip, segment)[1])

    steps = min(col_count // 2 - 1, HOPS // 2)
    early = max(steps - 1, 1)

    def chain(mine):
        pairs = []
        for step in range(steps + 1):
            if step:
                mine = lax.ppermute(mine, "cols", hop)
            pairs.append((mine, lax.ppermute(mine, "cols", swap)))
        return pairs

    def totals(keys, inside):
        acc = correlate(place, ranges, left, keys[:early], None, 0, inside)
        if early == steps:
            return acc
        return correlate(place, ranges, left, keys[early:steps], acc, early, inside)

    keys_a, keys_b = chain(right_a), chain(right_b)
    acc_a, acc_b = totals(keys_a, True), totals(keys_b, False)
    outs = finish(place, ranges, left, keys_a[steps], acc_a, None, True, steps)
    return finish(place, ranges, left, keys_b[steps], acc_b, outs, False, steps)


def solution(mesh):
    placed = (P(None, None, "rows", "cols"), P(), P(), P(None, "rows", "cols"))
    return jax.shard_map(
        program,
        mesh=mesh,
        in_specs=placed,
        out_specs=(P(None, "rows", "cols"), P("rows", "cols")),
        check_vma=False,
    )
```

```python
import functools

import jax
import jax.numpy as jnp
from jax import lax
from jax.experimental import pallas as pl
from jax.experimental.pallas import tpu as pltpu
from jax.sharding import PartitionSpec as P


RG = 8
FIRST_DILATION = 2
SECOND_DILATION = 4
HOPS = 18
REACH = FIRST_DILATION + SECOND_DILATION
SLOT = 16

EXTRA = 16

sharpness_divisor = 10.0
epsilon = 1e-05
VMEM_LIMIT = 64 << 20
LOG2E = 1.4426950408889634


def lane_iota(shape):
    return lax.broadcasted_iota(jnp.int32, shape, len(shape) - 1)


def cost(microseconds):
    return pl.CostEstimate(
        flops=int(microseconds * 1e9), transcendentals=0, bytes_accessed=int(microseconds * 3e6)
    )


def cost(microseconds):
    return pl.CostEstimate(
        flops=int(microseconds * 1e9), transcendentals=0, bytes_accessed=int(microseconds * 3e6)
    )


def edge_steps(rows, segment):
    spacing = (rows + 2 * SECOND_DILATION) // (segment // SLOT)
    return spacing, spacing + 2 * FIRST_DILATION


def kept(piece, inside):
    return jnp.where(inside, piece, jnp.zeros_like(piece))


def either_side(place_ref, near, far):
    odd = place_ref[0] % 2 == 1
    return jnp.where(odd, near, far), jnp.where(odd, far, near)


def pack_kernel(*refs, images, last_row):
    edge_ref = refs[-1]
    alone = len(refs) == 2
    place_ref = None if alone else refs[0]
    refs = refs[:-1] if alone else refs[1:-1]
    per_image = len(refs) // len(images)
    base = 0
    for n, chunks in enumerate(images):
        mid_ref = refs[n * per_image]
        around = refs[n * per_image + 1 : (n + 1) * per_image]
        rows, channels, segment = mid_ref.shape
        slot_of = lane_iota((channels, segment)) // SLOT

        def row_at(row):
            if 0 <= row < rows:
                return mid_ref[row]
            at = row + REACH if row < 0 else row - rows
            above, below = either_side(place_ref, around[0][at], around[1][at])
            return kept(above, place_ref[0] > 0) if row < 0 else kept(below, place_ref[0] < last_row)

        for count, first in chunks:
            spacing, steps = edge_steps(count, segment)
            for q in range(steps):
                packed = None
                for g in range(segment // SLOT):
                    shift = (SLOT * g + SLOT // 2) % segment
                    moved = pltpu.roll(row_at(first - REACH + g * spacing + q), shift, 1)
                    packed = moved if packed is None else jnp.where(slot_of == g, moved, packed)
                edge_ref[base + q] = packed
            base += steps


def whole(a):
    return pl.BlockSpec(a.shape, lambda i: (0,) * a.ndim)


def image_of(a, index):
    return pl.BlockSpec((None,) + a.shape[1:], lambda i: (index, 0, 0, 0))


def pack_edges(place, pieces, images, row_count):
    channels, segment = pieces[0].shape[2:]
    total = sum(edge_steps(count, segment)[1] for _, chunks in images for count, _ in chunks)
    given = () if len(pieces) == 1 else (place,)
    scalars = [pl.BlockSpec(memory_space=pltpu.SMEM)] * len(given)
    return pl.pallas_call(
        functools.partial(
            pack_kernel, images=tuple(chunks for _, chunks in images), last_row=row_count - 1
        ),
        out_shape=jax.ShapeDtypeStruct((total, channels, segment), jnp.bfloat16),
        grid=(1,),
        in_specs=scalars + [image_of(a, index) for index, _ in images for a in pieces],
        out_specs=pl.BlockSpec((total, channels, segment), lambda i: (0, 0, 0)),
        compiler_params=pltpu.CompilerParams(vmem_limit_bytes=VMEM_LIMIT),
        cost_estimate=cost(2),
    )(*given, *(list(pieces) * len(images)))


def feature_kernel(place_ref, *refs, spacing, offset, mesh_shape):
    (
        own_ref, partner_ref, cross_ref, w1_ref, w2_ref, unit_ref,
        w_ref, edge_ref, side_ref, p1_ref, p1e_ref, hid_ref, hide_ref, p2_ref, rhs0_ref, rhs1_ref, x_ref,
    ) = refs[-17:]
    part = pl.program_id(0)
    ends = len(refs) == 20
    mid_ref = refs[0]
    held, channels, segment = mid_ref.shape
    rows = unit_ref.shape[0]
    first_row, last_row = place_ref[0] == 0, place_ref[0] == mesh_shape[0] - 1
    first_col, last_col = place_ref[1] == 0, place_ref[1] == mesh_shape[1] - 1
    odd = place_ref[1] % 2 == 1
    above = first_row & (part == 0) & ends
    below = last_row & (part == pl.num_programs(0) - 1) & ends
    d1, d2 = FIRST_DILATION, SECOND_DILATION
    all_rows = rows + 2 * REACH
    hidden_rows = rows + 2 * d2
    steps = edge_ref.shape[0]
    groups = segment // SLOT
    lanes = lane_iota((channels, segment))
    in_slot = lanes % SLOT
    half = SLOT // 2
    rhs = (rhs0_ref, rhs1_ref)
    width = rhs0_ref.shape[1] // segment

    def stack(taps_ref):
        for a in range(3):
            for b in range(3):
                w_ref[a * channels : (a + 1) * channels, b * channels : (b + 1) * channels] = taps_ref[3 * a + b]

    for q in range(steps):
        own = own_ref[q]
        partner = partner_ref[q]
        cross = kept(cross_ref[q], ~(first_col | last_col))
        left = jnp.where(odd, partner, cross)
        right = jnp.where(odd, cross, partner)
        shift = half - REACH
        lower = pltpu.roll(jnp.where(in_slot < half, left, own), segment - shift, 1)
        upper = pltpu.roll(jnp.where(in_slot < half, own, right), shift, 1)
        edge_ref[q] = jnp.where(in_slot < half, lower, upper)
        side_ref[q] = pltpu.roll(jnp.where(in_slot < half, left, right), segment - shift, 1)

    def shifted(main, side, slot, amount):
        to_start = segment - REACH - slot * SLOT
        before = jnp.where(
            lanes < amount,
            pltpu.roll(side, lax.rem(to_start + amount, segment), 1),
            pltpu.roll(main, amount, 1),
        )
        after = jnp.where(
            lanes >= segment - amount,
            pltpu.roll(side, lax.rem(to_start + segment - amount, segment), 1),
            pltpu.roll(main, segment - amount, 1),
        )
        return before, after

    def put(target, j, main, before, after):
        lo = j * segment
        target[0:channels, lo : lo + segment] = before
        target[channels : 2 * channels, lo : lo + segment] = main
        target[2 * channels :, lo : lo + segment] = after

    def conv(source_ref, skip, sides_ref, product_ref, amount):
        def build(q, target):
            q = jnp.minimum(q, spacing - 1)
            side = sides_ref[q]
            for slot in range(groups):
                main = source_ref[slot * spacing + q + skip]
                put(target, slot, main, *shifted(main, side, slot, amount))

        def multiply_rows(q, source):
            product = jnp.dot(w_ref[...], source[...], preferred_element_type=jnp.float32)
            for slot in range(groups):
                product_ref[slot * spacing + q] = product[:, slot * segment : (slot + 1) * segment]

        build(0, rhs0_ref)

        def body(u, _):
            build(2 * u + 1, rhs1_ref)
            multiply_rows(2 * u, rhs0_ref)
            build(2 * u + 2, rhs0_ref)
            multiply_rows(2 * u + 1, rhs1_ref)
            return 0

        lax.fori_loop(0, spacing // 2, body, 0)
        if spacing % 2:
            multiply_rows(spacing - 1, rhs0_ref)

    if ends:
        top, bottom = either_side(place_ref, refs[1][...], refs[2][...])
        top, bottom = kept(top, ~first_row), kept(bottom, ~last_row)
        if rows == held:
            x_ref[0:REACH] = top
            x_ref[REACH : REACH + rows] = mid_ref[...]
            x_ref[REACH + rows :] = bottom
        else:

            @pl.when(part == 0)
            def _():
                x_ref[0:REACH] = top
                x_ref[REACH:] = mid_ref[: rows + REACH]

            @pl.when(part == 1)
            def _():
                x_ref[: rows + REACH] = mid_ref[held - rows - REACH :]
                x_ref[rows + REACH :] = bottom

    else:
        x_ref = mid_ref

    stack(w1_ref)
    conv(x_ref, offset, side_ref, p1_ref, d1)

    pending = [
        (p1_ref, row, x_ref[row + offset], groups - 1, row - (groups - 1) * spacing)
        for row in range(groups * spacing, all_rows)
    ]
    pending += [(p1e_ref, q, edge_ref[q], None, None) for q in range(steps)]
    for t in range(pl.cdiv(len(pending), width)):
        target = rhs[t % 2]
        batch = pending[t * width : (t + 1) * width]
        for j, (_, _, main, slot, q) in enumerate(batch):
            if slot is None:
                moved = pltpu.roll(main, d1, 1), pltpu.roll(main, segment - d1, 1)
            else:
                moved = shifted(main, side_ref[q], slot, d1)
            put(target, j, main, *moved)
        product = jnp.dot(
            w_ref[...], target[:, : len(batch) * segment], preferred_element_type=jnp.float32
        )
        for j, (product_ref, row, _, _, _) in enumerate(batch):
            product_ref[row] = product[:, j * segment : (j + 1) * segment]

    def three(product_ref, row, apart):
        return (
            product_ref[row, 0:channels]
            + product_ref[row + apart, channels : 2 * channels]
            + product_ref[row + 2 * apart, 2 * channels :]
        )

    def silu(v):
        return v / (1.0 + jnp.exp(-v))

    def hidden(t, _):
        for j in range(8):
            row = 8 * t + j
            outside = ((row < d2) & above) | ((row >= d2 + rows) & below)
            value = silu(three(p1_ref, row, d1))
            hid_ref[row] = jnp.where(outside, 0.0, value).astype(jnp.bfloat16)
        return 0

    lax.fori_loop(0, hidden_rows // 8, hidden, 0)

    left_out = (in_slot < REACH) & first_col
    right_out = (in_slot >= half + 2) & last_col
    for q in range(spacing):
        row = (lanes // SLOT) * spacing + q
        outside = ((row < d2) & above) | ((row >= d2 + rows) & below) | left_out | right_out
        value = silu(three(p1e_ref, q, d1))
        value = jnp.where(outside, 0.0, value).astype(jnp.bfloat16)
        gap = half + 2 - REACH
        hide_ref[q] = jnp.where(in_slot < REACH, value, pltpu.roll(value, segment - gap, 1))

    stack(w2_ref)
    conv(hid_ref, 0, hide_ref, p2_ref, d2)

    def finish(t, _):
        for j in range(8):
            row = 8 * t + j
            total = x_ref[row + offset + REACH].astype(jnp.float32) + three(p2_ref, row, d2)
            feature = total.astype(jnp.bfloat16).astype(jnp.float32)
            mean = jnp.sum(feature * feature, axis=0, keepdims=True) * (1.0 / channels)
            unit_ref[row] = (feature * lax.rsqrt(mean + epsilon)).astype(jnp.bfloat16)
        return 0

    lax.fori_loop(0, rows // 8, finish, 0)


def unit_features(place, pieces, index, parts, rows, offset, edges, base, w1, w2, mesh_shape):
    channels, segment = pieces[0].shape[2:]
    all_rows = rows + 2 * REACH
    hidden_rows = rows + 2 * SECOND_DILATION
    spacing, steps = edge_steps(rows, segment)
    width = segment // SLOT
    products = (3 * channels, segment)
    assembled = all_rows if len(pieces) == 3 else 1
    return pl.pallas_call(
        functools.partial(feature_kernel, spacing=spacing, offset=offset, mesh_shape=mesh_shape),
        out_shape=jax.ShapeDtypeStruct((parts * rows, channels, segment), jnp.bfloat16),
        grid=(parts,),
        in_specs=[pl.BlockSpec(memory_space=pltpu.SMEM)]
        + [image_of(a, index) for a in pieces]
        + [
            pl.BlockSpec(
                (pl.Element(steps), pl.Element(channels), pl.Element(segment)),
                lambda i: (base + i * steps, 0, 0),
            )
            for _ in edges
        ]
        + [whole(w1), whole(w2)],
        out_specs=pl.BlockSpec((rows, channels, segment), lambda i: (i, 0, 0)),
        scratch_shapes=[
            pltpu.VMEM((3 * channels, 3 * channels), jnp.bfloat16),
            pltpu.VMEM((steps, channels, segment), jnp.bfloat16),
            pltpu.VMEM((steps, channels, segment), jnp.bfloat16),
            pltpu.VMEM((all_rows,) + products, jnp.float32),
            pltpu.VMEM((steps,) + products, jnp.float32),
            pltpu.VMEM((hidden_rows, channels, segment), jnp.bfloat16),
            pltpu.VMEM((spacing, channels, segment), jnp.bfloat16),
            pltpu.VMEM((hidden_rows,) + products, jnp.float32),
            pltpu.VMEM((3 * channels, width * segment), jnp.bfloat16),
            pltpu.VMEM((3 * channels, width * segment), jnp.bfloat16),
            pltpu.VMEM((assembled, channels, segment), jnp.bfloat16),
        ],
        compiler_params=pltpu.CompilerParams(vmem_limit_bytes=VMEM_LIMIT),
        cost_estimate=cost(parts * rows * 0.2),
    )(place, *pieces, *edges, w1, w2)


def add_step(place_ref, range_ref, group, step, left_ref, mine_ref, theirs_ref, acc_ref, bias_ref, scores_ref):
    _, channels, segment = left_ref.shape
    block = place_ref[1]
    low = segment * range_ref[0, group]
    high = low + segment * range_ref[1, group]
    odd = block % 2
    base = segment * (block - 2 * (block // 2 - step))
    active = (base + segment - 1 >= low) & (base - 2 * segment + 1 < high) & (block // 2 >= step)
    scale = sharpness_divisor / channels * LOG2E

    def key_column(shape):
        column = lane_iota(shape)
        own = column < segment
        return column % segment + segment * jnp.where(own, odd, 1 - odd)

    @pl.when(active)
    def _():
        wide = (segment, 2 * segment)
        offsets = base + lax.broadcasted_iota(jnp.int32, wide, 0) - key_column(wide)
        inside = (offsets >= low) & (offsets < high)
        bias_ref[...] = jnp.where(inside, 0.0, -1e30)
        kind = lax.broadcasted_iota(jnp.int32, (EXTRA, 2 * segment), 0)
        column = key_column((EXTRA, 2 * segment))
        extra = jnp.where(kind == 0, 1, jnp.where(kind == 1, column, jnp.where(kind == 2, step, 0)))
        extra = extra.astype(jnp.float32).astype(jnp.bfloat16)
        rows = left_ref.shape[0]

        def score(r):
            keys = jnp.concatenate([mine_ref[r], theirs_ref[r]], axis=1)
            scores_ref[r % 2] = lax.dot_general(
                left_ref[r], keys, (((0,), (0,)), ((), ())), preferred_element_type=jnp.float32
            )

        score(0)
        for r in range(rows):
            if r + 1 < rows:
                score(r + 1)
            weights = jnp.exp2(scores_ref[r % 2] * scale + bias_ref[...]).astype(jnp.bfloat16)
            keys = jnp.concatenate([mine_ref[r], theirs_ref[r]], axis=1)
            extended = jnp.concatenate([keys, extra], axis=0)
            acc_ref[r] += lax.dot_general(
                extended, weights, (((1,), (1,)), ((), ())), preferred_element_type=jnp.float32
            )


def group_of(i, inner, groups):
    quarter = groups // 4
    return i + quarter if inner else jnp.where(i < quarter, i, i + 2 * quarter)


def gather_kernel(place_ref, range_ref, left_ref, *refs, inner, groups, start, count):
    keys, (acc_ref, bias_ref, scores_ref) = refs[: 2 * count], refs[-3:]
    group = group_of(pl.program_id(0), inner, groups)
    acc_ref[...] = refs[2 * count][...] if start else jnp.zeros_like(acc_ref)
    for index in range(count):
        add_step(
            place_ref, range_ref, group, start + index, left_ref, keys[2 * index], keys[2 * index + 1],
            acc_ref, bias_ref, scores_ref,
        )


def finish_kernel(
    place_ref, range_ref, left_ref, mine_ref, theirs_ref, acc_in_ref, *refs, inner, groups, step
):
    matched_ref, disparity_ref, acc_ref, bias_ref, scores_ref, rows_ref = refs[-6:]
    group = group_of(pl.program_id(0), inner, groups)
    rows, channels, segment = left_ref.shape
    acc_ref[...] = acc_in_ref[...]
    add_step(
        place_ref, range_ref, group, step, left_ref, mine_ref, theirs_ref, acc_ref, bias_ref, scores_ref
    )
    block = place_ref[1]
    low = segment * range_ref[0, group]
    high = low + segment * range_ref[1, group]
    x = block * segment + lane_iota((1, segment))
    from_chip = (x - 2 * segment * (block // 2)).astype(jnp.float32)
    start = jnp.maximum(low, x + 1)
    beyond = jnp.maximum(high - start, 0)
    beyond_sum = ((start + high - 1) * beyond).astype(jnp.float32) * 0.5
    beyond = beyond.astype(jnp.float32)
    for r in range(rows):
        turned = acc_ref[r]
        near = turned[channels : channels + 1]
        column = turned[channels + 1 : channels + 2]
        passed = turned[channels + 2 : channels + 3]
        inverse = 1.0 / (near + beyond)
        shift = from_chip * near - column + (2 * segment) * passed + beyond_sum
        rows_ref[r] = turned[:channels] * inverse
        disparity_ref[r : r + 1, :] = shift * inverse * (1.0 / segment)
    matched_ref[...] = jnp.swapaxes(rows_ref[...].astype(jnp.bfloat16), 0, 1)


def correlate(place, ranges, left, keys, acc, start, inner):
    rows, channels, segment = left.shape
    groups = rows // RG
    own_groups = keys[0][0].shape[0] // RG
    block = (RG, channels, segment)
    smem = pl.BlockSpec(memory_space=pltpu.SMEM)
    held = channels + EXTRA
    acc_spec = pl.BlockSpec((RG, held, segment), lambda i: (i, 0, 0))
    given = (acc,) if start else ()
    return pl.pallas_call(
        functools.partial(gather_kernel, inner=inner, groups=groups, start=start, count=len(keys)),
        out_shape=jax.ShapeDtypeStruct((own_groups * RG, held, segment), jnp.float32),
        grid=(own_groups,),
        in_specs=[smem, smem, pl.BlockSpec(block, lambda i: (group_of(i, inner, groups), 0, 0))]
        + [pl.BlockSpec(block, lambda i: (i, 0, 0))] * (2 * len(keys))
        + [acc_spec] * len(given),
        out_specs=acc_spec,
        scratch_shapes=[
            pltpu.VMEM((segment, 2 * segment), jnp.float32),
            pltpu.VMEM((2, segment, 2 * segment), jnp.float32),
        ],
        input_output_aliases={3 + 2 * len(keys): 0} if given else {},
        compiler_params=pltpu.CompilerParams(vmem_limit_bytes=VMEM_LIMIT),
        cost_estimate=cost(1.5 * own_groups),
    )(place, ranges, left, *[a for pair in keys for a in pair], *given)


def finish(place, ranges, left, pair, acc, outs, inner, step):
    rows, channels, segment = left.shape
    groups = rows // RG
    own_groups = pair[0].shape[0] // RG
    block = (RG, channels, segment)
    smem = pl.BlockSpec(memory_space=pltpu.SMEM)

    def group(i):
        return group_of(i, inner, groups)

    given = () if outs is None else tuple(outs)
    return pl.pallas_call(
        functools.partial(finish_kernel, inner=inner, groups=groups, step=step),
        out_shape=(
            jax.ShapeDtypeStruct((channels, rows, segment), jnp.bfloat16),
            jax.ShapeDtypeStruct((rows, segment), jnp.float32),
        ),
        grid=(own_groups,),
        in_specs=[
            smem,
            smem,
            pl.BlockSpec(block, lambda i: (group(i), 0, 0)),
            pl.BlockSpec(block, lambda i: (i, 0, 0)),
            pl.BlockSpec(block, lambda i: (i, 0, 0)),
            pl.BlockSpec((RG, channels + EXTRA, segment), lambda i: (i, 0, 0)),
        ]
        + [pl.BlockSpec(memory_space=pl.ANY)] * len(given),
        out_specs=(
            pl.BlockSpec((channels, RG, segment), lambda i: (0, group(i), 0)),
            pl.BlockSpec((RG, segment), lambda i: (group(i), 0)),
        ),
        scratch_shapes=[
            pltpu.VMEM((RG, channels + EXTRA, segment), jnp.float32),
            pltpu.VMEM((segment, 2 * segment), jnp.float32),
            pltpu.VMEM((2, segment, 2 * segment), jnp.float32),
            pltpu.VMEM((RG, channels, segment), jnp.float32),
        ],
        input_output_aliases={6: 0, 7: 1} if given else {},
        compiler_params=pltpu.CompilerParams(vmem_limit_bytes=VMEM_LIMIT),
        cost_estimate=cost(own_groups),
    )(place, ranges, left, *pair, acc, *given)


def both_ways(pairs):
    return pairs + [(b, a) for a, b in pairs]


def program(images, first_weight, second_weight, search_ranges):
    row_count = lax.axis_size("rows")
    col_count = lax.axis_size("cols")
    col = lax.axis_index("cols")
    _, rows, segment = images.shape[1:]
    place = jnp.stack([lax.axis_index("rows"), col]).astype(jnp.int32)
    ranges = search_ranges.reshape(2, rows // RG)

    swap = [(i, i ^ 1) for i in range(col_count)]
    across = both_ways([(i, i + 1) for i in range(1, col_count - 1, 2)])
    around_across = across + both_ways([(0, col_count - 1)])
    hop = [(i, (i + 2) % col_count) for i in range(col_count)]
    near_pairs = both_ways([(i, i + 1) for i in range(0, row_count, 2)])
    far_pairs = both_ways([(i, (i + 1) % row_count) for i in range(1, row_count, 2)])

    def exchanged(pieces, chunks, pairs):
        own = pack_edges(place, pieces, chunks, row_count)
        cross = lax.ppermute(own, "cols", pairs)
        partner = lax.ppermute(own, "cols", swap)
        return own, partner, cross

    def features(pieces, index, parts, count, offset, edges, base):
        return unit_features(
            place, pieces, index, parts, count, offset, edges, base,
            first_weight, second_weight, (row_count, col_count),
        )

    mid = images.transpose(0, 2, 1, 3)
    odd_row = lax.axis_index("rows") % 2 == 1
    first_rows, last_rows = mid[:, :REACH], mid[:, rows - REACH :]
    near = lax.ppermute(jnp.where(odd_row, first_rows, last_rows), "rows", near_pairs)
    far = lax.ppermute(jnp.where(odd_row, last_rows, first_rows), "rows", far_pairs)

    strip = rows // 4
    inner = rows - 2 * strip
    around = (mid, near, far)
    edges_a = exchanged((mid,), ((1, ((inner, strip),)),), around_across)
    chunks_r = (1, ((strip, 0), (strip, rows - strip))), (0, ((rows, 0),))
    edges_r = exchanged(around, chunks_r, across)
    right_a = features((mid,), 1, 1, inner, strip - REACH, edges_a, 0)
    right_b = features(around, 1, 2, strip, 0, edges_r, 0)
    left = features(around, 0, 1, rows, 0, edges_r, 2 * edge_steps(strip, segment)[1])

    steps = min(col_count // 2 - 1, HOPS // 2)
    early = max(steps - 1, 1)

    def chain(mine):
        pairs = []
        for step in range(steps + 1):
            if step:
                mine = lax.ppermute(mine, "cols", hop)
            pairs.append((mine, lax.ppermute(mine, "cols", swap)))
        return pairs

    def totals(keys, inside):
        acc = correlate(place, ranges, left, keys[:early], None, 0, inside)
        if early == steps:
            return acc
        return correlate(place, ranges, left, keys[early:steps], acc, early, inside)

    keys_a, keys_b = chain(right_a), chain(right_b)
    acc_a, acc_b = totals(keys_a, True), totals(keys_b, False)
    outs = finish(place, ranges, left, keys_a[steps], acc_a, None, True, steps)
    return finish(place, ranges, left, keys_b[steps], acc_b, outs, False, steps)


def solution(mesh):
    placed = (P(None, None, "rows", "cols"), P(), P(), P(None, "rows", "cols"))
    return jax.shard_map(
        program,
        mesh=mesh,
        in_specs=placed,
        out_specs=(P(None, "rows", "cols"), P("rows", "cols")),
        check_vma=False,
    )
```

```python
import functools

import jax
import jax.numpy as jnp
from jax import lax
from jax.experimental import pallas as pl
from jax.experimental.pallas import tpu as pltpu
from jax.sharding import PartitionSpec as P


RG = 8
FIRST_DILATION = 2
SECOND_DILATION = 4
HOPS = 18
REACH = FIRST_DILATION + SECOND_DILATION
SLOT = 16

EXTRA = 16

sharpness_divisor = 10.0
epsilon = 1e-05
VMEM_LIMIT = 64 << 20
LOG2E = 1.4426950408889634


def lane_iota(shape):
    return lax.broadcasted_iota(jnp.int32, shape, len(shape) - 1)


def cost(microseconds):
    return pl.CostEstimate(
        flops=int(microseconds * 1e9), transcendentals=0, bytes_accessed=int(microseconds * 3e6)
    )


def cost(microseconds):
    return pl.CostEstimate(
        flops=int(microseconds * 1e9), transcendentals=0, bytes_accessed=int(microseconds * 3e6)
    )


def ends_kernel(low_ref, high_ref, first_ref, last_ref):
    first_ref[...] = jnp.swapaxes(low_ref[...], 0, 1)[:REACH]
    last_ref[...] = jnp.swapaxes(high_ref[...], 0, 1)[RG - REACH :]


def end_rows(images):
    count, channels, rows, segment = images.shape
    tile = (None, channels, RG, segment)
    ends = jax.ShapeDtypeStruct((count, REACH, channels, segment), jnp.bfloat16)
    ends_spec = pl.BlockSpec((None, REACH, channels, segment), lambda n: (n, 0, 0, 0))
    return pl.pallas_call(
        ends_kernel,
        out_shape=(ends, ends),
        grid=(count,),
        in_specs=[
            pl.BlockSpec(tile, lambda n: (n, 0, 0, 0)),
            pl.BlockSpec(tile, lambda n: (n, 0, rows // RG - 1, 0)),
        ],
        out_specs=(ends_spec, ends_spec),
        compiler_params=pltpu.CompilerParams(vmem_limit_bytes=VMEM_LIMIT),
        cost_estimate=cost(1),
    )(images, images)


def edge_steps(rows, segment):
    spacing = (rows + 2 * SECOND_DILATION) // (segment // SLOT)
    return spacing, spacing + 2 * FIRST_DILATION


def kept(piece, inside):
    return jnp.where(inside, piece, jnp.zeros_like(piece))


def pack_kernel(*refs, images, last_row):
    edge_ref = refs[-1]
    alone = len(refs) == 2
    place_ref = None if alone else refs[0]
    refs = refs[:-1] if alone else refs[1:-1]
    per_image = len(refs) // len(images)
    base = 0
    for n, chunks in enumerate(images):
        mid_ref = refs[n * per_image]
        around = refs[n * per_image + 1 : (n + 1) * per_image]
        rows, channels, segment = mid_ref.shape
        slot_of = lane_iota((channels, segment)) // SLOT

        def row_at(row):
            if row < 0:
                return kept(around[0][row + REACH], place_ref[0] > 0)
            if row >= rows:
                return kept(around[1][row - rows], place_ref[0] < last_row)
            return mid_ref[row]

        for count, first in chunks:
            spacing, steps = edge_steps(count, segment)
            for q in range(steps):
                packed = None
                for g in range(segment // SLOT):
                    shift = (SLOT * g + SLOT // 2) % segment
                    moved = pltpu.roll(row_at(first - REACH + g * spacing + q), shift, 1)
                    packed = moved if packed is None else jnp.where(slot_of == g, moved, packed)
                edge_ref[base + q] = packed
            base += steps


def whole(a):
    return pl.BlockSpec(a.shape, lambda i: (0,) * a.ndim)


def image_of(a, index):
    return pl.BlockSpec((None,) + a.shape[1:], lambda i: (index, 0, 0, 0))


def pack_edges(place, pieces, images, row_count):
    channels, segment = pieces[0].shape[2:]
    total = sum(edge_steps(count, segment)[1] for _, chunks in images for count, _ in chunks)
    given = () if len(pieces) == 1 else (place,)
    scalars = [pl.BlockSpec(memory_space=pltpu.SMEM)] * len(given)
    return pl.pallas_call(
        functools.partial(
            pack_kernel, images=tuple(chunks for _, chunks in images), last_row=row_count - 1
        ),
        out_shape=jax.ShapeDtypeStruct((total, channels, segment), jnp.bfloat16),
        grid=(1,),
        in_specs=scalars + [image_of(a, index) for index, _ in images for a in pieces],
        out_specs=pl.BlockSpec((total, channels, segment), lambda i: (0, 0, 0)),
        compiler_params=pltpu.CompilerParams(vmem_limit_bytes=VMEM_LIMIT),
        cost_estimate=cost(2),
    )(*given, *(list(pieces) * len(images)))


def feature_kernel(place_ref, *refs, spacing, offset, mesh_shape):
    (
        own_ref, partner_ref, cross_ref, w1_ref, w2_ref, unit_ref,
        w_ref, edge_ref, side_ref, p1_ref, p1e_ref, hid_ref, hide_ref, p2_ref, rhs0_ref, rhs1_ref, x_ref,
    ) = refs[-17:]
    part = pl.program_id(0)
    ends = len(refs) == 20
    mid_ref = refs[0]
    held, channels, segment = mid_ref.shape
    rows = unit_ref.shape[0]
    first_row, last_row = place_ref[0] == 0, place_ref[0] == mesh_shape[0] - 1
    first_col, last_col = place_ref[1] == 0, place_ref[1] == mesh_shape[1] - 1
    odd = place_ref[1] % 2 == 1
    above = first_row & (part == 0) & ends
    below = last_row & (part == pl.num_programs(0) - 1) & ends
    d1, d2 = FIRST_DILATION, SECOND_DILATION
    all_rows = rows + 2 * REACH
    hidden_rows = rows + 2 * d2
    steps = edge_ref.shape[0]
    groups = segment // SLOT
    lanes = lane_iota((channels, segment))
    in_slot = lanes % SLOT
    half = SLOT // 2
    rhs = (rhs0_ref, rhs1_ref)
    width = rhs0_ref.shape[1] // segment

    def stack(taps_ref):
        for a in range(3):
            for b in range(3):
                w_ref[a * channels : (a + 1) * channels, b * channels : (b + 1) * channels] = taps_ref[3 * a + b]

    for q in range(steps):
        own = own_ref[q]
        partner = partner_ref[q]
        cross = cross_ref[q]
        left = jnp.where(odd, partner, cross)
        right = jnp.where(odd, cross, partner)
        shift = half - REACH
        lower = pltpu.roll(jnp.where(in_slot < half, left, own), segment - shift, 1)
        upper = pltpu.roll(jnp.where(in_slot < half, own, right), shift, 1)
        edge_ref[q] = jnp.where(in_slot < half, lower, upper)
        side_ref[q] = pltpu.roll(jnp.where(in_slot < half, left, right), segment - shift, 1)

    def shifted(main, side, slot, amount):
        to_start = segment - REACH - slot * SLOT
        before = jnp.where(
            lanes < amount,
            pltpu.roll(side, lax.rem(to_start + amount, segment), 1),
            pltpu.roll(main, amount, 1),
        )
        after = jnp.where(
            lanes >= segment - amount,
            pltpu.roll(side, lax.rem(to_start + segment - amount, segment), 1),
            pltpu.roll(main, segment - amount, 1),
        )
        return before, after

    def put(target, j, main, before, after):
        lo = j * segment
        target[0:channels, lo : lo + segment] = before
        target[channels : 2 * channels, lo : lo + segment] = main
        target[2 * channels :, lo : lo + segment] = after

    def conv(source_ref, skip, sides_ref, product_ref, amount):
        def build(q, target):
            q = jnp.minimum(q, spacing - 1)
            side = sides_ref[q]
            for slot in range(groups):
                main = source_ref[slot * spacing + q + skip]
                put(target, slot, main, *shifted(main, side, slot, amount))

        def multiply_rows(q, source):
            product = jnp.dot(w_ref[...], source[...], preferred_element_type=jnp.float32)
            for slot in range(groups):
                product_ref[slot * spacing + q] = product[:, slot * segment : (slot + 1) * segment]

        build(0, rhs0_ref)

        def body(u, _):
            build(2 * u + 1, rhs1_ref)
            multiply_rows(2 * u, rhs0_ref)
            build(2 * u + 2, rhs0_ref)
            multiply_rows(2 * u + 1, rhs1_ref)
            return 0

        lax.fori_loop(0, spacing // 2, body, 0)
        if spacing % 2:
            multiply_rows(spacing - 1, rhs0_ref)

    if ends:
        top = kept(refs[1][...], ~first_row)
        bottom = kept(refs[2][...], ~last_row)
        if rows == held:
            x_ref[0:REACH] = top
            x_ref[REACH : REACH + rows] = mid_ref[...]
            x_ref[REACH + rows :] = bottom
        else:

            @pl.when(part == 0)
            def _():
                x_ref[0:REACH] = top
                x_ref[REACH:] = mid_ref[: rows + REACH]

            @pl.when(part == 1)
            def _():
                x_ref[: rows + REACH] = mid_ref[held - rows - REACH :]
                x_ref[rows + REACH :] = bottom

    else:
        x_ref = mid_ref

    stack(w1_ref)
    conv(x_ref, offset, side_ref, p1_ref, d1)

    pending = [
        (p1_ref, row, x_ref[row + offset], groups - 1, row - (groups - 1) * spacing)
        for row in range(groups * spacing, all_rows)
    ]
    pending += [(p1e_ref, q, edge_ref[q], None, None) for q in range(steps)]
    for t in range(pl.cdiv(len(pending), width)):
        target = rhs[t % 2]
        batch = pending[t * width : (t + 1) * width]
        for j, (_, _, main, slot, q) in enumerate(batch):
            if slot is None:
                moved = pltpu.roll(main, d1, 1), pltpu.roll(main, segment - d1, 1)
            else:
                moved = shifted(main, side_ref[q], slot, d1)
            put(target, j, main, *moved)
        product = jnp.dot(
            w_ref[...], target[:, : len(batch) * segment], preferred_element_type=jnp.float32
        )
        for j, (product_ref, row, _, _, _) in enumerate(batch):
            product_ref[row] = product[:, j * segment : (j + 1) * segment]

    def three(product_ref, row, apart):
        return (
            product_ref[row, 0:channels]
            + product_ref[row + apart, channels : 2 * channels]
            + product_ref[row + 2 * apart, 2 * channels :]
        )

    def silu(v):
        return v / (1.0 + jnp.exp(-v))

    def hidden(t, _):
        for j in range(8):
            row = 8 * t + j
            outside = ((row < d2) & above) | ((row >= d2 + rows) & below)
            value = silu(three(p1_ref, row, d1))
            hid_ref[row] = jnp.where(outside, 0.0, value).astype(jnp.bfloat16)
        return 0

    lax.fori_loop(0, hidden_rows // 8, hidden, 0)

    left_out = (in_slot < REACH) & first_col
    right_out = (in_slot >= half + 2) & last_col
    for q in range(spacing):
        row = (lanes // SLOT) * spacing + q
        outside = ((row < d2) & above) | ((row >= d2 + rows) & below) | left_out | right_out
        value = silu(three(p1e_ref, q, d1))
        value = jnp.where(outside, 0.0, value).astype(jnp.bfloat16)
        gap = half + 2 - REACH
        hide_ref[q] = jnp.where(in_slot < REACH, value, pltpu.roll(value, segment - gap, 1))

    stack(w2_ref)
    conv(hid_ref, 0, hide_ref, p2_ref, d2)

    def finish(t, _):
        for j in range(8):
            row = 8 * t + j
            total = x_ref[row + offset + REACH].astype(jnp.float32) + three(p2_ref, row, d2)
            feature = total.astype(jnp.bfloat16).astype(jnp.float32)
            mean = jnp.sum(feature * feature, axis=0, keepdims=True) * (1.0 / channels)
            unit_ref[row] = (feature * lax.rsqrt(mean + epsilon)).astype(jnp.bfloat16)
        return 0

    lax.fori_loop(0, rows // 8, finish, 0)


def unit_features(place, pieces, index, parts, rows, offset, edges, base, w1, w2, mesh_shape):
    channels, segment = pieces[0].shape[2:]
    all_rows = rows + 2 * REACH
    hidden_rows = rows + 2 * SECOND_DILATION
    spacing, steps = edge_steps(rows, segment)
    width = segment // SLOT
    products = (3 * channels, segment)
    assembled = all_rows if len(pieces) == 3 else 1
    return pl.pallas_call(
        functools.partial(feature_kernel, spacing=spacing, offset=offset, mesh_shape=mesh_shape),
        out_shape=jax.ShapeDtypeStruct((parts * rows, channels, segment), jnp.bfloat16),
        grid=(parts,),
        in_specs=[pl.BlockSpec(memory_space=pltpu.SMEM)]
        + [image_of(a, index) for a in pieces]
        + [
            pl.BlockSpec(
                (pl.Element(steps), pl.Element(channels), pl.Element(segment)),
                lambda i: (base + i * steps, 0, 0),
            )
            for _ in edges
        ]
        + [whole(w1), whole(w2)],
        out_specs=pl.BlockSpec((rows, channels, segment), lambda i: (i, 0, 0)),
        scratch_shapes=[
            pltpu.VMEM((3 * channels, 3 * channels), jnp.bfloat16),
            pltpu.VMEM((steps, channels, segment), jnp.bfloat16),
            pltpu.VMEM((steps, channels, segment), jnp.bfloat16),
            pltpu.VMEM((all_rows,) + products, jnp.float32),
            pltpu.VMEM((steps,) + products, jnp.float32),
            pltpu.VMEM((hidden_rows, channels, segment), jnp.bfloat16),
            pltpu.VMEM((spacing, channels, segment), jnp.bfloat16),
            pltpu.VMEM((hidden_rows,) + products, jnp.float32),
            pltpu.VMEM((3 * channels, width * segment), jnp.bfloat16),
            pltpu.VMEM((3 * channels, width * segment), jnp.bfloat16),
            pltpu.VMEM((assembled, channels, segment), jnp.bfloat16),
        ],
        compiler_params=pltpu.CompilerParams(vmem_limit_bytes=VMEM_LIMIT),
        cost_estimate=cost(parts * rows * 0.2),
    )(place, *pieces, *edges, w1, w2)


def add_step(place_ref, range_ref, group, step, left_ref, mine_ref, theirs_ref, acc_ref, bias_ref, scores_ref):
    _, channels, segment = left_ref.shape
    block = place_ref[1]
    low = segment * range_ref[0, group]
    high = low + segment * range_ref[1, group]
    odd = block % 2
    base = segment * (block - 2 * (block // 2 - step))
    active = (base + segment - 1 >= low) & (base - 2 * segment + 1 < high) & (block // 2 >= step)
    scale = sharpness_divisor / channels * LOG2E

    def key_column(shape):
        column = lane_iota(shape)
        own = column < segment
        return column % segment + segment * jnp.where(own, odd, 1 - odd)

    @pl.when(active)
    def _():
        wide = (segment, 2 * segment)
        offsets = base + lax.broadcasted_iota(jnp.int32, wide, 0) - key_column(wide)
        inside = (offsets >= low) & (offsets < high)
        bias_ref[...] = jnp.where(inside, 0.0, -1e30)
        kind = lax.broadcasted_iota(jnp.int32, (EXTRA, 2 * segment), 0)
        column = key_column((EXTRA, 2 * segment))
        extra = jnp.where(kind == 0, 1, jnp.where(kind == 1, column, jnp.where(kind == 2, step, 0)))
        extra = extra.astype(jnp.float32).astype(jnp.bfloat16)
        rows = left_ref.shape[0]

        def score(r):
            keys = jnp.concatenate([mine_ref[r], theirs_ref[r]], axis=1)
            scores_ref[r % 2] = lax.dot_general(
                left_ref[r], keys, (((0,), (0,)), ((), ())), preferred_element_type=jnp.float32
            )

        score(0)
        for r in range(rows):
            if r + 1 < rows:
                score(r + 1)
            weights = jnp.exp2(scores_ref[r % 2] * scale + bias_ref[...]).astype(jnp.bfloat16)
            keys = jnp.concatenate([mine_ref[r], theirs_ref[r]], axis=1)
            extended = jnp.concatenate([keys, extra], axis=0)
            acc_ref[r] += lax.dot_general(
                extended, weights, (((1,), (1,)), ((), ())), preferred_element_type=jnp.float32
            )


def group_of(i, inner, groups):
    quarter = groups // 4
    return i + quarter if inner else jnp.where(i < quarter, i, i + 2 * quarter)


def gather_kernel(place_ref, range_ref, left_ref, *refs, inner, groups, start, count):
    keys, (acc_ref, bias_ref, scores_ref) = refs[: 2 * count], refs[-3:]
    group = group_of(pl.program_id(0), inner, groups)
    acc_ref[...] = refs[2 * count][...] if start else jnp.zeros_like(acc_ref)
    for index in range(count):
        add_step(
            place_ref, range_ref, group, start + index, left_ref, keys[2 * index], keys[2 * index + 1],
            acc_ref, bias_ref, scores_ref,
        )


def finish_kernel(
    place_ref, range_ref, left_ref, mine_ref, theirs_ref, acc_in_ref, *refs, inner, groups, step
):
    matched_ref, disparity_ref, acc_ref, bias_ref, scores_ref, rows_ref = refs[-6:]
    group = group_of(pl.program_id(0), inner, groups)
    rows, channels, segment = left_ref.shape
    acc_ref[...] = acc_in_ref[...]
    add_step(
        place_ref, range_ref, group, step, left_ref, mine_ref, theirs_ref, acc_ref, bias_ref, scores_ref
    )
    block = place_ref[1]
    low = segment * range_ref[0, group]
    high = low + segment * range_ref[1, group]
    x = block * segment + lane_iota((1, segment))
    from_chip = (x - 2 * segment * (block // 2)).astype(jnp.float32)
    start = jnp.maximum(low, x + 1)
    beyond = jnp.maximum(high - start, 0)
    beyond_sum = ((start + high - 1) * beyond).astype(jnp.float32) * 0.5
    beyond = beyond.astype(jnp.float32)
    for r in range(rows):
        turned = acc_ref[r]
        near = turned[channels : channels + 1]
        column = turned[channels + 1 : channels + 2]
        passed = turned[channels + 2 : channels + 3]
        inverse = 1.0 / (near + beyond)
        shift = from_chip * near - column + (2 * segment) * passed + beyond_sum
        rows_ref[r] = turned[:channels] * inverse
        disparity_ref[r : r + 1, :] = shift * inverse * (1.0 / segment)
    matched_ref[...] = jnp.swapaxes(rows_ref[...].astype(jnp.bfloat16), 0, 1)


def correlate(place, ranges, left, keys, acc, start, inner):
    rows, channels, segment = left.shape
    groups = rows // RG
    own_groups = keys[0][0].shape[0] // RG
    block = (RG, channels, segment)
    smem = pl.BlockSpec(memory_space=pltpu.SMEM)
    held = channels + EXTRA
    acc_spec = pl.BlockSpec((RG, held, segment), lambda i: (i, 0, 0))
    given = (acc,) if start else ()
    return pl.pallas_call(
        functools.partial(gather_kernel, inner=inner, groups=groups, start=start, count=len(keys)),
        out_shape=jax.ShapeDtypeStruct((own_groups * RG, held, segment), jnp.float32),
        grid=(own_groups,),
        in_specs=[smem, smem, pl.BlockSpec(block, lambda i: (group_of(i, inner, groups), 0, 0))]
        + [pl.BlockSpec(block, lambda i: (i, 0, 0))] * (2 * len(keys))
        + [acc_spec] * len(given),
        out_specs=acc_spec,
        scratch_shapes=[
            pltpu.VMEM((segment, 2 * segment), jnp.float32),
            pltpu.VMEM((2, segment, 2 * segment), jnp.float32),
        ],
        input_output_aliases={3 + 2 * len(keys): 0} if given else {},
        compiler_params=pltpu.CompilerParams(vmem_limit_bytes=VMEM_LIMIT),
        cost_estimate=cost(1.5 * own_groups),
    )(place, ranges, left, *[a for pair in keys for a in pair], *given)


def finish(place, ranges, left, pair, acc, outs, inner, step):
    rows, channels, segment = left.shape
    groups = rows // RG
    own_groups = pair[0].shape[0] // RG
    block = (RG, channels, segment)
    smem = pl.BlockSpec(memory_space=pltpu.SMEM)

    def group(i):
        return group_of(i, inner, groups)

    given = () if outs is None else tuple(outs)
    return pl.pallas_call(
        functools.partial(finish_kernel, inner=inner, groups=groups, step=step),
        out_shape=(
            jax.ShapeDtypeStruct((channels, rows, segment), jnp.bfloat16),
            jax.ShapeDtypeStruct((rows, segment), jnp.float32),
        ),
        grid=(own_groups,),
        in_specs=[
            smem,
            smem,
            pl.BlockSpec(block, lambda i: (group(i), 0, 0)),
            pl.BlockSpec(block, lambda i: (i, 0, 0)),
            pl.BlockSpec(block, lambda i: (i, 0, 0)),
            pl.BlockSpec((RG, channels + EXTRA, segment), lambda i: (i, 0, 0)),
        ]
        + [pl.BlockSpec(memory_space=pl.ANY)] * len(given),
        out_specs=(
            pl.BlockSpec((channels, RG, segment), lambda i: (0, group(i), 0)),
            pl.BlockSpec((RG, segment), lambda i: (group(i), 0)),
        ),
        scratch_shapes=[
            pltpu.VMEM((RG, channels + EXTRA, segment), jnp.float32),
            pltpu.VMEM((segment, 2 * segment), jnp.float32),
            pltpu.VMEM((2, segment, 2 * segment), jnp.float32),
            pltpu.VMEM((RG, channels, segment), jnp.float32),
        ],
        input_output_aliases={6: 0, 7: 1} if given else {},
        compiler_params=pltpu.CompilerParams(vmem_limit_bytes=VMEM_LIMIT),
        cost_estimate=cost(own_groups),
    )(place, ranges, left, *pair, acc, *given)


def both_ways(pairs):
    return pairs + [(b, a) for a, b in pairs]


def program(images, first_weight, second_weight, search_ranges):
    row_count = lax.axis_size("rows")
    col_count = lax.axis_size("cols")
    col = lax.axis_index("cols")
    _, rows, segment = images.shape[1:]
    place = jnp.stack([lax.axis_index("rows"), col]).astype(jnp.int32)
    ranges = search_ranges.reshape(2, rows // RG)

    steps = min(col_count // 2 - 1, HOPS // 2)
    swap = [(i, i ^ 1) for i in range(col_count)]
    across = both_ways([(i, i + 1) for i in range(1, col_count - 1, 2)])
    hop = [(i, (i + 2) % col_count) for i in range(col_count)]
    last_hop = [(i, i + 2) for i in range(2 * (steps - 1), col_count - 2)]
    down = [(i, (i + 1) % row_count) for i in range(row_count)]
    up = [(b, a) for a, b in down]

    def exchanged(pieces, chunks):
        own = pack_edges(place, pieces, chunks, row_count)
        cross = lax.ppermute(own, "cols", across)
        partner = lax.ppermute(own, "cols", swap)
        return own, partner, cross

    def features(pieces, index, parts, count, offset, edges, base):
        return unit_features(
            place, pieces, index, parts, count, offset, edges, base,
            first_weight, second_weight, (row_count, col_count),
        )

    first_rows, last_rows = end_rows(images)
    above = lax.ppermute(last_rows, "rows", down)
    below = lax.ppermute(first_rows, "rows", up)
    mid = images.transpose(0, 2, 1, 3)

    strip = rows // 4
    inner = rows - 2 * strip
    around = (mid, above, below)
    edges_a = exchanged((mid,), ((1, ((inner, strip),)),))
    edges_r = exchanged(around, ((1, ((strip, 0), (strip, rows - strip))), (0, ((rows, 0),))))
    right_a = features((mid,), 1, 1, inner, strip - REACH, edges_a, 0)
    right_b = features(around, 1, 2, strip, 0, edges_r, 0)
    left = features(around, 0, 1, rows, 0, edges_r, 2 * edge_steps(strip, segment)[1])

    early = max(steps - 1, 1)

    def chain(mine):
        pairs = []
        for step in range(steps + 1):
            if step:
                mine = lax.ppermute(mine, "cols", hop if step < steps else last_hop)
            pairs.append((mine, lax.ppermute(mine, "cols", swap)))
        return pairs

    def totals(keys, inside):
        acc = correlate(place, ranges, left, keys[:early], None, 0, inside)
        if early == steps:
            return acc
        return correlate(place, ranges, left, keys[early:steps], acc, early, inside)

    keys_a, keys_b = chain(right_a), chain(right_b)
    acc_a, acc_b = totals(keys_a, True), totals(keys_b, False)
    outs = finish(place, ranges, left, keys_a[steps], acc_a, None, True, steps)
    return finish(place, ranges, left, keys_b[steps], acc_b, outs, False, steps)


def solution(mesh):
    placed = (P(None, None, "rows", "cols"), P(), P(), P(None, "rows", "cols"))
    return jax.shard_map(
        program,
        mesh=mesh,
        in_specs=placed,
        out_specs=(P(None, "rows", "cols"), P("rows", "cols")),
        check_vma=False,
    )
```

```python
import functools

import jax
import jax.numpy as jnp
from jax import lax
from jax.experimental import pallas as pl
from jax.experimental.pallas import tpu as pltpu
from jax.sharding import PartitionSpec as P


RG = 8
FIRST_DILATION = 2
SECOND_DILATION = 4
HOPS = 18
REACH = FIRST_DILATION + SECOND_DILATION
SLOT = 16

EXTRA = 16

sharpness_divisor = 10.0
epsilon = 1e-05
VMEM_LIMIT = 64 << 20
LOG2E = 1.4426950408889634


def lane_iota(shape):
    return lax.broadcasted_iota(jnp.int32, shape, len(shape) - 1)


def cost(microseconds):
    return pl.CostEstimate(
        flops=int(microseconds * 1e9), transcendentals=0, bytes_accessed=int(microseconds * 3e6)
    )


def cost(microseconds):
    return pl.CostEstimate(
        flops=int(microseconds * 1e9), transcendentals=0, bytes_accessed=int(microseconds * 3e6)
    )


def ends_kernel(low_ref, high_ref, first_ref, last_ref):
    first_ref[...] = jnp.swapaxes(low_ref[...], 0, 1)[:REACH]
    last_ref[...] = jnp.swapaxes(high_ref[...], 0, 1)[RG - REACH :]


def end_rows(images):
    count, channels, rows, segment = images.shape
    tile = (None, channels, RG, segment)
    ends = jax.ShapeDtypeStruct((count, REACH, channels, segment), jnp.bfloat16)
    ends_spec = pl.BlockSpec((None, REACH, channels, segment), lambda n: (n, 0, 0, 0))
    return pl.pallas_call(
        ends_kernel,
        out_shape=(ends, ends),
        grid=(count,),
        in_specs=[
            pl.BlockSpec(tile, lambda n: (n, 0, 0, 0)),
            pl.BlockSpec(tile, lambda n: (n, 0, rows // RG - 1, 0)),
        ],
        out_specs=(ends_spec, ends_spec),
        compiler_params=pltpu.CompilerParams(vmem_limit_bytes=VMEM_LIMIT),
        cost_estimate=cost(1),
    )(images, images)


def edge_steps(rows, segment):
    spacing = (rows + 2 * SECOND_DILATION) // (segment // SLOT)
    return spacing, spacing + 2 * FIRST_DILATION


def kept(piece, inside):
    return jnp.where(inside, piece, jnp.zeros_like(piece))


def pack_kernel(*refs, images, last_row):
    edge_ref = refs[-1]
    alone = len(refs) == 2
    place_ref = None if alone else refs[0]
    refs = refs[:-1] if alone else refs[1:-1]
    per_image = len(refs) // len(images)
    base = 0
    for n, chunks in enumerate(images):
        mid_ref = refs[n * per_image]
        around = refs[n * per_image + 1 : (n + 1) * per_image]
        rows, channels, segment = mid_ref.shape
        slot_of = lane_iota((channels, segment)) // SLOT

        def row_at(row):
            if row < 0:
                return kept(around[0][row + REACH], place_ref[0] > 0)
            if row >= rows:
                return kept(around[1][row - rows], place_ref[0] < last_row)
            return mid_ref[row]

        for count, first in chunks:
            spacing, steps = edge_steps(count, segment)
            for q in range(steps):
                packed = None
                for g in range(segment // SLOT):
                    shift = (SLOT * g + SLOT // 2) % segment
                    moved = pltpu.roll(row_at(first - REACH + g * spacing + q), shift, 1)
                    packed = moved if packed is None else jnp.where(slot_of == g, moved, packed)
                edge_ref[base + q] = packed
            base += steps


def whole(a):
    return pl.BlockSpec(a.shape, lambda i: (0,) * a.ndim)


def image_of(a, index):
    return pl.BlockSpec((None,) + a.shape[1:], lambda i: (index, 0, 0, 0))


def pack_edges(place, pieces, images, row_count):
    channels, segment = pieces[0].shape[2:]
    total = sum(edge_steps(count, segment)[1] for _, chunks in images for count, _ in chunks)
    given = () if len(pieces) == 1 else (place,)
    scalars = [pl.BlockSpec(memory_space=pltpu.SMEM)] * len(given)
    return pl.pallas_call(
        functools.partial(
            pack_kernel, images=tuple(chunks for _, chunks in images), last_row=row_count - 1
        ),
        out_shape=jax.ShapeDtypeStruct((total, channels, segment), jnp.bfloat16),
        grid=(1,),
        in_specs=scalars + [image_of(a, index) for index, _ in images for a in pieces],
        out_specs=pl.BlockSpec((total, channels, segment), lambda i: (0, 0, 0)),
        compiler_params=pltpu.CompilerParams(vmem_limit_bytes=VMEM_LIMIT),
        cost_estimate=cost(2),
    )(*given, *(list(pieces) * len(images)))


def feature_kernel(place_ref, *refs, spacing, offset, mesh_shape):
    (
        own_ref, partner_ref, cross_ref, w1_ref, w2_ref, unit_ref,
        w_ref, edge_ref, side_ref, p1_ref, p1e_ref, hid_ref, hide_ref, p2_ref, rhs0_ref, rhs1_ref, x_ref,
    ) = refs[-17:]
    part = pl.program_id(0)
    ends = len(refs) == 20
    mid_ref = refs[0]
    held, channels, segment = mid_ref.shape
    rows = unit_ref.shape[0]
    first_row, last_row = place_ref[0] == 0, place_ref[0] == mesh_shape[0] - 1
    first_col, last_col = place_ref[1] == 0, place_ref[1] == mesh_shape[1] - 1
    odd = place_ref[1] % 2 == 1
    above = first_row & (part == 0) & ends
    below = last_row & (part == pl.num_programs(0) - 1) & ends
    d1, d2 = FIRST_DILATION, SECOND_DILATION
    all_rows = rows + 2 * REACH
    hidden_rows = rows + 2 * d2
    steps = edge_ref.shape[0]
    groups = segment // SLOT
    lanes = lane_iota((channels, segment))
    in_slot = lanes % SLOT
    half = SLOT // 2
    rhs = (rhs0_ref, rhs1_ref)
    width = rhs0_ref.shape[1] // segment

    def stack(taps_ref):
        for a in range(3):
            for b in range(3):
                w_ref[a * channels : (a + 1) * channels, b * channels : (b + 1) * channels] = taps_ref[3 * a + b]

    for q in range(steps):
        own = own_ref[q]
        partner = partner_ref[q]
        cross = kept(cross_ref[q], ~(first_col | last_col))
        left = jnp.where(odd, partner, cross)
        right = jnp.where(odd, cross, partner)
        shift = half - REACH
        lower = pltpu.roll(jnp.where(in_slot < half, left, own), segment - shift, 1)
        upper = pltpu.roll(jnp.where(in_slot < half, own, right), shift, 1)
        edge_ref[q] = jnp.where(in_slot < half, lower, upper)
        side_ref[q] = pltpu.roll(jnp.where(in_slot < half, left, right), segment - shift, 1)

    def shifted(main, side, slot, amount):
        to_start = segment - REACH - slot * SLOT
        before = jnp.where(
            lanes < amount,
            pltpu.roll(side, lax.rem(to_start + amount, segment), 1),
            pltpu.roll(main, amount, 1),
        )
        after = jnp.where(
            lanes >= segment - amount,
            pltpu.roll(side, lax.rem(to_start + segment - amount, segment), 1),
            pltpu.roll(main, segment - amount, 1),
        )
        return before, after

    def put(target, j, main, before, after):
        lo = j * segment
        target[0:channels, lo : lo + segment] = before
        target[channels : 2 * channels, lo : lo + segment] = main
        target[2 * channels :, lo : lo + segment] = after

    def conv(source_ref, skip, sides_ref, product_ref, amount):
        def build(q, target):
            q = jnp.minimum(q, spacing - 1)
            side = sides_ref[q]
            for slot in range(groups):
                main = source_ref[slot * spacing + q + skip]
                put(target, slot, main, *shifted(main, side, slot, amount))

        def multiply_rows(q, source):
            product = jnp.dot(w_ref[...], source[...], preferred_element_type=jnp.float32)
            for slot in range(groups):
                product_ref[slot * spacing + q] = product[:, slot * segment : (slot + 1) * segment]

        build(0, rhs0_ref)

        def body(u, _):
            build(2 * u + 1, rhs1_ref)
            multiply_rows(2 * u, rhs0_ref)
            build(2 * u + 2, rhs0_ref)
            multiply_rows(2 * u + 1, rhs1_ref)
            return 0

        lax.fori_loop(0, spacing // 2, body, 0)
        if spacing % 2:
            multiply_rows(spacing - 1, rhs0_ref)

    if ends:
        top = kept(refs[1][...], ~first_row)
        bottom = kept(refs[2][...], ~last_row)
        if rows == held:
            x_ref[0:REACH] = top
            x_ref[REACH : REACH + rows] = mid_ref[...]
            x_ref[REACH + rows :] = bottom
        else:

            @pl.when(part == 0)
            def _():
                x_ref[0:REACH] = top
                x_ref[REACH:] = mid_ref[: rows + REACH]

            @pl.when(part == 1)
            def _():
                x_ref[: rows + REACH] = mid_ref[held - rows - REACH :]
                x_ref[rows + REACH :] = bottom

    else:
        x_ref = mid_ref

    stack(w1_ref)
    conv(x_ref, offset, side_ref, p1_ref, d1)

    pending = [
        (p1_ref, row, x_ref[row + offset], groups - 1, row - (groups - 1) * spacing)
        for row in range(groups * spacing, all_rows)
    ]
    pending += [(p1e_ref, q, edge_ref[q], None, None) for q in range(steps)]
    for t in range(pl.cdiv(len(pending), width)):
        target = rhs[t % 2]
        batch = pending[t * width : (t + 1) * width]
        for j, (_, _, main, slot, q) in enumerate(batch):
            if slot is None:
                moved = pltpu.roll(main, d1, 1), pltpu.roll(main, segment - d1, 1)
            else:
                moved = shifted(main, side_ref[q], slot, d1)
            put(target, j, main, *moved)
        product = jnp.dot(
            w_ref[...], target[:, : len(batch) * segment], preferred_element_type=jnp.float32
        )
        for j, (product_ref, row, _, _, _) in enumerate(batch):
            product_ref[row] = product[:, j * segment : (j + 1) * segment]

    def three(product_ref, row, apart):
        return (
            product_ref[row, 0:channels]
            + product_ref[row + apart, channels : 2 * channels]
            + product_ref[row + 2 * apart, 2 * channels :]
        )

    def silu(v):
        return v / (1.0 + jnp.exp(-v))

    def hidden(t, _):
        for j in range(8):
            row = 8 * t + j
            outside = ((row < d2) & above) | ((row >= d2 + rows) & below)
            value = silu(three(p1_ref, row, d1))
            hid_ref[row] = jnp.where(outside, 0.0, value).astype(jnp.bfloat16)
        return 0

    lax.fori_loop(0, hidden_rows // 8, hidden, 0)

    left_out = (in_slot < REACH) & first_col
    right_out = (in_slot >= half + 2) & last_col
    for q in range(spacing):
        row = (lanes // SLOT) * spacing + q
        outside = ((row < d2) & above) | ((row >= d2 + rows) & below) | left_out | right_out
        value = silu(three(p1e_ref, q, d1))
        value = jnp.where(outside, 0.0, value).astype(jnp.bfloat16)
        gap = half + 2 - REACH
        hide_ref[q] = jnp.where(in_slot < REACH, value, pltpu.roll(value, segment - gap, 1))

    stack(w2_ref)
    conv(hid_ref, 0, hide_ref, p2_ref, d2)

    def finish(t, _):
        for j in range(8):
            row = 8 * t + j
            total = x_ref[row + offset + REACH].astype(jnp.float32) + three(p2_ref, row, d2)
            feature = total.astype(jnp.bfloat16).astype(jnp.float32)
            mean = jnp.sum(feature * feature, axis=0, keepdims=True) * (1.0 / channels)
            unit_ref[row] = (feature * lax.rsqrt(mean + epsilon)).astype(jnp.bfloat16)
        return 0

    lax.fori_loop(0, rows // 8, finish, 0)


def unit_features(place, pieces, index, parts, rows, offset, edges, base, w1, w2, mesh_shape):
    channels, segment = pieces[0].shape[2:]
    all_rows = rows + 2 * REACH
    hidden_rows = rows + 2 * SECOND_DILATION
    spacing, steps = edge_steps(rows, segment)
    width = segment // SLOT
    products = (3 * channels, segment)
    assembled = all_rows if len(pieces) == 3 else 1
    return pl.pallas_call(
        functools.partial(feature_kernel, spacing=spacing, offset=offset, mesh_shape=mesh_shape),
        out_shape=jax.ShapeDtypeStruct((parts * rows, channels, segment), jnp.bfloat16),
        grid=(parts,),
        in_specs=[pl.BlockSpec(memory_space=pltpu.SMEM)]
        + [image_of(a, index) for a in pieces]
        + [
            pl.BlockSpec(
                (pl.Element(steps), pl.Element(channels), pl.Element(segment)),
                lambda i: (base + i * steps, 0, 0),
            )
            for _ in edges
        ]
        + [whole(w1), whole(w2)],
        out_specs=pl.BlockSpec((rows, channels, segment), lambda i: (i, 0, 0)),
        scratch_shapes=[
            pltpu.VMEM((3 * channels, 3 * channels), jnp.bfloat16),
            pltpu.VMEM((steps, channels, segment), jnp.bfloat16),
            pltpu.VMEM((steps, channels, segment), jnp.bfloat16),
            pltpu.VMEM((all_rows,) + products, jnp.float32),
            pltpu.VMEM((steps,) + products, jnp.float32),
            pltpu.VMEM((hidden_rows, channels, segment), jnp.bfloat16),
            pltpu.VMEM((spacing, channels, segment), jnp.bfloat16),
            pltpu.VMEM((hidden_rows,) + products, jnp.float32),
            pltpu.VMEM((3 * channels, width * segment), jnp.bfloat16),
            pltpu.VMEM((3 * channels, width * segment), jnp.bfloat16),
            pltpu.VMEM((assembled, channels, segment), jnp.bfloat16),
        ],
        compiler_params=pltpu.CompilerParams(vmem_limit_bytes=VMEM_LIMIT),
        cost_estimate=cost(parts * rows * 0.2),
    )(place, *pieces, *edges, w1, w2)


def add_step(place_ref, range_ref, group, step, left_ref, mine_ref, theirs_ref, acc_ref, bias_ref, scores_ref):
    _, channels, segment = left_ref.shape
    block = place_ref[1]
    low = segment * range_ref[0, group]
    high = low + segment * range_ref[1, group]
    odd = block % 2
    base = segment * (block - 2 * (block // 2 - step))
    active = (base + segment - 1 >= low) & (base - 2 * segment + 1 < high) & (block // 2 >= step)
    scale = sharpness_divisor / channels * LOG2E

    def key_column(shape):
        column = lane_iota(shape)
        own = column < segment
        return column % segment + segment * jnp.where(own, odd, 1 - odd)

    @pl.when(active)
    def _():
        wide = (segment, 2 * segment)
        offsets = base + lax.broadcasted_iota(jnp.int32, wide, 0) - key_column(wide)
        inside = (offsets >= low) & (offsets < high)
        bias_ref[...] = jnp.where(inside, 0.0, -1e30)
        kind = lax.broadcasted_iota(jnp.int32, (EXTRA, 2 * segment), 0)
        column = key_column((EXTRA, 2 * segment))
        extra = jnp.where(kind == 0, 1, jnp.where(kind == 1, column, jnp.where(kind == 2, step, 0)))
        extra = extra.astype(jnp.float32).astype(jnp.bfloat16)
        rows = left_ref.shape[0]

        def score(r):
            keys = jnp.concatenate([mine_ref[r], theirs_ref[r]], axis=1)
            scores_ref[r % 2] = lax.dot_general(
                left_ref[r], keys, (((0,), (0,)), ((), ())), preferred_element_type=jnp.float32
            )

        score(0)
        for r in range(rows):
            if r + 1 < rows:
                score(r + 1)
            weights = jnp.exp2(scores_ref[r % 2] * scale + bias_ref[...]).astype(jnp.bfloat16)
            keys = jnp.concatenate([mine_ref[r], theirs_ref[r]], axis=1)
            extended = jnp.concatenate([keys, extra], axis=0)
            acc_ref[r] += lax.dot_general(
                extended, weights, (((1,), (1,)), ((), ())), preferred_element_type=jnp.float32
            )


def group_of(i, inner, groups):
    quarter = groups // 4
    return i + quarter if inner else jnp.where(i < quarter, i, i + 2 * quarter)


def gather_kernel(place_ref, range_ref, left_ref, *refs, inner, groups, start, count):
    keys, (acc_ref, bias_ref, scores_ref) = refs[: 2 * count], refs[-3:]
    group = group_of(pl.program_id(0), inner, groups)
    acc_ref[...] = refs[2 * count][...] if start else jnp.zeros_like(acc_ref)
    for index in range(count):
        add_step(
            place_ref, range_ref, group, start + index, left_ref, keys[2 * index], keys[2 * index + 1],
            acc_ref, bias_ref, scores_ref,
        )


def finish_kernel(
    place_ref, range_ref, left_ref, mine_ref, theirs_ref, acc_in_ref, *refs, inner, groups, step
):
    matched_ref, disparity_ref, acc_ref, bias_ref, scores_ref, rows_ref = refs[-6:]
    group = group_of(pl.program_id(0), inner, groups)
    rows, channels, segment = left_ref.shape
    acc_ref[...] = acc_in_ref[...]
    add_step(
        place_ref, range_ref, group, step, left_ref, mine_ref, theirs_ref, acc_ref, bias_ref, scores_ref
    )
    block = place_ref[1]
    low = segment * range_ref[0, group]
    high = low + segment * range_ref[1, group]
    x = block * segment + lane_iota((1, segment))
    from_chip = (x - 2 * segment * (block // 2)).astype(jnp.float32)
    start = jnp.maximum(low, x + 1)
    beyond = jnp.maximum(high - start, 0)
    beyond_sum = ((start + high - 1) * beyond).astype(jnp.float32) * 0.5
    beyond = beyond.astype(jnp.float32)
    for r in range(rows):
        turned = acc_ref[r]
        near = turned[channels : channels + 1]
        column = turned[channels + 1 : channels + 2]
        passed = turned[channels + 2 : channels + 3]
        inverse = 1.0 / (near + beyond)
        shift = from_chip * near - column + (2 * segment) * passed + beyond_sum
        rows_ref[r] = turned[:channels] * inverse
        disparity_ref[r : r + 1, :] = shift * inverse * (1.0 / segment)
    matched_ref[...] = jnp.swapaxes(rows_ref[...].astype(jnp.bfloat16), 0, 1)


def correlate(place, ranges, left, keys, acc, start, inner):
    rows, channels, segment = left.shape
    groups = rows // RG
    own_groups = keys[0][0].shape[0] // RG
    block = (RG, channels, segment)
    smem = pl.BlockSpec(memory_space=pltpu.SMEM)
    held = channels + EXTRA
    acc_spec = pl.BlockSpec((RG, held, segment), lambda i: (i, 0, 0))
    given = (acc,) if start else ()
    return pl.pallas_call(
        functools.partial(gather_kernel, inner=inner, groups=groups, start=start, count=len(keys)),
        out_shape=jax.ShapeDtypeStruct((own_groups * RG, held, segment), jnp.float32),
        grid=(own_groups,),
        in_specs=[smem, smem, pl.BlockSpec(block, lambda i: (group_of(i, inner, groups), 0, 0))]
        + [pl.BlockSpec(block, lambda i: (i, 0, 0))] * (2 * len(keys))
        + [acc_spec] * len(given),
        out_specs=acc_spec,
        scratch_shapes=[
            pltpu.VMEM((segment, 2 * segment), jnp.float32),
            pltpu.VMEM((2, segment, 2 * segment), jnp.float32),
        ],
        input_output_aliases={3 + 2 * len(keys): 0} if given else {},
        compiler_params=pltpu.CompilerParams(vmem_limit_bytes=VMEM_LIMIT),
        cost_estimate=cost(1.5 * own_groups),
    )(place, ranges, left, *[a for pair in keys for a in pair], *given)


def finish(place, ranges, left, pair, acc, outs, inner, step):
    rows, channels, segment = left.shape
    groups = rows // RG
    own_groups = pair[0].shape[0] // RG
    block = (RG, channels, segment)
    smem = pl.BlockSpec(memory_space=pltpu.SMEM)

    def group(i):
        return group_of(i, inner, groups)

    given = () if outs is None else tuple(outs)
    return pl.pallas_call(
        functools.partial(finish_kernel, inner=inner, groups=groups, step=step),
        out_shape=(
            jax.ShapeDtypeStruct((channels, rows, segment), jnp.bfloat16),
            jax.ShapeDtypeStruct((rows, segment), jnp.float32),
        ),
        grid=(own_groups,),
        in_specs=[
            smem,
            smem,
            pl.BlockSpec(block, lambda i: (group(i), 0, 0)),
            pl.BlockSpec(block, lambda i: (i, 0, 0)),
            pl.BlockSpec(block, lambda i: (i, 0, 0)),
            pl.BlockSpec((RG, channels + EXTRA, segment), lambda i: (i, 0, 0)),
        ]
        + [pl.BlockSpec(memory_space=pl.ANY)] * len(given),
        out_specs=(
            pl.BlockSpec((channels, RG, segment), lambda i: (0, group(i), 0)),
            pl.BlockSpec((RG, segment), lambda i: (group(i), 0)),
        ),
        scratch_shapes=[
            pltpu.VMEM((RG, channels + EXTRA, segment), jnp.float32),
            pltpu.VMEM((segment, 2 * segment), jnp.float32),
            pltpu.VMEM((2, segment, 2 * segment), jnp.float32),
            pltpu.VMEM((RG, channels, segment), jnp.float32),
        ],
        input_output_aliases={6: 0, 7: 1} if given else {},
        compiler_params=pltpu.CompilerParams(vmem_limit_bytes=VMEM_LIMIT),
        cost_estimate=cost(own_groups),
    )(place, ranges, left, *pair, acc, *given)


def both_ways(pairs):
    return pairs + [(b, a) for a, b in pairs]


def program(images, first_weight, second_weight, search_ranges):
    row_count = lax.axis_size("rows")
    col_count = lax.axis_size("cols")
    col = lax.axis_index("cols")
    _, rows, segment = images.shape[1:]
    place = jnp.stack([lax.axis_index("rows"), col]).astype(jnp.int32)
    ranges = search_ranges.reshape(2, rows // RG)

    steps = min(col_count // 2 - 1, HOPS // 2)
    swap = [(i, i ^ 1) for i in range(col_count)]
    across = both_ways([(i, i + 1) for i in range(1, col_count - 1, 2)])
    around_across = across + both_ways([(0, col_count - 1)])
    hop = [(i, (i + 2) % col_count) for i in range(col_count)]
    last_hop = [(i, i + 2) for i in range(2 * (steps - 1), col_count - 2)]
    down = [(i, (i + 1) % row_count) for i in range(row_count)]
    up = [(b, a) for a, b in down]

    def exchanged(pieces, chunks, pairs):
        own = pack_edges(place, pieces, chunks, row_count)
        cross = lax.ppermute(own, "cols", pairs)
        partner = lax.ppermute(own, "cols", swap)
        return own, partner, cross

    def features(pieces, index, parts, count, offset, edges, base):
        return unit_features(
            place, pieces, index, parts, count, offset, edges, base,
            first_weight, second_weight, (row_count, col_count),
        )

    first_rows, last_rows = end_rows(images)
    above = lax.ppermute(last_rows, "rows", down)
    below = lax.ppermute(first_rows, "rows", up)
    mid = images.transpose(0, 2, 1, 3)

    strip = rows // 4
    inner = rows - 2 * strip
    around = (mid, above, below)
    edges_a = exchanged((mid,), ((1, ((inner, strip),)),), around_across)
    chunks_r = (1, ((strip, 0), (strip, rows - strip))), (0, ((rows, 0),))
    edges_r = exchanged(around, chunks_r, across)
    right_a = features((mid,), 1, 1, inner, strip - REACH, edges_a, 0)
    right_b = features(around, 1, 2, strip, 0, edges_r, 0)
    left = features(around, 0, 1, rows, 0, edges_r, 2 * edge_steps(strip, segment)[1])

    early = max(steps - 1, 1)

    def chain(mine):
        pairs = []
        for step in range(steps + 1):
            if step:
                mine = lax.ppermute(mine, "cols", hop if step < steps else last_hop)
            pairs.append((mine, lax.ppermute(mine, "cols", swap)))
        return pairs

    def totals(keys, inside):
        acc = correlate(place, ranges, left, keys[:early], None, 0, inside)
        if early == steps:
            return acc
        return correlate(place, ranges, left, keys[early:steps], acc, early, inside)

    keys_a, keys_b = chain(right_a), chain(right_b)
    acc_a, acc_b = totals(keys_a, True), totals(keys_b, False)
    outs = finish(place, ranges, left, keys_a[steps], acc_a, None, True, steps)
    return finish(place, ranges, left, keys_b[steps], acc_b, outs, False, steps)


def solution(mesh):
    placed = (P(None, None, "rows", "cols"), P(), P(), P(None, "rows", "cols"))
    return jax.shard_map(
        program,
        mesh=mesh,
        in_specs=placed,
        out_specs=(P(None, "rows", "cols"), P("rows", "cols")),
        check_vma=False,
    )
```

```python
import functools

import jax
import jax.numpy as jnp
from jax import lax
from jax.experimental import pallas as pl
from jax.experimental.pallas import tpu as pltpu
from jax.sharding import PartitionSpec as P


RG = 8
FIRST_DILATION = 2
SECOND_DILATION = 4
HOPS = 18
REACH = FIRST_DILATION + SECOND_DILATION
SLOT = 16

EXTRA = 16

sharpness_divisor = 10.0
epsilon = 1e-05
VMEM_LIMIT = 64 << 20
LOG2E = 1.4426950408889634


def lane_iota(shape):
    return lax.broadcasted_iota(jnp.int32, shape, len(shape) - 1)


def cost(microseconds):
    return pl.CostEstimate(
        flops=int(microseconds * 1e9), transcendentals=0, bytes_accessed=int(microseconds * 3e6)
    )


def cost(microseconds):
    return pl.CostEstimate(
        flops=int(microseconds * 1e9), transcendentals=0, bytes_accessed=int(microseconds * 3e6)
    )


def ends_kernel(low_ref, high_ref, first_ref, last_ref):
    first_ref[...] = jnp.swapaxes(low_ref[...], 0, 1)[:REACH]
    last_ref[...] = jnp.swapaxes(high_ref[...], 0, 1)[RG - REACH :]


def end_rows(images):
    count, channels, rows, segment = images.shape
    tile = (None, channels, RG, segment)
    ends = jax.ShapeDtypeStruct((count, REACH, channels, segment), jnp.bfloat16)
    ends_spec = pl.BlockSpec((None, REACH, channels, segment), lambda n: (n, 0, 0, 0))
    return pl.pallas_call(
        ends_kernel,
        out_shape=(ends, ends),
        grid=(count,),
        in_specs=[
            pl.BlockSpec(tile, lambda n: (n, 0, 0, 0)),
            pl.BlockSpec(tile, lambda n: (n, 0, rows // RG - 1, 0)),
        ],
        out_specs=(ends_spec, ends_spec),
        compiler_params=pltpu.CompilerParams(vmem_limit_bytes=VMEM_LIMIT),
        cost_estimate=cost(1),
    )(images, images)


def edge_steps(rows, segment):
    spacing = (rows + 2 * SECOND_DILATION) // (segment // SLOT)
    return spacing, spacing + 2 * FIRST_DILATION


def kept(piece, inside):
    return jnp.where(inside, piece, jnp.zeros_like(piece))


def pack_kernel(*refs, images, last_row):
    edge_ref = refs[-1]
    alone = len(refs) == 2
    place_ref = None if alone else refs[0]
    refs = refs[:-1] if alone else refs[1:-1]
    per_image = len(refs) // len(images)
    base = 0
    for n, chunks in enumerate(images):
        mid_ref = refs[n * per_image]
        around = refs[n * per_image + 1 : (n + 1) * per_image]
        rows, channels, segment = mid_ref.shape
        slot_of = lane_iota((channels, segment)) // SLOT

        def row_at(row):
            if row < 0:
                return kept(around[0][row + REACH], place_ref[0] > 0)
            if row >= rows:
                return kept(around[1][row - rows], place_ref[0] < last_row)
            return mid_ref[row]

        for count, first in chunks:
            spacing, steps = edge_steps(count, segment)
            for q in range(steps):
                packed = None
                for g in range(segment // SLOT):
                    shift = (SLOT * g + SLOT // 2) % segment
                    moved = pltpu.roll(row_at(first - REACH + g * spacing + q), shift, 1)
                    packed = moved if packed is None else jnp.where(slot_of == g, moved, packed)
                edge_ref[base + q] = packed
            base += steps


def whole(a):
    return pl.BlockSpec(a.shape, lambda i: (0,) * a.ndim)


def image_of(a, index):
    return pl.BlockSpec((None,) + a.shape[1:], lambda i: (index, 0, 0, 0))


def pack_edges(place, pieces, images, row_count):
    channels, segment = pieces[0].shape[2:]
    total = sum(edge_steps(count, segment)[1] for _, chunks in images for count, _ in chunks)
    given = () if len(pieces) == 1 else (place,)
    scalars = [pl.BlockSpec(memory_space=pltpu.SMEM)] * len(given)
    return pl.pallas_call(
        functools.partial(
            pack_kernel, images=tuple(chunks for _, chunks in images), last_row=row_count - 1
        ),
        out_shape=jax.ShapeDtypeStruct((total, channels, segment), jnp.bfloat16),
        grid=(1,),
        in_specs=scalars + [image_of(a, index) for index, _ in images for a in pieces],
        out_specs=pl.BlockSpec((total, channels, segment), lambda i: (0, 0, 0)),
        compiler_params=pltpu.CompilerParams(vmem_limit_bytes=VMEM_LIMIT),
        cost_estimate=cost(2),
    )(*given, *(list(pieces) * len(images)))


def feature_kernel(place_ref, *refs, spacing, offset, mesh_shape):
    (
        own_ref, partner_ref, cross_ref, w1_ref, w2_ref, unit_ref,
        w_ref, edge_ref, side_ref, p1_ref, p1e_ref, hid_ref, hide_ref, p2_ref, rhs0_ref, rhs1_ref, x_ref,
    ) = refs[-17:]
    part = pl.program_id(0)
    ends = len(refs) == 20
    mid_ref = refs[0]
    held, channels, segment = mid_ref.shape
    rows = unit_ref.shape[0]
    first_row, last_row = place_ref[0] == 0, place_ref[0] == mesh_shape[0] - 1
    first_col, last_col = place_ref[1] == 0, place_ref[1] == mesh_shape[1] - 1
    odd = place_ref[1] % 2 == 1
    above = first_row & (part == 0) & ends
    below = last_row & (part == pl.num_programs(0) - 1) & ends
    d1, d2 = FIRST_DILATION, SECOND_DILATION
    all_rows = rows + 2 * REACH
    hidden_rows = rows + 2 * d2
    steps = edge_ref.shape[0]
    groups = segment // SLOT
    lanes = lane_iota((channels, segment))
    in_slot = lanes % SLOT
    half = SLOT // 2
    rhs = (rhs0_ref, rhs1_ref)
    width = rhs0_ref.shape[1] // segment

    def stack(taps_ref):
        for a in range(3):
            for b in range(3):
                w_ref[a * channels : (a + 1) * channels, b * channels : (b + 1) * channels] = taps_ref[3 * a + b]

    for q in range(steps):
        own = own_ref[q]
        partner = partner_ref[q]
        cross = kept(cross_ref[q], ~(first_col | last_col))
        left = jnp.where(odd, partner, cross)
        right = jnp.where(odd, cross, partner)
        shift = half - REACH
        lower = pltpu.roll(jnp.where(in_slot < half, left, own), segment - shift, 1)
        upper = pltpu.roll(jnp.where(in_slot < half, own, right), shift, 1)
        edge_ref[q] = jnp.where(in_slot < half, lower, upper)
        side_ref[q] = pltpu.roll(jnp.where(in_slot < half, left, right), segment - shift, 1)

    def shifted(main, side, slot, amount):
        to_start = segment - REACH - slot * SLOT
        before = jnp.where(
            lanes < amount,
            pltpu.roll(side, lax.rem(to_start + amount, segment), 1),
            pltpu.roll(main, amount, 1),
        )
        after = jnp.where(
            lanes >= segment - amount,
            pltpu.roll(side, lax.rem(to_start + segment - amount, segment), 1),
            pltpu.roll(main, segment - amount, 1),
        )
        return before, after

    def put(target, j, main, before, after):
        lo = j * segment
        target[0:channels, lo : lo + segment] = before
        target[channels : 2 * channels, lo : lo + segment] = main
        target[2 * channels :, lo : lo + segment] = after

    def conv(source_ref, skip, sides_ref, product_ref, amount):
        def build(q, target):
            q = jnp.minimum(q, spacing - 1)
            side = sides_ref[q]
            for slot in range(groups):
                main = source_ref[slot * spacing + q + skip]
                put(target, slot, main, *shifted(main, side, slot, amount))

        def multiply_rows(q, source):
            product = jnp.dot(w_ref[...], source[...], preferred_element_type=jnp.float32)
            for slot in range(groups):
                product_ref[slot * spacing + q] = product[:, slot * segment : (slot + 1) * segment]

        build(0, rhs0_ref)

        def body(u, _):
            build(2 * u + 1, rhs1_ref)
            multiply_rows(2 * u, rhs0_ref)
            build(2 * u + 2, rhs0_ref)
            multiply_rows(2 * u + 1, rhs1_ref)
            return 0

        lax.fori_loop(0, spacing // 2, body, 0)
        if spacing % 2:
            multiply_rows(spacing - 1, rhs0_ref)

    if ends:
        top = kept(refs[1][...], ~first_row)
        bottom = kept(refs[2][...], ~last_row)
        if rows == held:
            x_ref[0:REACH] = top
            x_ref[REACH : REACH + rows] = mid_ref[...]
            x_ref[REACH + rows :] = bottom
        else:

            @pl.when(part == 0)
            def _():
                x_ref[0:REACH] = top
                x_ref[REACH:] = mid_ref[: rows + REACH]

            @pl.when(part == 1)
            def _():
                x_ref[: rows + REACH] = mid_ref[held - rows - REACH :]
                x_ref[rows + REACH :] = bottom

    else:
        x_ref = mid_ref

    stack(w1_ref)
    conv(x_ref, offset, side_ref, p1_ref, d1)

    pending = [
        (p1_ref, row, x_ref[row + offset], groups - 1, row - (groups - 1) * spacing)
        for row in range(groups * spacing, all_rows)
    ]
    pending += [(p1e_ref, q, edge_ref[q], None, None) for q in range(steps)]
    for t in range(pl.cdiv(len(pending), width)):
        target = rhs[t % 2]
        batch = pending[t * width : (t + 1) * width]
        for j, (_, _, main, slot, q) in enumerate(batch):
            if slot is None:
                moved = pltpu.roll(main, d1, 1), pltpu.roll(main, segment - d1, 1)
            else:
                moved = shifted(main, side_ref[q], slot, d1)
            put(target, j, main, *moved)
        product = jnp.dot(
            w_ref[...], target[:, : len(batch) * segment], preferred_element_type=jnp.float32
        )
        for j, (product_ref, row, _, _, _) in enumerate(batch):
            product_ref[row] = product[:, j * segment : (j + 1) * segment]

    def three(product_ref, row, apart):
        return (
            product_ref[row, 0:channels]
            + product_ref[row + apart, channels : 2 * channels]
            + product_ref[row + 2 * apart, 2 * channels :]
        )

    def silu(v):
        return v / (1.0 + jnp.exp(-v))

    def hidden(t, _):
        for j in range(8):
            row = 8 * t + j
            outside = ((row < d2) & above) | ((row >= d2 + rows) & below)
            value = silu(three(p1_ref, row, d1))
            hid_ref[row] = jnp.where(outside, 0.0, value).astype(jnp.bfloat16)
        return 0

    lax.fori_loop(0, hidden_rows // 8, hidden, 0)

    left_out = (in_slot < REACH) & first_col
    right_out = (in_slot >= half + 2) & last_col
    for q in range(spacing):
        row = (lanes // SLOT) * spacing + q
        outside = ((row < d2) & above) | ((row >= d2 + rows) & below) | left_out | right_out
        value = silu(three(p1e_ref, q, d1))
        value = jnp.where(outside, 0.0, value).astype(jnp.bfloat16)
        gap = half + 2 - REACH
        hide_ref[q] = jnp.where(in_slot < REACH, value, pltpu.roll(value, segment - gap, 1))

    stack(w2_ref)
    conv(hid_ref, 0, hide_ref, p2_ref, d2)

    def finish(t, _):
        for j in range(8):
            row = 8 * t + j
            total = x_ref[row + offset + REACH].astype(jnp.float32) + three(p2_ref, row, d2)
            feature = total.astype(jnp.bfloat16).astype(jnp.float32)
            mean = jnp.sum(feature * feature, axis=0, keepdims=True) * (1.0 / channels)
            unit_ref[row] = (feature * lax.rsqrt(mean + epsilon)).astype(jnp.bfloat16)
        return 0

    lax.fori_loop(0, rows // 8, finish, 0)


def unit_features(place, pieces, index, parts, rows, offset, edges, base, w1, w2, mesh_shape):
    channels, segment = pieces[0].shape[2:]
    all_rows = rows + 2 * REACH
    hidden_rows = rows + 2 * SECOND_DILATION
    spacing, steps = edge_steps(rows, segment)
    width = segment // SLOT
    products = (3 * channels, segment)
    assembled = all_rows if len(pieces) == 3 else 1
    return pl.pallas_call(
        functools.partial(feature_kernel, spacing=spacing, offset=offset, mesh_shape=mesh_shape),
        out_shape=jax.ShapeDtypeStruct((parts * rows, channels, segment), jnp.bfloat16),
        grid=(parts,),
        in_specs=[pl.BlockSpec(memory_space=pltpu.SMEM)]
        + [image_of(a, index) for a in pieces]
        + [
            pl.BlockSpec(
                (pl.Element(steps), pl.Element(channels), pl.Element(segment)),
                lambda i: (base + i * steps, 0, 0),
            )
            for _ in edges
        ]
        + [whole(w1), whole(w2)],
        out_specs=pl.BlockSpec((rows, channels, segment), lambda i: (i, 0, 0)),
        scratch_shapes=[
            pltpu.VMEM((3 * channels, 3 * channels), jnp.bfloat16),
            pltpu.VMEM((steps, channels, segment), jnp.bfloat16),
            pltpu.VMEM((steps, channels, segment), jnp.bfloat16),
            pltpu.VMEM((all_rows,) + products, jnp.float32),
            pltpu.VMEM((steps,) + products, jnp.float32),
            pltpu.VMEM((hidden_rows, channels, segment), jnp.bfloat16),
            pltpu.VMEM((spacing, channels, segment), jnp.bfloat16),
            pltpu.VMEM((hidden_rows,) + products, jnp.float32),
            pltpu.VMEM((3 * channels, width * segment), jnp.bfloat16),
            pltpu.VMEM((3 * channels, width * segment), jnp.bfloat16),
            pltpu.VMEM((assembled, channels, segment), jnp.bfloat16),
        ],
        compiler_params=pltpu.CompilerParams(vmem_limit_bytes=VMEM_LIMIT),
        cost_estimate=cost(parts * rows * 0.2),
    )(place, *pieces, *edges, w1, w2)


def add_step(place_ref, range_ref, group, step, left_ref, key_refs, acc_ref, bias_ref, scores_ref, which=None):
    _, channels, segment = left_ref.shape
    block = place_ref[1]
    low = segment * range_ref[0, group]
    high = low + segment * range_ref[1, group]
    odd = block % 2
    base = segment * (block - 2 * (block // 2 - step))
    active = (base + segment - 1 >= low) & (base - 2 * segment + 1 < high) & (block // 2 >= step)
    scale = sharpness_divisor / channels * LOG2E

    def key_column(shape):
        column = lane_iota(shape)
        own = column < segment if which is None else which == "mine"
        return column % segment + segment * jnp.where(own, odd, 1 - odd)

    width = len(key_refs) * segment

    @pl.when(active)
    def _():
        wide = (segment, width)
        offsets = base + lax.broadcasted_iota(jnp.int32, wide, 0) - key_column(wide)
        inside = (offsets >= low) & (offsets < high)
        bias_ref[:, :width] = jnp.where(inside, 0.0, -1e30)
        kind = lax.broadcasted_iota(jnp.int32, (EXTRA, width), 0)
        column = key_column((EXTRA, width))
        extra = jnp.where(kind == 0, 1, jnp.where(kind == 1, column, jnp.where(kind == 2, step, 0)))
        extra = extra.astype(jnp.float32).astype(jnp.bfloat16)
        rows = left_ref.shape[0]

        def score(r):
            keys = jnp.concatenate([ref[r] for ref in key_refs], axis=1)
            scores_ref[r % 2, :, :width] = lax.dot_general(
                left_ref[r], keys, (((0,), (0,)), ((), ())), preferred_element_type=jnp.float32
            )

        score(0)
        for r in range(rows):
            if r + 1 < rows:
                score(r + 1)
            weights = jnp.exp2(scores_ref[r % 2, :, :width] * scale + bias_ref[:, :width]).astype(jnp.bfloat16)
            keys = jnp.concatenate([ref[r] for ref in key_refs], axis=1)
            extended = jnp.concatenate([keys, extra], axis=0)
            acc_ref[r] += lax.dot_general(
                extended, weights, (((1,), (1,)), ((), ())), preferred_element_type=jnp.float32
            )


def group_of(i, inner, groups):
    quarter = groups // 4
    return i + quarter if inner else jnp.where(i < quarter, i, i + 2 * quarter)


def gather_kernel(place_ref, range_ref, left_ref, *refs, inner, groups, start, per_step, which):
    acc_ref, bias_ref, scores_ref = refs[-3:]
    keys = refs[: -4 if start else -3]
    group = group_of(pl.program_id(0), inner, groups)
    acc_ref[...] = refs[-4][...] if start else jnp.zeros_like(acc_ref)
    for index in range(len(keys) // per_step):
        add_step(
            place_ref, range_ref, group, start + index, left_ref,
            keys[per_step * index : per_step * (index + 1)], acc_ref, bias_ref, scores_ref, which,
        )


def finish_kernel(place_ref, range_ref, left_ref, *refs, inner, groups, step, per_step, which):
    keys, acc_in_ref = refs[:per_step], refs[per_step]
    matched_ref, disparity_ref, acc_ref, bias_ref, scores_ref, rows_ref = refs[-6:]
    group = group_of(pl.program_id(0), inner, groups)
    rows, channels, segment = left_ref.shape
    acc_ref[...] = acc_in_ref[...]
    add_step(
        place_ref, range_ref, group, step, left_ref, keys, acc_ref, bias_ref, scores_ref, which
    )
    block = place_ref[1]
    low = segment * range_ref[0, group]
    high = low + segment * range_ref[1, group]
    x = block * segment + lane_iota((1, segment))
    from_chip = (x - 2 * segment * (block // 2)).astype(jnp.float32)
    start = jnp.maximum(low, x + 1)
    beyond = jnp.maximum(high - start, 0)
    beyond_sum = ((start + high - 1) * beyond).astype(jnp.float32) * 0.5
    beyond = beyond.astype(jnp.float32)
    for r in range(rows):
        turned = acc_ref[r]
        near = turned[channels : channels + 1]
        column = turned[channels + 1 : channels + 2]
        passed = turned[channels + 2 : channels + 3]
        inverse = 1.0 / (near + beyond)
        shift = from_chip * near - column + (2 * segment) * passed + beyond_sum
        rows_ref[r] = turned[:channels] * inverse
        disparity_ref[r : r + 1, :] = shift * inverse * (1.0 / segment)
    matched_ref[...] = jnp.swapaxes(rows_ref[...].astype(jnp.bfloat16), 0, 1)


def correlate(place, ranges, left, keys, acc, start, inner, which=None):
    rows, channels, segment = left.shape
    groups = rows // RG
    own_groups = keys[0][0].shape[0] // RG
    block = (RG, channels, segment)
    smem = pl.BlockSpec(memory_space=pltpu.SMEM)
    held = channels + EXTRA
    acc_spec = pl.BlockSpec((RG, held, segment), lambda i: (i, 0, 0))
    given = (acc,) if start else ()
    return pl.pallas_call(
        functools.partial(
            gather_kernel, inner=inner, groups=groups, start=start, per_step=len(keys[0]), which=which
        ),
        out_shape=jax.ShapeDtypeStruct((own_groups * RG, held, segment), jnp.float32),
        grid=(own_groups,),
        in_specs=[smem, smem, pl.BlockSpec(block, lambda i: (group_of(i, inner, groups), 0, 0))]
        + [pl.BlockSpec(block, lambda i: (i, 0, 0))] * sum(map(len, keys))
        + [acc_spec] * len(given),
        out_specs=acc_spec,
        scratch_shapes=[
            pltpu.VMEM((segment, 2 * segment), jnp.float32),
            pltpu.VMEM((2, segment, 2 * segment), jnp.float32),
        ],
        input_output_aliases={3 + sum(map(len, keys)): 0} if given else {},
        compiler_params=pltpu.CompilerParams(vmem_limit_bytes=VMEM_LIMIT),
        cost_estimate=cost(1.5 * own_groups),
    )(place, ranges, left, *[a for pair in keys for a in pair], *given)


def finish(place, ranges, left, keys, acc, outs, inner, step, which=None):
    rows, channels, segment = left.shape
    groups = rows // RG
    own_groups = keys[0].shape[0] // RG
    block = (RG, channels, segment)
    smem = pl.BlockSpec(memory_space=pltpu.SMEM)

    def group(i):
        return group_of(i, inner, groups)

    given = () if outs is None else tuple(outs)
    return pl.pallas_call(
        functools.partial(
            finish_kernel, inner=inner, groups=groups, step=step, per_step=len(keys), which=which
        ),
        out_shape=(
            jax.ShapeDtypeStruct((channels, rows, segment), jnp.bfloat16),
            jax.ShapeDtypeStruct((rows, segment), jnp.float32),
        ),
        grid=(own_groups,),
        in_specs=[
            smem,
            smem,
            pl.BlockSpec(block, lambda i: (group(i), 0, 0)),
            *[pl.BlockSpec(block, lambda i: (i, 0, 0)) for _ in keys],
            pl.BlockSpec((RG, channels + EXTRA, segment), lambda i: (i, 0, 0)),
        ]
        + [pl.BlockSpec(memory_space=pl.ANY)] * len(given),
        out_specs=(
            pl.BlockSpec((channels, RG, segment), lambda i: (0, group(i), 0)),
            pl.BlockSpec((RG, segment), lambda i: (group(i), 0)),
        ),
        scratch_shapes=[
            pltpu.VMEM((RG, channels + EXTRA, segment), jnp.float32),
            pltpu.VMEM((segment, 2 * segment), jnp.float32),
            pltpu.VMEM((2, segment, 2 * segment), jnp.float32),
            pltpu.VMEM((RG, channels, segment), jnp.float32),
        ],
        input_output_aliases={4 + len(keys): 0, 5 + len(keys): 1} if given else {},
        compiler_params=pltpu.CompilerParams(vmem_limit_bytes=VMEM_LIMIT),
        cost_estimate=cost(own_groups),
    )(place, ranges, left, *keys, acc, *given)


def both_ways(pairs):
    return pairs + [(b, a) for a, b in pairs]


def program(images, first_weight, second_weight, search_ranges):
    row_count = lax.axis_size("rows")
    col_count = lax.axis_size("cols")
    col = lax.axis_index("cols")
    _, rows, segment = images.shape[1:]
    place = jnp.stack([lax.axis_index("rows"), col]).astype(jnp.int32)
    ranges = search_ranges.reshape(2, rows // RG)

    steps = min(col_count // 2 - 1, HOPS // 2)
    swap = [(i, i ^ 1) for i in range(col_count)]
    across = both_ways([(i, i + 1) for i in range(1, col_count - 1, 2)])
    around_across = across + both_ways([(0, col_count - 1)])
    hop = [(i, (i + 2) % col_count) for i in range(col_count)]
    last_hop = [(i, i + 2) for i in range(2 * (steps - 1), col_count - 2)]
    down = [(i, (i + 1) % row_count) for i in range(row_count)]
    up = [(b, a) for a, b in down]

    def exchanged(pieces, chunks, pairs):
        own = pack_edges(place, pieces, chunks, row_count)
        cross = lax.ppermute(own, "cols", pairs)
        partner = lax.ppermute(own, "cols", swap)
        return own, partner, cross

    def features(pieces, index, parts, count, offset, edges, base):
        return unit_features(
            place, pieces, index, parts, count, offset, edges, base,
            first_weight, second_weight, (row_count, col_count),
        )

    first_rows, last_rows = end_rows(images)
    above = lax.ppermute(last_rows, "rows", down)
    below = lax.ppermute(first_rows, "rows", up)
    mid = images.transpose(0, 2, 1, 3)

    strip = rows // 4
    inner = rows - 2 * strip
    around = (mid, above, below)
    edges_a = exchanged((mid,), ((1, ((inner, strip),)),), around_across)
    chunks_r = (1, ((strip, 0), (strip, rows - strip))), (0, ((rows, 0),))
    edges_r = exchanged(around, chunks_r, across)
    right_a = features((mid,), 1, 1, inner, strip - REACH, edges_a, 0)
    right_b = features(around, 1, 2, strip, 0, edges_r, 0)
    left = features(around, 0, 1, rows, 0, edges_r, 2 * edge_steps(strip, segment)[1])

    early = max(steps - 1, 1)

    def chain(mine):
        pairs = []
        for step in range(steps + 1):
            if step:
                mine = lax.ppermute(mine, "cols", hop if step < steps else last_hop)
            pairs.append((mine, lax.ppermute(mine, "cols", swap)))
        return pairs

    def totals(keys, inside):
        acc = correlate(place, ranges, left, keys[:early], None, 0, inside)
        if early == steps:
            return acc
        return correlate(place, ranges, left, keys[early:steps], acc, early, inside)

    keys_a, keys_b = chain(right_a), chain(right_b)
    acc_a, acc_b = totals(keys_a, True), totals(keys_b, False)
    outs = finish(place, ranges, left, keys_a[steps], acc_a, None, True, steps)
    mine, theirs = keys_b[steps]
    acc_b = correlate(place, ranges, left, [(mine,)], acc_b, steps, False, "mine")
    return finish(place, ranges, left, (theirs,), acc_b, outs, False, steps, "theirs")


def solution(mesh):
    placed = (P(None, None, "rows", "cols"), P(), P(), P(None, "rows", "cols"))
    return jax.shard_map(
        program,
        mesh=mesh,
        in_specs=placed,
        out_specs=(P(None, "rows", "cols"), P("rows", "cols")),
        check_vma=False,
    )
```
